512 devices in a mesh: shard: 64 (over z, y), tensor: 4 (over x), section: 2 (over core).
Axes of the slice: x: 4, y: 8, z: 8, core: 2. Of those that a mesh axis runs over, the one named last changes fastest.
Arguments:
- grad_parts: bfloat16 [64, 2, 4, 1024, 1024], P('shard', 'section', None, 'tensor'), may hold values from -45 to 45
- vector_grads: bfloat16 [64, 2, 4, 1024], P('shard', 'section', None, 'tensor'), may hold values from -16 to 16
- momentum: float32 [2, 4, 1024, 1024], P('section', None, ('tensor', 'shard')), may hold values from -6 to 6
- weights: bfloat16 [2, 4, 1024, 1024], P('section', None, ('tensor', 'shard')), may hold values from -0.1875 to 0.1875
- vectors: float32 [2, 4, 1024], P('section', None, ('tensor', 'shard')), may hold values from 0.5 to 1.5
- first_moment: float32 [2, 4, 1024], P('section', None, ('tensor', 'shard')), may hold values from -3 to 3
- second_moment: float32 [2, 4, 1024], P('section', None, ('tensor', 'shard')), may hold values from 0.05 to 2
Outputs:
- new_momentum: float32 [2, 4, 1024, 1024], P('section', None, ('tensor', 'shard'))
- orthogonal_update: bfloat16 [2, 4, 1024, 1024], P('section', None, ('tensor', 'shard'))
- new_weights: bfloat16 [2, 4, 1024, 1024], P('section', None, ('tensor', 'shard'))
- adam_direction: float32 [2, 4, 1024], P('section', None, ('tensor', 'shard'))
- new_vectors: float32 [2, 4, 1024], P('section', None, ('tensor', 'shard'))
The draws below stay inside these ranges and needn't reach their ends.
All inputs are finite; a program needn't handle non-finite values.
Results may differ from the reference program's by a relative error of at most 0.0048.
The reference program's roundings to bfloat16 on the way (of `scaled`, `block_gram`, `gram_matrix` and `first_product`) count: a program that leaves them out, or rounds other values in their place, can miss the bound.
Values may be sent and summed in bfloat16 or wider, within the bound.
A program may use at most 64 MiB of HBM per device.

```python
import math
import jax
import jax.numpy as jnp
from jax import lax

D = 1024
MATS = 4
VECS = 4
NS_STEPS = 2
N_SHARD = 64
N_TENSOR = 4
N_SECTION = 2


def row_weighting(key):
    block_pick = jax.random.randint(jax.random.fold_in(key, 101), (N_SECTION, MATS, 1, 1), 0, N_TENSOR)
    row_block = (jnp.arange(D) // (D // N_TENSOR)).reshape(1, 1, D, 1)
    return jnp.where(row_block == block_pick, 1.0, 0.1).astype(jnp.float32)


def draw_grad_parts(key, part):
    keys = jax.random.split(key, 5)
    row_scale = jnp.exp(jax.random.uniform(keys[0], (1, N_SECTION, MATS, D, 1), jnp.float32, 0.0, math.log(10.0)))
    col_scale = jnp.exp(jax.random.uniform(keys[1], (1, N_SECTION, MATS, 1, D), jnp.float32, 0.0, math.log(10.0)))
    ramp = 1.0 + 2.0 * jnp.arange(D, dtype=jnp.float32).reshape(1, 1, 1, D, 1) / (D - 1)
    heavier = jax.random.randint(jax.random.fold_in(key, 202), (), 0, N_SECTION)
    ratio = jax.random.uniform(jax.random.fold_in(key, 203), (), jnp.float32, 2.5, 4.0)
    section_gain = jnp.where(jnp.arange(N_SECTION) == heavier, 1.75, 1.75 / ratio).astype(jnp.float32).reshape(1, N_SECTION, 1, 1, 1)
    light_rows = row_weighting(key)[None]
    values = jax.random.truncated_normal(keys[4], -4.0, 4.0, (N_SHARD, N_SECTION, MATS, D, D), jnp.float32)
    return (0.02 * values * row_scale * col_scale * ramp * section_gain * light_rows).astype(jnp.bfloat16)


def draw_momentum(key, part):
    light_rows = row_weighting(key)
    value_key = jax.random.fold_in(key, 303)
    values = jax.random.truncated_normal(value_key, -6.0, 6.0, (N_SECTION, MATS, D, D), jnp.float32)
    return (values * light_rows).astype(jnp.float32)


def strengthened(array, own_key, source, target, blocks, factor):
    def block_of(position):
        return (jnp.arange(array.shape[position]) // (array.shape[position] // blocks)).reshape((-1,) + (1,) * (array.ndim - 1 - position))

    one_side = jax.random.permutation(own_key, blocks)[block_of(target)]
    far = (block_of(target) + blocks // 2) % blocks
    return jnp.where((block_of(source) == one_side) | (block_of(source) == far), factor * array, array)


def levels(own_key, extent, shards, smallest, high):
    def one(axis_at, shards_of):
        draws = jax.random.uniform(jax.random.fold_in(jax.random.fold_in(own_key, 6), axis_at), (shards_of,), jnp.float32, smallest / len(shards), high / len(shards))
        return jnp.repeat(jnp.exp(draws), extent[axis_at] // shards_of).reshape((-1,) + (1,) * (len(extent) - axis_at - 1))

    level = one(*shards[0])
    for cut in shards[1:]:
        level = level * one(*cut)
    return level


def gaussian(own_key, dims, width, bound, shards=(), held_as=jnp.bfloat16):
    factor_of = levels(own_key, dims, shards, -0.22, 0.18) if shards else 1.0
    values = jax.random.normal(own_key, dims, jnp.float32) * width * factor_of
    return jnp.minimum(jnp.maximum(values, -bound), bound).astype(held_as)


def noise_with(rng, shape, spread, most, cuts, heavy, kind=jnp.bfloat16):
    drawn = spread * jax.random.normal(rng, shape, jnp.float32)
    if cuts:
        drawn = drawn * levels(rng, shape, cuts, -0.22, 0.18)
    return jnp.clip(strengthened(drawn, jax.random.fold_in(rng, 3), *heavy), -most, most).astype(kind)


def setup_inputs(seed: int = 0) -> dict:
    seeds = jax.random.split(jax.random.key(seed), 8)
    return {
        "grad_parts": draw_grad_parts(jax.random.fold_in(seeds[7], 71), 0),
        "vector_grads": noise_with(seeds[1], (N_SHARD, N_SECTION, VECS, D), 1.0, 16.0, ((0, 64), (1, 2), (3, 4)), (0, 3, 64, 4.0)),
        "momentum": draw_momentum(jax.random.fold_in(seeds[7], 71), 0),
        "weights": gaussian(seeds[3], (N_SECTION, MATS, D, D), D ** -0.5, 0.1875, ((0, 2), (2, 256))),
        "vectors": jnp.clip(1.0 + 0.1 * jax.random.normal(seeds[4], (N_SECTION, VECS, D), jnp.float32), 0.5, 1.5),
        "first_moment": gaussian(seeds[5], (N_SECTION, VECS, D), 0.5, 3.0, ((0, 2), (2, 256)), jnp.float32),
        "second_moment": jnp.clip(jnp.exp(math.log(2.0) - 3.6888794 * jax.random.uniform(seeds[6], (N_SECTION, VECS, D), jnp.float32) ** levels(seeds[6], (N_SECTION, VECS, D), ((0, 2), (2, 256)), -0.2, 0.2)), 0.05, 2.0),
    }


ns_first = 3.4445
ns_second = -4.775
ns_third = 2.0315
mom_beta = 0.95
max_norm = 1024.0
muon_rate = 0.02
muon_decay = 0.1
adam_rate = 0.001
adam_decay = 0.01

def orthogonalize(matrix):
    for iteration in range(NS_STEPS):
        blocks = matrix.reshape(N_TENSOR, D // N_TENSOR, D).astype(jnp.float32)
        block_gram = jnp.einsum('brc,brd->bcd', blocks, blocks, precision=lax.Precision.HIGHEST)
        rounded = lax.optimization_barrier(block_gram.astype(jnp.bfloat16)).astype(jnp.float32)
        gram_matrix = lax.optimization_barrier(jnp.sum(rounded, axis=0)).astype(jnp.bfloat16)
        first_product = jnp.dot(matrix, gram_matrix, preferred_element_type=jnp.float32).astype(jnp.bfloat16)
        second_product = jnp.dot(first_product, gram_matrix, preferred_element_type=jnp.float32)
        combined = ns_first * matrix.astype(jnp.float32) + ns_second * first_product.astype(jnp.float32) + ns_third * second_product
        matrix = combined.astype(jnp.bfloat16)
    return matrix

def reference(grad_parts, vector_grads, momentum, weights, vectors, first_moment, second_moment):

    def add_part(part_index, accumulated):
        return accumulated + grad_parts[part_index].astype(jnp.float32)
    grad_sum = lax.fori_loop(0, N_SHARD, add_part, jnp.zeros(grad_parts.shape[1:], jnp.float32))
    vector_sum = lax.optimization_barrier(jnp.sum(vector_grads.astype(jnp.float32), axis=0))
    grand_total = jnp.sum(grad_sum * grad_sum) + jnp.sum(vector_sum * vector_sum)
    clip_factor = jnp.minimum(1.0, max_norm / (jnp.sqrt(grand_total) + 1e-06))
    new_momentum = mom_beta * momentum + clip_factor * grad_sum
    nesterov = clip_factor * grad_sum + mom_beta * new_momentum
    update_norm = lax.optimization_barrier(jnp.sum(nesterov * nesterov, axis=(2, 3), keepdims=True))
    scaled = (nesterov / (jnp.sqrt(update_norm) + 1e-07)).astype(jnp.bfloat16)
    orthogonal_update = jnp.stack([jnp.stack([orthogonalize(scaled[section_index, matrix_index]) for matrix_index in range(MATS)]) for section_index in range(N_SECTION)])
    muon_scale = 0.2 * math.sqrt(D)
    new_weights = (weights.astype(jnp.float32) * (1.0 - muon_rate * muon_decay) - muon_rate * muon_scale * orthogonal_update.astype(jnp.float32)).astype(jnp.bfloat16)
    vector_clipped = clip_factor * vector_sum
    updated_first = 0.9 * first_moment + 0.1 * vector_clipped
    updated_second = 0.999 * second_moment + 0.001 * vector_clipped * vector_clipped
    adam_direction = updated_first / (jnp.sqrt(updated_second) + 1e-08)
    new_vectors = vectors * (1.0 - adam_rate * adam_decay) - adam_rate * adam_direction
    return (new_momentum, orthogonal_update, new_weights, adam_direction, new_vectors)
```

```python
import functools
import math

import jax
import jax.numpy as jnp
from jax import lax
from jax.experimental import pallas as pl
from jax.experimental.pallas import tpu as pltpu
from jax.sharding import PartitionSpec as P

NS_STEPS = 2
ns_first = 3.4445
ns_second = -4.775
ns_third = 2.0315
mom_beta = 0.95
max_norm = 1024.0
muon_rate = 0.02
muon_decay = 0.1
adam_rate = 0.001
adam_decay = 0.01

MESH = pl.DeviceIdType.MESH
f32 = jnp.float32
bf16 = jnp.bfloat16
LANES = 128


def kernel(
    NZ, NY, NX, MATS, LOCAL, WIDTH,
    grad, vec, mom, wts, vecs, fm, sm,
    new_mom, upd_out, new_wts, adam_dir, new_vecs,
    halfb, shufb, rz, ry, own_a, own_b, acc_a, send_a, send_b, r2a, r2b,
    vrz, vry, vsum, stat, srz, sry, srx, xsc, xr, stage, X, G, X1, gacc, p_last, ret, upd,
    s_loc, s_rz, r_rz, s_ry, r_ry, s_2a, r_2a, s_2b, r_2b,
    s_vz, r_vz, s_vy, r_vy, s_sz, r_sz, s_sy, r_sy, s_sx, r_sx,
    s_x1, r_x1, s_gz, r_gz, s_gl, s_gr, r_gl, r_gr, s_fl, s_fr, r_fl, r_fr, s_rt, r_rt,
):
    HM = MATS // 2
    ROWS = NZ * NY * LOCAL
    ZR = NY * LOCAL
    D = WIDTH
    shard = lax.axis_index("shard")
    x = lax.axis_index("tensor")
    c = lax.axis_index("section")
    z = lax.div(shard, NY)
    y = lax.rem(shard, NY)

    def at_z(dz):
        return lax.rem(z + dz + NZ, NZ)

    def at_y(dy):
        return lax.rem(y + dy + NY, NY)

    def dev_z(dz):
        return (at_z(dz) * NY + y, x, c)

    def dev_y(dy):
        return (z * NY + at_y(dy), x, c)

    def dev_yabs(yy):
        return (z * NY + yy, x, c)

    def dev_x(dx, dc):
        return (shard, lax.rem(x + dx + NX, NX), lax.rem(c + dc, 2))

    xpeers = [(dx, dc) for dx in range(NX) for dc in range(2) if (dx, dc) != (0, 0)]

    def rcopy(src, dst, ss, rs, dev):
        return pltpu.make_async_remote_copy(
            src_ref=src, dst_ref=dst, send_sem=ss, recv_sem=rs, device_id=dev, device_id_type=MESH
        )

    off_z = pl.multiple_of(z * ZR, ZR)
    loc_a = pltpu.make_async_copy(grad.at[pl.ds(0, HM), pl.ds(off_z, ZR), :], own_a, s_loc.at[0])
    loc_b = pltpu.make_async_copy(grad.at[pl.ds(HM, HM)], halfb, s_loc.at[1])
    loc_b.start()
    loc_a.start()

    barrier = pltpu.get_barrier_semaphore()
    for d in range(1, NZ):
        pl.semaphore_signal(barrier, inc=1, device_id=dev_z(d), device_id_type=MESH)
    for d in range(1, NY):
        pl.semaphore_signal(barrier, inc=1, device_id=dev_y(d), device_id_type=MESH)
    for dx, dc in xpeers:
        pl.semaphore_signal(barrier, inc=1, device_id=dev_x(dx, dc), device_id_type=MESH)
    pl.semaphore_wait(barrier, NZ - 1 + NY - 1 + len(xpeers))

    ph1a = []
    for d in range(1, NZ):
        dst_off = pl.multiple_of(at_z(d) * ZR, ZR)
        cp = rcopy(
            grad.at[pl.ds(0, HM), pl.ds(dst_off, ZR), :], rz.at[d - 1],
            s_rz.at[d - 1], r_rz.at[d - 1], dev_z(d),
        )
        cp.start()
        ph1a.append(cp)
    vz = []
    for d in range(1, NZ):
        cp = rcopy(vec, vrz.at[d - 1], s_vz.at[d - 1], r_vz.at[d - 1], dev_z(d))
        cp.start()
        vz.append(cp)

    loc_b.wait()
    for m in range(HM):
        for zz in range(NZ):
            rows = halfb[m, zz * ZR:(zz + 1) * ZR, :].astype(f32)
            for yy in range(NY):
                shufb[yy, m, zz] = rows[yy * LOCAL:(yy + 1) * LOCAL, :].astype(bf16)
    ph1b = []
    for d in range(1, NY):
        cp = rcopy(
            shufb.at[at_y(d)], ry.at[d - 1], s_ry.at[d - 1], r_ry.at[d - 1], dev_y(d)
        )
        cp.start()
        ph1b.append(cp)

    for cp in vz:
        cp.wait()
    vs = vec[...].astype(f32)
    for d in range(1, NZ):
        vs = vs + vrz[d - 1].astype(f32)
    vsum[...] = vs
    vy = []
    for d in range(1, NY):
        cp = rcopy(vsum, vry.at[d - 1], s_vy.at[d - 1], r_vy.at[d - 1], dev_y(d))
        cp.start()
        vy.append(cp)

    loc_a.wait()
    acc_a[...] = own_a[...].astype(f32)
    for cp in ph1a:
        cp.wait()
    for d in range(1, NZ):
        acc_a[...] += rz[d - 1].astype(f32)
    for m in range(HM):
        for yy in range(NY):
            send_a[yy, m] = acc_a[m, yy * LOCAL:(yy + 1) * LOCAL, :]
    ph2a = []
    for d in range(1, NY):
        cp = rcopy(send_a.at[at_y(d)], r2a.at[d - 1], s_2a.at[d - 1], r_2a.at[d - 1], dev_y(d))
        cp.start()
        ph2a.append(cp)

    for cp in ph1b:
        cp.wait()
    for m in range(HM):
        for zz in range(NZ):
            tot = shufb[y, m, zz].astype(f32)
            for d in range(1, NY):
                tot = tot + ry[d - 1, m, zz].astype(f32)
            send_b[zz, m] = tot
    ph2b = []
    for d in range(1, NZ):
        cp = rcopy(send_b.at[at_z(d)], r2b.at[d - 1], s_2b.at[d - 1], r_2b.at[d - 1], dev_z(d))
        cp.start()
        ph2b.append(cp)

    for cp in vy:
        cp.wait()
    vt = vsum[...]
    for d in range(1, NY):
        vt = vt + vry[d - 1]

    for cp in ph2a:
        cp.wait()
    for cp in ph2b:
        cp.wait()
    gs = []
    for m in range(HM):
        tot = send_a[y, m]
        for d in range(1, NY):
            tot = tot + r2a[d - 1, m]
        gs.append(tot)
    for m in range(HM):
        tot = send_b[z, m]
        for d in range(1, NZ):
            tot = tot + r2b[d - 1, m]
        gs.append(tot)

    def lane_sum(v):
        total = jnp.sum(v, axis=0, keepdims=True)
        out = total[:, :LANES]
        for k in range(1, v.shape[1] // LANES):
            out = out + total[:, k * LANES:(k + 1) * LANES]
        return out

    stat[...] = jnp.zeros_like(stat)
    grand = lane_sum(vt * vt) * (1.0 / (NZ * NY))
    for m in range(MATS):
        gg = lane_sum(gs[m] * gs[m])
        mm = mom[m]
        stat[m:m + 1, :] = gg
        stat[MATS + m:MATS + m + 1, :] = lane_sum(gs[m] * mm)
        stat[2 * MATS + m:2 * MATS + m + 1, :] = lane_sum(mm * mm)
        grand = grand + gg
    stat[3 * MATS:3 * MATS + 1, :] = grand

    st = []
    for d in range(1, NZ):
        cp = rcopy(stat, srz.at[d - 1], s_sz.at[d - 1], r_sz.at[d - 1], dev_z(d))
        cp.start()
        st.append(cp)
    for cp in st:
        cp.wait()
    tot = stat[...]
    for d in range(1, NZ):
        tot = tot + srz[d - 1]
    stat[...] = tot
    st = []
    for d in range(1, NY):
        cp = rcopy(stat, sry.at[d - 1], s_sy.at[d - 1], r_sy.at[d - 1], dev_y(d))
        cp.start()
        st.append(cp)
    for cp in st:
        cp.wait()
    for d in range(1, NY):
        tot = tot + sry[d - 1]
    stat[...] = tot
    st = []
    for i, (dx, dc) in enumerate(xpeers):
        cp = rcopy(stat, srx.at[i], s_sx.at[i], r_sx.at[i], dev_x(dx, dc))
        cp.start()
        st.append(cp)
    for cp in st:
        cp.wait()
    other = jnp.zeros((1, LANES), f32)
    for i, (dx, dc) in enumerate(xpeers):
        if dc == 0:
            tot = tot + srx[i]
        else:
            other = other + srx[i, 3 * MATS:3 * MATS + 1, :]
    own_sums = jnp.sum(tot, axis=1, keepdims=True)
    grand_total = jnp.sum(other, axis=1, keepdims=True) + own_sums[3 * MATS:3 * MATS + 1]
    clip = jnp.minimum(1.0, max_norm / (jnp.sqrt(grand_total) + 1e-06))

    for m in range(MATS):
        cg = clip * gs[m]
        nm = mom_beta * mom[m] + cg
        new_mom[m] = nm
        nest = cg + mom_beta * nm
        gg = own_sums[m:m + 1]
        gm = own_sums[MATS + m:MATS + m + 1]
        mm = own_sums[2 * MATS + m:2 * MATS + m + 1]
        cc = (1.0 + mom_beta) * clip
        b2 = mom_beta * mom_beta
        norm2 = jnp.maximum(cc * cc * gg + (2.0 * b2) * cc * gm + (b2 * b2) * mm, 0.0)
        xsc[m] = (nest / (jnp.sqrt(norm2) + 1e-07)).astype(bf16)

    for m in range(MATS):
        yt = c * MATS + m

        @pl.when(y != yt)
        def _():
            rcopy(xsc.at[m], xr.at[y], s_x1.at[m], r_x1.at[y], dev_yabs(yt)).start()

    vlane = lax.broadcasted_iota(jnp.int32, vt.shape, 1)
    for k in range(LOCAL):
        vg = clip * jnp.sum(jnp.where(vlane == shard * LOCAL + k, vt, 0.0), axis=1, keepdims=True)
        uf = 0.9 * fm[:, k:k + 1] + 0.1 * vg
        us = 0.999 * sm[:, k:k + 1] + 0.001 * vg * vg
        ad = uf / (jnp.sqrt(us) + 1e-08)
        adam_dir[:, k:k + 1] = ad
        new_vecs[:, k:k + 1] = vecs[:, k:k + 1] * (1.0 - adam_rate * adam_decay) - adam_rate * ad

    my_m = y - c * MATS
    active = lax.div(y, MATS) == c
    my_row = x * ROWS + z * ZR
    my_off = pl.multiple_of(my_row, ZR)

    @pl.when(active)
    def _():
        xr[y] = xsc[my_m]
        for yy in range(NY):
            @pl.when(y != yy)
            def _():
                rcopy(xsc.at[0], xr.at[yy], s_x1.at[0], r_x1.at[yy], dev_yabs(yy)).wait_recv()
            stage[yy * LOCAL:(yy + 1) * LOCAL, :] = xr[yy].astype(f32)
        X[pl.ds(my_off, ZR), :] = stage[...].astype(bf16)

        def block(dz, dx):
            row = lax.rem(x + dx + NX, NX) * ROWS + at_z(dz) * ZR
            return X.at[pl.ds(pl.multiple_of(row, ZR), ZR), :]

        mine = block(0, 0)
        zc = []
        for d in range(1, NZ):
            cp = rcopy(mine, mine, s_gz.at[d - 1], r_gz.at[d - 1], dev_z(d))
            cp.start()
            zc.append(cp)
        order = [0]
        for d in range(1, NZ // 2 + 1):
            order.append(d)
            if NZ - d != d:
                order.append(NZ - d)
        xc = {}
        fwd = []

        def forward(k):
            xc[k][0].wait_recv()
            if k % 2 == 0:
                b = block(-k, -1)
                cp = rcopy(b, b, s_fr.at[k], r_fr.at[k], dev_x(1, 0))
                cp.start()
                fwd.append(cp)
            xc[k][1].wait_recv()
            if k % 2 == 1:
                b = block(-k, 1)
                cp = rcopy(b, b, s_fl.at[k], r_fl.at[k], dev_x(-1, 0))
                cp.start()
                fwd.append(cp)

        prev = None
        for k in order:
            if k > 0:
                zc[k - 1].wait_recv()
            b = block(-k, 0)
            right = rcopy(b, b, s_gr.at[k], r_gr.at[k], dev_x(1, 0))
            left = rcopy(b, b, s_gl.at[k], r_gl.at[k], dev_x(-1, 0))
            right.start()
            left.start()
            xc[k] = (right, left)
            if prev is not None:
                forward(prev)
            prev = k
        forward(prev)
        for cp in fwd:
            cp.wait()
        for k in order:
            xc[k][0].wait_send()
            xc[k][1].wait_send()
        for cp in zc:
            cp.wait_send()

        TILE = min(256, D)
        NT = D // TILE
        dn0 = (((0,), (0,)), ((), ()))

        def gram(src):
            @pl.loop(0, NT)
            def _(j):
                cols = pl.ds(pl.multiple_of(j * TILE, TILE), TILE)
                for b in range(NX):
                    xb = src[b * ROWS:(b + 1) * ROWS, :]
                    xc_ = src[b * ROWS:(b + 1) * ROWS, cols]
                    pr = lax.dot_general(xb, xc_, dn0, preferred_element_type=f32).astype(bf16).astype(f32)
                    if b == 0:
                        gacc[...] = pr
                    else:
                        gacc[...] += pr
                G[:, cols] = gacc[...].astype(bf16)

        def step(rows):
            p1 = jnp.dot(rows, G[...], preferred_element_type=f32).astype(bf16)
            p2 = jnp.dot(p1, G[...], preferred_element_type=f32)
            return (ns_first * rows.astype(f32) + ns_second * p1.astype(f32) + ns_third * p2).astype(bf16)

        gram(X)

        @pl.loop(0, NX)
        def _(i):
            rows = pl.ds(pl.multiple_of(i * ROWS, ROWS), ROWS)
            X1[rows, :] = step(X[rows, :])

        gram(X1)
        p_last[...] = step(X1[pl.ds(my_off, ZR), :]).astype(f32)
        for yy in range(NY):
            ret[yy] = p_last[yy * LOCAL:(yy + 1) * LOCAL, :].astype(bf16)
        for yy in range(NY):
            @pl.when(y != yy)
            def _():
                rcopy(ret.at[yy], upd.at[my_m], s_rt.at[yy], r_rt.at[my_m], dev_yabs(yy)).start()
        upd[my_m] = ret[y]

    muon_scale = 0.2 * math.sqrt(D)
    for m in range(MATS):
        @pl.when(y != c * MATS + m)
        def _():
            rcopy(ret.at[0], upd.at[m], s_rt.at[0], r_rt.at[m], dev_yabs(y)).wait_recv()
        u = upd[m]
        upd_out[m] = u
        new_wts[m] = (
            wts[m].astype(f32) * (1.0 - muon_rate * muon_decay) - muon_rate * muon_scale * u.astype(f32)
        ).astype(bf16)

    for m in range(MATS):
        @pl.when(y != c * MATS + m)
        def _():
            rcopy(xsc.at[m], xr.at[0], s_x1.at[m], r_x1.at[0], dev_yabs(y)).wait_send()

    @pl.when(active)
    def _():
        for yy in range(NY):
            @pl.when(y != yy)
            def _():
                rcopy(ret.at[yy], upd.at[0], s_rt.at[yy], r_rt.at[0], dev_yabs(yy)).wait_send()


def build(mesh_shape, NZ, NY, MATS, LOCAL, WIDTH):
    NX = mesh_shape["tensor"]
    HM = MATS // 2
    ROWS = NZ * NY * LOCAL
    ZR = NY * LOCAL
    D = WIDTH
    DMA = pltpu.SemaphoreType.DMA
    V = pltpu.VMEM
    SR = -(-(3 * MATS + 1) // 8) * 8
    VW = ROWS
    NXP = 2 * NX - 1
    scratch = [
        V((HM, ROWS, D), bf16),
        V((NY, HM, NZ, LOCAL, D), bf16),
        V((NZ - 1, HM, ZR, D), bf16),
        V((NY - 1, HM, NZ, LOCAL, D), bf16),
        V((HM, ZR, D), bf16),
        V((8, LANES), f32),
        V((HM, ZR, D), f32),
        V((NY, HM, LOCAL, D), f32),
        V((NZ, HM, LOCAL, D), f32),
        V((NY - 1, HM, LOCAL, D), f32),
        V((NZ - 1, HM, LOCAL, D), f32),
        V((NZ - 1, MATS, VW), bf16),
        V((NY - 1, MATS, VW), f32),
        V((MATS, VW), f32),
        V((SR, LANES), f32),
        V((NZ - 1, SR, LANES), f32),
        V((NY - 1, SR, LANES), f32),
        V((NXP, SR, LANES), f32),
        V((MATS, LOCAL, D), bf16),
        V((NY, LOCAL, D), bf16),
        V((ZR, D), f32),
        V((NX * ROWS, D), bf16),
        V((D, D), bf16),
        V((NX * ROWS, D), bf16),
        V((D, min(256, D)), f32),
        V((ZR, D), f32),
        V((NY, LOCAL, D), bf16),
        V((MATS, LOCAL, D), bf16),
        DMA((2,)),
        DMA((NZ - 1,)), DMA((NZ - 1,)), DMA((NY - 1,)), DMA((NY - 1,)),
        DMA((NY - 1,)), DMA((NY - 1,)), DMA((NZ - 1,)), DMA((NZ - 1,)),
        DMA((NZ - 1,)), DMA((NZ - 1,)), DMA((NY - 1,)), DMA((NY - 1,)),
        DMA((NZ - 1,)), DMA((NZ - 1,)), DMA((NY - 1,)), DMA((NY - 1,)),
        DMA((NXP,)), DMA((NXP,)),
        DMA((MATS,)), DMA((NY,)),
        DMA((NZ - 1,)), DMA((NZ - 1,)),
        DMA((NZ,)), DMA((NZ,)), DMA((NZ,)), DMA((NZ,)),
        DMA((NZ,)), DMA((NZ,)), DMA((NZ,)), DMA((NZ,)),
        DMA((NY,)), DMA((MATS,)),
    ]
    vm = pl.BlockSpec(memory_space=pltpu.VMEM)
    return pl.pallas_call(
        functools.partial(kernel, NZ, NY, NX, MATS, LOCAL, WIDTH),
        out_shape=(
            jax.ShapeDtypeStruct((MATS, LOCAL, D), f32),
            jax.ShapeDtypeStruct((MATS, LOCAL, D), bf16),
            jax.ShapeDtypeStruct((MATS, LOCAL, D), bf16),
            jax.ShapeDtypeStruct((MATS, LOCAL), f32),
            jax.ShapeDtypeStruct((MATS, LOCAL), f32),
        ),
        in_specs=[pl.BlockSpec(memory_space=pl.ANY)] + [vm] * 6,
        out_specs=(vm,) * 5,
        scratch_shapes=scratch,
        compiler_params=pltpu.CompilerParams(
            collective_id=0, has_side_effects=True, vmem_limit_bytes=48 << 20
        ),
    )


def solution(mesh, NZ=8, NY=8):
    def per_device(grad_parts, vector_grads, momentum, weights, vectors, first_moment, second_moment):
        MATS, LOCAL, WIDTH = momentum.shape[1:]
        call = build(mesh.shape, NZ, NY, MATS, LOCAL, WIDTH)
        outs = call(
            grad_parts[0, 0], vector_grads[0, 0], momentum[0], weights[0],
            vectors[0], first_moment[0], second_moment[0],
        )
        return tuple(o[None] for o in outs)

    rows = P("section", None, ("tensor", "shard"), None)
    cols = P("section", None, ("tensor", "shard"))
    return jax.shard_map(
        per_device,
        mesh=mesh,
        in_specs=(
            P("shard", "section", None, "tensor", None),
            P("shard", "section", None, "tensor"),
            rows, rows, cols, cols, cols,
        ),
        out_specs=(rows, rows, rows, cols, cols),
        check_vma=False,
    )
```

```python
import functools
import math

import jax
import jax.numpy as jnp
from jax import lax
from jax.experimental import pallas as pl
from jax.experimental.pallas import tpu as pltpu
from jax.sharding import PartitionSpec as P


ns_first = 3.4445
ns_second = -4.775
ns_third = 2.0315
mom_beta = 0.95
max_norm = 1024.0
muon_rate = 0.02
muon_decay = 0.1
adam_rate = 0.001
adam_decay = 0.01

MESH = pl.DeviceIdType.MESH
f32 = jnp.float32
bf16 = jnp.bfloat16
LANES = 128


def near_first(n):
    order = []
    for d in range(1, n // 2 + 1):
        order.append(d)
        if n - d != d:
            order.append(n - d)
    return order


def kernel(
    NZ, NY, NX, MATS, LOCAL, D,
    grad, vec, mom, wts, vecs, fm, sm,
    new_mom, upd_out, new_wts, adam_dir, new_vecs,
    vecv, wtv, vecsv, fmv, smv,
    own_a, acc_a, rz, ry, send_b, r2a, r2b, mrx, mst, gbuf, nms,
    vrz, vry, vsum, stat, srz, srx, sry, stat2, clipb, X, G, X1, gacc, ret,
    s_loc, s_rz, r_rz, s_ry, r_ry, s_2a, r_2a, s_2b, r_2b, s_mm, r_mm,
    s_vz, r_vz, s_vy, r_vy, s_sz, r_sz, s_sx, r_sx, s_sy, r_sy, s_cl, r_cl,
    s_gz, r_gz, s_gl, s_gr, r_gl, r_gr, s_fl, s_fr, r_fl, r_fr,
    s_nm, r_nm, s_rt, r_rt,
):
    ROWS = NZ * NY * LOCAL
    ZR = NY * LOCAL
    HC = D // 2
    shard = lax.axis_index("shard")
    x = lax.axis_index("tensor")
    c = lax.axis_index("section")
    z = lax.div(shard, NY)
    y = lax.rem(shard, NY)
    active = lax.div(y, MATS) == c
    my_m = lax.rem(y, MATS)

    def at_z(d):
        return lax.rem(z + d + NZ, NZ)

    def dev_z(d):
        return (at_z(d) * NY + y, x, c)

    def dev_y(d):
        return (z * NY + lax.rem(y + d + NY, NY), x, c)

    def dev_yabs(yy):
        return (z * NY + yy, x, c)

    def dev_col(yy):
        return (z * NY + yy, x, lax.div(yy, MATS))

    def dev_x(d):
        return (shard, lax.rem(x + d + NX, NX), c)

    partner = (shard, x, 1 - c)
    y_of = [c * MATS + m for m in range(MATS)]

    def rcopy(src, dst, ss, rs, dev):
        return pltpu.make_async_remote_copy(
            src_ref=src, dst_ref=dst, send_sem=ss, recv_sem=rs, device_id=dev, device_id_type=MESH
        )

    zn = near_first(NZ)
    zf = zn[::-1]
    yf = near_first(NY)[::-1]

    off_z = pl.multiple_of(z * ZR, ZR)
    loc = [
        pltpu.make_async_copy(grad.at[:, pl.ds(off_z, ZR), pl.ds(0, HC)], own_a, s_loc.at[0]),
        pltpu.make_async_copy(vec, vecv, s_loc.at[1]),
        pltpu.make_async_copy(wts, wtv, s_loc.at[2]),
        pltpu.make_async_copy(vecs, vecsv, s_loc.at[3]),
        pltpu.make_async_copy(fm, fmv, s_loc.at[4]),
        pltpu.make_async_copy(sm, smv, s_loc.at[5]),
    ]
    for cp in loc:
        cp.start()
    loc_ry = pltpu.make_async_copy(grad.at[my_m, :, pl.ds(HC, HC)], ry.at[y], s_loc.at[6])
    loc_mm = pltpu.make_async_copy(mom.at[my_m], mrx.at[y], s_loc.at[7])

    barrier = pltpu.get_barrier_semaphore()

    def greet(dev):
        pl.semaphore_signal(barrier, inc=1, device_id=dev, device_id_type=MESH)

    for d in range(1, NZ):
        greet(dev_z(d))
    for d in range(1, NY):
        greet(dev_y(d))
    for d in range(1, NX):
        greet(dev_x(d))
    greet(partner)
    for j in range(MATS):
        greet((z * NY + (1 - lax.div(y, MATS)) * MATS + j, x, 1 - c))
    pl.semaphore_wait(barrier, NZ - 1 + NY - 1 + NX - 1 + 1 + MATS)

    ph1a = {}
    for d in zf:
        dst_off = pl.multiple_of(at_z(d) * ZR, ZR)
        cp = rcopy(
            grad.at[:, pl.ds(dst_off, ZR), pl.ds(0, HC)], rz.at[d - 1],
            s_rz.at[d - 1], r_rz.at[d - 1], dev_z(d),
        )
        cp.start()
        ph1a[d] = cp
    for m in range(MATS):
        @pl.when(y != y_of[m])
        def _():
            rcopy(
                grad.at[m, :, pl.ds(HC, HC)], ry.at[y], s_ry.at[m], r_ry.at[y], dev_yabs(y_of[m])
            ).start()
    vz = []
    for d in range(1, NZ):
        cp = rcopy(vec, vrz.at[d - 1], s_vz.at[d - 1], r_vz.at[d - 1], dev_z(d))
        cp.start()
        vz.append(cp)
    for m in range(MATS):
        @pl.when(y != y_of[m])
        def _():
            rcopy(mom.at[m], mrx.at[y], s_mm.at[m], r_mm.at[y], dev_yabs(y_of[m])).start()

    @pl.when(active)
    def _():
        loc_ry.start()
        loc_mm.start()

    for cp in loc:
        cp.wait()
    for cp in vz:
        cp.wait_recv()
    vs = vecv[...].astype(f32)
    for d in range(1, NZ):
        vs = vs + vrz[d - 1].astype(f32)
    vsum[...] = vs
    vy = []
    for d in range(1, NY):
        cp = rcopy(vsum, vry.at[d - 1], s_vy.at[d - 1], r_vy.at[d - 1], dev_y(d))
        cp.start()
        vy.append(cp)

    @pl.when(active)
    def _():
        loc_mm.wait()
        for yy in range(NY):
            @pl.when(y != yy)
            def _():
                rcopy(mom.at[0], mrx.at[yy], s_mm.at[0], r_mm.at[yy], dev_yabs(yy)).wait_recv()
            mst[yy * LOCAL:(yy + 1) * LOCAL, :] = mrx[yy]

    acc_a[...] = own_a[...].astype(f32)
    for d in zn:
        ph1a[d].wait_recv()
        acc_a[...] += rz[d - 1].astype(f32)
    for m in range(MATS):
        @pl.when(y != y_of[m])
        def _():
            rcopy(acc_a.at[m], r2a.at[y], s_2a.at[m], r_2a.at[y], dev_yabs(y_of[m])).start()

    for cp in vy:
        cp.wait_recv()
    vt = vsum[...]
    for d in range(1, NY):
        vt = vt + vry[d - 1]

    def lane_sum(v):
        total = jnp.sum(v, axis=0, keepdims=True)
        out = total[:, :LANES]
        for k in range(1, v.shape[1] // LANES):
            out = out + total[:, k * LANES:(k + 1) * LANES]
        return out

    def b2(v):
        return jnp.broadcast_to(v, (1, LANES))

    my_row = x * ROWS + z * ZR
    my_off = pl.multiple_of(my_row, ZR)

    def column_sum():
        loc_ry.wait()
        r2a[y] = acc_a[my_m]
        for yy in range(NY):
            @pl.when(y != yy)
            def _():
                rcopy(
                    grad.at[0, :, pl.ds(HC, HC)], ry.at[yy], s_ry.at[0], r_ry.at[yy], dev_yabs(yy)
                ).wait_recv()
        ph2b = {}
        for d in zf + [0]:
            rows = pl.ds(pl.multiple_of(at_z(d) * ZR, ZR), ZR)
            tot = ry[0, rows, :].astype(f32)
            for yy in range(1, NY):
                tot = tot + ry[yy, rows, :].astype(f32)
            send_b[d] = tot
            if d > 0:
                cp = rcopy(send_b.at[d], r2b.at[d - 1], s_2b.at[d - 1], r_2b.at[d - 1], dev_z(d))
                cp.start()
                ph2b[d] = cp
        mm_sum = lane_sum(mst[...] * mst[...])
        for yy in range(NY):
            @pl.when(y != yy)
            def _():
                rcopy(acc_a.at[0], r2a.at[yy], s_2a.at[0], r_2a.at[yy], dev_yabs(yy)).wait_recv()
        tot = r2a[0]
        for yy in range(1, NY):
            tot = tot + r2a[yy]
        gbuf[:, :HC] = tot
        tot = send_b[0]
        for d in zn:
            ph2b[d].wait_recv()
            tot = tot + r2b[d - 1]
        gbuf[:, HC:] = tot

        gv = gbuf[...]
        gg = lane_sum(gv * gv)
        stat[...] = jnp.zeros_like(stat)
        stat[0:1, :] = gg
        stat[1:2, :] = lane_sum(gv * mst[...])
        stat[2:3, :] = mm_sum
        stat[3:4, :] = gg + lane_sum(vt * vt) * (1.0 / (NZ * MATS))
        st = []
        for d in zf:
            cp = rcopy(stat, srz.at[d - 1], s_sz.at[d - 1], r_sz.at[d - 1], dev_z(d))
            cp.start()
            st.append(cp)
        for cp in st:
            cp.wait()
        tot = stat[...]
        for d in range(1, NZ):
            tot = tot + srz[d - 1]
        stat[...] = tot
        st = []
        for d in range(1, NX):
            cp = rcopy(stat, srx.at[d - 1], s_sx.at[d - 1], r_sx.at[d - 1], dev_x(d))
            cp.start()
            st.append(cp)
        for cp in st:
            cp.wait()
        for d in range(1, NX):
            tot = tot + srx[d - 1]
        stat[...] = tot
        for yy in range(NY):
            @pl.when(y != yy)
            def _():
                rcopy(stat, sry.at[y], s_sy.at[yy], r_sy.at[y], dev_col(yy)).start()
        sry[y] = tot
        for yy in range(NY):
            @pl.when(y != yy)
            def _():
                rcopy(stat, sry.at[yy], s_sy.at[yy], r_sy.at[yy], dev_col(yy)).wait()
        grand = sry[0, 3:4, :]
        for yy in range(1, NY):
            grand = grand + sry[yy, 3:4, :]
        grand_total = jnp.sum(grand, axis=1, keepdims=True)
        own = jnp.sum(tot, axis=1, keepdims=True)
        clip = jnp.minimum(1.0, max_norm / (jnp.sqrt(grand_total) + 1e-06))
        stat2[...] = jnp.broadcast_to(clip, stat2.shape)
        rcopy(stat2, clipb, s_cl.at[0], r_cl.at[0], partner).start()
        cc = (1.0 + mom_beta) * clip
        bb = mom_beta * mom_beta
        norm2 = jnp.maximum(cc * cc * own[0:1] + (2.0 * bb) * cc * own[1:2] + (bb * bb) * own[2:3], 0.0)
        inv = 1.0 / (jnp.sqrt(norm2) + 1e-07)
        return clip, inv

    def block(dz, dx):
        row = lax.rem(x + dx + NX, NX) * ROWS + at_z(dz) * ZR
        return X.at[pl.ds(pl.multiple_of(row, ZR), ZR), :]

    def adam(clip):
        vlane = lax.broadcasted_iota(jnp.int32, vt.shape, 1)
        for k in range(LOCAL):
            vg = clip * jnp.sum(jnp.where(vlane == shard * LOCAL + k, vt, 0.0), axis=1, keepdims=True)
            uf = 0.9 * fmv[:, k:k + 1] + 0.1 * vg
            us = 0.999 * smv[:, k:k + 1] + 0.001 * vg * vg
            ad = uf / (jnp.sqrt(us) + 1e-08)
            adam_dir[:, k:k + 1] = ad
            new_vecs[:, k:k + 1] = vecsv[:, k:k + 1] * (1.0 - adam_rate * adam_decay) - adam_rate * ad

    TILE = min(256, D)
    NT = D // TILE
    dn0 = (((0,), (0,)), ((), ()))

    def block_gram(src, xb, first, last):
        rows = pl.ds(pl.multiple_of(xb * ROWS, ROWS), ROWS)

        @pl.loop(0, NT)
        def _(j):
            cols = pl.ds(pl.multiple_of(j * TILE, TILE), TILE)
            pr = lax.dot_general(
                src[rows, :], src[rows, cols], dn0, preferred_element_type=f32
            ).astype(bf16).astype(f32)
            if first:
                gacc[:, cols] = pr
            elif last:
                G[:, cols] = (gacc[:, cols] + pr).astype(bf16)
            else:
                gacc[:, cols] += pr

    def step(rows):
        p1 = jnp.dot(rows, G[...], preferred_element_type=f32).astype(bf16)
        p2 = jnp.dot(p1, G[...], preferred_element_type=f32)
        return ns_first * rows.astype(f32) + ns_second * p1.astype(f32) + ns_third * p2

    @pl.when(active)
    def _():
        clip, inv = column_sum()
        cg = clip * gbuf[...]
        nm = mom_beta * mst[...] + cg
        X[pl.ds(my_off, ZR), :] = ((cg + mom_beta * nm) * inv).astype(bf16)

        mine = block(0, 0)
        zc = {}
        xc = {}
        fwd = []

        def send_x(k):
            b = block(-k, 0)
            right = rcopy(b, b, s_gr.at[k], r_gr.at[k], dev_x(1))
            left = rcopy(b, b, s_gl.at[k], r_gl.at[k], dev_x(-1))
            right.start()
            left.start()
            xc[k] = (right, left)

        def forward(k):
            xc[k][0].wait_recv()
            if k % 2 == 0:
                b = block(-k, -1)
                cp = rcopy(b, b, s_fr.at[k], r_fr.at[k], dev_x(1))
                cp.start()
                fwd.append(cp)
            xc[k][1].wait_recv()
            if k % 2 == 1:
                b = block(-k, 1)
                cp = rcopy(b, b, s_fl.at[k], r_fl.at[k], dev_x(-1))
                cp.start()
                fwd.append(cp)

        for d in zf:
            cp = rcopy(mine, mine, s_gz.at[d - 1], r_gz.at[d - 1], dev_z(d))
            cp.start()
            zc[d] = cp
        send_x(0)

        for yy in range(NY):
            nms[yy] = nm[yy * LOCAL:(yy + 1) * LOCAL, :]
        new_mom[my_m] = nms[y]
        for yy in range(NY):
            @pl.when(y != yy)
            def _():
                rcopy(nms.at[yy], new_mom.at[my_m], s_nm.at[yy], r_nm.at[my_m], dev_yabs(yy)).start()
        adam(clip)

        order = [0] + zn
        for i, k in enumerate(order):
            if k > 0:
                zc[k].wait_recv()
                send_x(k)
            if i >= 3:
                forward(order[i - 3])
        block_gram(X, x, True, False)
        for k in order[-3:]:
            forward(k)
        block_gram(X, lax.rem(x + NX - 1, NX), False, False)
        block_gram(X, lax.rem(x + 1, NX), False, False)
        for cp in fwd:
            cp.wait()
        block_gram(X, lax.rem(x + 2, NX), False, True)

        @pl.loop(0, NX)
        def _(i):
            rows = pl.ds(pl.multiple_of(i * ROWS, ROWS), ROWS)
            X1[rows, :] = step(X[rows, :]).astype(bf16)

        for b in range(NX):
            block_gram(X1, b, b == 0, b == NX - 1)
        last = step(X1[pl.ds(my_off, ZR), :])
        for yy in range(NY):
            ret[yy] = last[yy * LOCAL:(yy + 1) * LOCAL, :].astype(bf16)
        for yy in range(NY):
            @pl.when(y != yy)
            def _():
                rcopy(ret.at[yy], upd_out.at[my_m], s_rt.at[yy], r_rt.at[my_m], dev_yabs(yy)).start()
        upd_out[my_m] = ret[y]
        for k in order:
            xc[k][0].wait_send()
            xc[k][1].wait_send()
        for d in zf:
            zc[d].wait_send()
            rcopy(send_b.at[d], r2b.at[d - 1], s_2b.at[d - 1], r_2b.at[d - 1], dev_z(d)).wait_send()
        rcopy(stat2, clipb, s_cl.at[0], r_cl.at[0], partner).wait_send()

    @pl.when(jnp.logical_not(active))
    def _():
        rcopy(stat2, clipb, s_cl.at[0], r_cl.at[0], partner).wait_recv()
        adam(clipb[0:1, 0:1])

    for d in zn:
        ph1a[d].wait_send()
    for cp in vz + vy:
        cp.wait_send()
    for m in range(MATS):
        @pl.when(y != y_of[m])
        def _():
            rcopy(
                grad.at[m, :, pl.ds(HC, HC)], ry.at[y], s_ry.at[m], r_ry.at[y], dev_yabs(y_of[m])
            ).wait_send()
            rcopy(mom.at[m], mrx.at[y], s_mm.at[m], r_mm.at[y], dev_yabs(y_of[m])).wait_send()
            rcopy(acc_a.at[m], r2a.at[y], s_2a.at[m], r_2a.at[y], dev_yabs(y_of[m])).wait_send()

    muon_scale = 0.2 * math.sqrt(D)
    for m in range(MATS):
        @pl.when(y != y_of[m])
        def _():
            rcopy(nms.at[0], new_mom.at[m], s_nm.at[0], r_nm.at[m], dev_yabs(y_of[m])).wait_recv()
            rcopy(ret.at[0], upd_out.at[m], s_rt.at[0], r_rt.at[m], dev_yabs(y_of[m])).wait_recv()
        new_wts[m] = (
            wtv[m].astype(f32) * (1.0 - muon_rate * muon_decay)
            - muon_rate * muon_scale * upd_out[m].astype(f32)
        ).astype(bf16)

    @pl.when(active)
    def _():
        for yy in range(NY):
            @pl.when(y != yy)
            def _():
                rcopy(nms.at[yy], new_mom.at[my_m], s_nm.at[yy], r_nm.at[my_m], dev_yabs(yy)).wait_send()
                rcopy(ret.at[yy], upd_out.at[my_m], s_rt.at[yy], r_rt.at[my_m], dev_yabs(yy)).wait_send()


def build(mesh_shape, NZ, NY, MATS, LOCAL, D):
    NX = mesh_shape["tensor"]
    ROWS = NZ * NY * LOCAL
    ZR = NY * LOCAL
    HC = D // 2
    DMA = pltpu.SemaphoreType.DMA
    V = pltpu.VMEM
    scratch = [
        V((MATS, ROWS), bf16),
        V((MATS, LOCAL, D), bf16),
        V((MATS, LOCAL), f32),
        V((MATS, LOCAL), f32),
        V((MATS, LOCAL), f32),
        V((MATS, ZR, HC), bf16),
        V((MATS, ZR, HC), f32),
        V((NZ - 1, MATS, ZR, HC), bf16),
        V((NY, ROWS, HC), bf16),
        V((NZ, ZR, HC), f32),
        V((NY, ZR, HC), f32),
        V((NZ - 1, ZR, HC), f32),
        V((NY, LOCAL, D), f32),
        V((ZR, D), f32),
        V((ZR, D), f32),
        V((NY, LOCAL, D), f32),
        V((NZ - 1, MATS, ROWS), bf16),
        V((NY - 1, MATS, ROWS), f32),
        V((MATS, ROWS), f32),
        V((8, LANES), f32),
        V((NZ - 1, 8, LANES), f32),
        V((NX - 1, 8, LANES), f32),
        V((NY, 8, LANES), f32),
        V((8, LANES), f32),
        V((8, LANES), f32),
        V((NX * ROWS, D), bf16),
        V((D, D), bf16),
        V((NX * ROWS, D), bf16),
        V((D, D), f32),
        V((NY, LOCAL, D), bf16),
        DMA((8,)),
        DMA((NZ - 1,)), DMA((NZ - 1,)), DMA((MATS,)), DMA((NY,)),
        DMA((MATS,)), DMA((NY,)), DMA((NZ - 1,)), DMA((NZ - 1,)), DMA((MATS,)), DMA((NY,)),
        DMA((NZ - 1,)), DMA((NZ - 1,)), DMA((NY - 1,)), DMA((NY - 1,)),
        DMA((NZ - 1,)), DMA((NZ - 1,)), DMA((NX - 1,)), DMA((NX - 1,)), DMA((NY,)), DMA((NY,)),
        DMA((1,)), DMA((1,)),
        DMA((NZ - 1,)), DMA((NZ - 1,)),
        DMA((NZ,)), DMA((NZ,)), DMA((NZ,)), DMA((NZ,)),
        DMA((NZ,)), DMA((NZ,)), DMA((NZ,)), DMA((NZ,)),
        DMA((NY,)), DMA((MATS,)), DMA((NY,)), DMA((MATS,)),
    ]
    vm = pl.BlockSpec(memory_space=pltpu.VMEM)
    hbm = pl.BlockSpec(memory_space=pltpu.HBM)
    return pl.pallas_call(
        functools.partial(kernel, NZ, NY, NX, MATS, LOCAL, D),
        out_shape=(
            jax.ShapeDtypeStruct((MATS, LOCAL, D), f32),
            jax.ShapeDtypeStruct((MATS, LOCAL, D), bf16),
            jax.ShapeDtypeStruct((MATS, LOCAL, D), bf16),
            jax.ShapeDtypeStruct((MATS, LOCAL), f32),
            jax.ShapeDtypeStruct((MATS, LOCAL), f32),
        ),
        in_specs=[hbm] * 7,
        out_specs=(vm,) * 5,
        scratch_shapes=scratch,
        compiler_params=pltpu.CompilerParams(
            collective_id=0, has_side_effects=True, vmem_limit_bytes=48 << 20
        ),
    )


def solution(mesh, NZ=8, NY=8):
    def per_device(grad_parts, vector_grads, momentum, weights, vectors, first_moment, second_moment):
        MATS, LOCAL, WIDTH = momentum.shape[1:]
        call = build(mesh.shape, NZ, NY, MATS, LOCAL, WIDTH)
        outs = call(
            grad_parts[0, 0], vector_grads[0, 0], momentum[0], weights[0],
            vectors[0], first_moment[0], second_moment[0],
        )
        return tuple(o[None] for o in outs)

    rows = P("section", None, ("tensor", "shard"), None)
    cols = P("section", None, ("tensor", "shard"))
    return jax.shard_map(
        per_device,
        mesh=mesh,
        in_specs=(
            P("shard", "section", None, "tensor", None),
            P("shard", "section", None, "tensor"),
            rows, rows, cols, cols, cols,
        ),
        out_specs=(rows, rows, rows, cols, cols),
        check_vma=False,
    )
```

```python
import functools
import math

import jax
import jax.numpy as jnp
from jax import lax
from jax.experimental import pallas as pl
from jax.experimental.pallas import tpu as pltpu
from jax.sharding import PartitionSpec as P


ns_first = 3.4445
ns_second = -4.775
ns_third = 2.0315
mom_beta = 0.95
max_norm = 1024.0
muon_rate = 0.02
muon_decay = 0.1
adam_rate = 0.001
adam_decay = 0.01

MESH = pl.DeviceIdType.MESH
f32 = jnp.float32
bf16 = jnp.bfloat16
LANES = 128


def near_first(n):
    order = []
    for d in range(1, n // 2 + 1):
        order.append(d)
        if n - d != d:
            order.append(n - d)
    return order


def relay_plan(n):
    if n == 8:
        return [(4, 5), (3, 2), (6, 7)], [1]
    if n == 4:
        return [(2, 3)], [1]
    return [], list(range(1, n))


def kernel(
    NZ, NY, NX, MATS, LOCAL, D,
    grad, vec, mom, wts, vecs, fm, sm,
    new_mom, upd_out, new_wts, adam_dir, new_vecs,
    vecv, wtv, vecsv, fmv, smv,
    own_a, ownp, p1a, out_a, ra, acc_a, ownb, p1b, out_b, rb, send_b, r2a, r2b, mrx, mst, gbuf, nms,
    vrz, vry, vsum, stat, srz, srx, sry, stat2, clipb, X, G, X1, gacc, ret,
    s_loc, s_p1a, r_p1a, s_ra, r_ra, s_p1b, r_p1b, s_rb, r_rb, s_2a, r_2a, s_2b, r_2b, s_mm, r_mm,
    s_vz, r_vz, s_vy, r_vy, s_sz, r_sz, s_sx, r_sx, s_sy, r_sy, s_cl, r_cl,
    s_gz, r_gz, s_gl, s_gr, r_gl, r_gr, s_fl, s_fr, r_fl, r_fr,
    s_nm, r_nm, s_rt, r_rt,
):
    ROWS = NZ * NY * LOCAL
    ZR = NY * LOCAL
    HC = D // 2
    shard = lax.axis_index("shard")
    x = lax.axis_index("tensor")
    c = lax.axis_index("section")
    z = lax.div(shard, NY)
    y = lax.rem(shard, NY)
    active = lax.div(y, MATS) == c
    my_m = lax.rem(y, MATS)

    def at_z(d):
        return lax.rem(z + d + NZ, NZ)

    def dev_z(d):
        return (at_z(d) * NY + y, x, c)

    def dev_y(d):
        return (z * NY + lax.rem(y + d + NY, NY), x, c)

    def dev_yabs(yy):
        return (z * NY + yy, x, c)

    def dev_col(yy):
        return (z * NY + yy, x, lax.div(yy, MATS))

    def dev_x(d):
        return (shard, lax.rem(x + d + NX, NX), c)

    partner = (shard, x, 1 - c)
    y_of = [c * MATS + m for m in range(MATS)]

    def rcopy(src, dst, ss, rs, dev):
        return pltpu.make_async_remote_copy(
            src_ref=src, dst_ref=dst, send_sem=ss, recv_sem=rs, device_id=dev, device_id_type=MESH
        )

    zn = near_first(NZ)
    zf = zn[::-1]
    yf = near_first(NY)[::-1]

    sg = 1 - 2 * c
    pairs_z, single_z = relay_plan(NZ)
    pairs_y, single_y = relay_plan(NY)

    def zt(o):
        return lax.rem(z - sg * o + 2 * NZ, NZ)

    def yt(o):
        return lax.rem(y - sg * o + 2 * NY, NY)

    def dev_zabs(zz):
        return (zz * NY + y, x, c)

    def chunk_a(zz):
        return grad.at[:, pl.ds(pl.multiple_of(zz * ZR, ZR), ZR), pl.ds(0, HC)]

    def chunk_b(m):
        return grad.at[m, :, pl.ds(HC, HC)]

    o_of = [lax.rem(sg * (y - y_of[m]) + 2 * NY, NY) for m in range(MATS)]

    loc = [
        pltpu.make_async_copy(chunk_a(z), own_a, s_loc.at[0]),
        pltpu.make_async_copy(grad.at[:, :, pl.ds(HC, HC)], ownb, s_loc.at[1]),
        pltpu.make_async_copy(vec, vecv, s_loc.at[2]),
        pltpu.make_async_copy(wts, wtv, s_loc.at[3]),
        pltpu.make_async_copy(vecs, vecsv, s_loc.at[4]),
        pltpu.make_async_copy(fm, fmv, s_loc.at[5]),
        pltpu.make_async_copy(sm, smv, s_loc.at[6]),
    ]
    for i, (_, g) in enumerate(pairs_z):
        loc.append(pltpu.make_async_copy(chunk_a(zt(g)), ownp.at[i], s_loc.at[8 + i]))
    for cp in loc:
        cp.start()
    loc_mm = pltpu.make_async_copy(mom.at[my_m], mrx.at[y], s_loc.at[7])

    barrier = pltpu.get_barrier_semaphore()

    def greet(dev):
        pl.semaphore_signal(barrier, inc=1, device_id=dev, device_id_type=MESH)

    for d in range(1, NZ):
        greet(dev_z(d))
    for d in range(1, NY):
        greet(dev_y(d))
    for d in range(1, NX):
        greet(dev_x(d))
    greet(partner)
    for j in range(MATS):
        greet((z * NY + (1 - lax.div(y, MATS)) * MATS + j, x, 1 - c))
    pl.semaphore_wait(barrier, NZ - 1 + NY - 1 + NX - 1 + 1 + MATS)

    first_a = []
    for i, (f, g) in enumerate(pairs_z):
        cp = rcopy(chunk_a(zt(f)), p1a.at[i], s_p1a.at[i], r_p1a.at[i], dev_zabs(zt(f - g)))
        cp.start()
        first_a.append(cp)

    def first_b(m, f, g):
        return rcopy(chunk_b(m), p1b.at[m], s_p1b.at[m], r_p1b.at[m], dev_yabs(yt(f - g)))

    def single_b(m, o):
        return rcopy(chunk_b(m), rb.at[o], s_rb.at[m], r_rb.at[o], dev_yabs(y_of[m]))

    def second_b(m):
        return rcopy(out_b.at[m], rb.at[o_of[m]], s_rb.at[m], r_rb.at[o_of[m]], dev_yabs(y_of[m]))

    def is_relay(m):
        hit = o_of[m] == pairs_y[0][1]
        for _, g in pairs_y[1:]:
            hit = jnp.logical_or(hit, o_of[m] == g)
        return hit

    for m in range(MATS):
        for f, g in pairs_y:
            @pl.when(o_of[m] == f)
            def _():
                first_b(m, f, g).start()
    last_a = {}
    for o in single_z:
        cp = rcopy(chunk_a(zt(o)), ra.at[o], s_ra.at[o], r_ra.at[o], dev_zabs(zt(o)))
        cp.start()
        last_a[o] = cp
    for m in range(MATS):
        for o in single_y:
            @pl.when(o_of[m] == o)
            def _():
                single_b(m, o).start()
    vz = []
    for d in range(1, NZ):
        cp = rcopy(vec, vrz.at[d - 1], s_vz.at[d - 1], r_vz.at[d - 1], dev_z(d))
        cp.start()
        vz.append(cp)
    for m in range(MATS):
        @pl.when(y != y_of[m])
        def _():
            rcopy(mom.at[m], mrx.at[y], s_mm.at[m], r_mm.at[y], dev_yabs(y_of[m])).start()

    @pl.when(active)
    def _():
        loc_mm.start()

    for cp in loc:
        cp.wait()
    for i, (f, g) in enumerate(pairs_z):
        first_a[i].wait_recv()
        out_a[i] = (ownp[i].astype(f32) + p1a[i].astype(f32)).astype(bf16)
        cp = rcopy(out_a.at[i], ra.at[g], s_ra.at[g], r_ra.at[g], dev_zabs(zt(g)))
        cp.start()
        last_a[g] = cp
    if pairs_y:
        for m in range(MATS):
            @pl.when(is_relay(m))
            def _():
                rcopy(chunk_b(m), p1b.at[m], s_p1b.at[m], r_p1b.at[m], dev_yabs(y)).wait_recv()
                out_b[m] = (ownb[m].astype(f32) + p1b[m].astype(f32)).astype(bf16)
                second_b(m).start()

    for cp in vz:
        cp.wait_recv()
    vs = vecv[...].astype(f32)
    for d in range(1, NZ):
        vs = vs + vrz[d - 1].astype(f32)
    vsum[...] = vs
    vy = []
    for d in range(1, NY):
        cp = rcopy(vsum, vry.at[d - 1], s_vy.at[d - 1], r_vy.at[d - 1], dev_y(d))
        cp.start()
        vy.append(cp)

    @pl.when(active)
    def _():
        loc_mm.wait()
        for yy in range(NY):
            @pl.when(y != yy)
            def _():
                rcopy(mom.at[0], mrx.at[yy], s_mm.at[0], r_mm.at[yy], dev_yabs(yy)).wait_recv()
            mst[yy * LOCAL:(yy + 1) * LOCAL, :] = mrx[yy]

    acc_a[...] = own_a[...].astype(f32)
    for o in single_z + [g for _, g in pairs_z[::-1]]:
        last_a[o].wait_recv()
        acc_a[...] += ra[o].astype(f32)
    for m in range(MATS):
        @pl.when(y != y_of[m])
        def _():
            rcopy(acc_a.at[m], r2a.at[y], s_2a.at[m], r_2a.at[y], dev_yabs(y_of[m])).start()

    for cp in vy:
        cp.wait_recv()
    vt = vsum[...]
    for d in range(1, NY):
        vt = vt + vry[d - 1]

    def lane_sum(v):
        total = jnp.sum(v, axis=0, keepdims=True)
        out = total[:, :LANES]
        for k in range(1, v.shape[1] // LANES):
            out = out + total[:, k * LANES:(k + 1) * LANES]
        return out

    def b2(v):
        return jnp.broadcast_to(v, (1, LANES))

    my_row = x * ROWS + z * ZR
    my_off = pl.multiple_of(my_row, ZR)

    def column_sum():
        r2a[y] = acc_a[my_m]
        sources = single_y + [g for _, g in pairs_y]
        for o in sources:
            rcopy(chunk_b(0), rb.at[o], s_rb.at[0], r_rb.at[o], dev_yabs(y)).wait_recv()
        ph2b = {}
        for d in zf + [0]:
            rows = pl.ds(pl.multiple_of(at_z(d) * ZR, ZR), ZR)
            tot = ownb[my_m, rows, :].astype(f32)
            for o in sources:
                tot = tot + rb[o, rows, :].astype(f32)
            send_b[d] = tot
            if d > 0:
                cp = rcopy(send_b.at[d], r2b.at[d - 1], s_2b.at[d - 1], r_2b.at[d - 1], dev_z(d))
                cp.start()
                ph2b[d] = cp
        mm_sum = lane_sum(mst[...] * mst[...])
        for yy in range(NY):
            @pl.when(y != yy)
            def _():
                rcopy(acc_a.at[0], r2a.at[yy], s_2a.at[0], r_2a.at[yy], dev_yabs(yy)).wait_recv()
        tot = r2a[0]
        for yy in range(1, NY):
            tot = tot + r2a[yy]
        gbuf[:, :HC] = tot
        tot = send_b[0]
        for d in zn:
            ph2b[d].wait_recv()
            tot = tot + r2b[d - 1]
        gbuf[:, HC:] = tot

        gv = gbuf[...]
        gg = lane_sum(gv * gv)
        stat[...] = jnp.zeros_like(stat)
        stat[0:1, :] = gg
        stat[1:2, :] = lane_sum(gv * mst[...])
        stat[2:3, :] = mm_sum
        stat[3:4, :] = gg + lane_sum(vt * vt) * (1.0 / (NZ * MATS))
        st = []
        for d in zf:
            cp = rcopy(stat, srz.at[d - 1], s_sz.at[d - 1], r_sz.at[d - 1], dev_z(d))
            cp.start()
            st.append(cp)
        for cp in st:
            cp.wait()
        tot = stat[...]
        for d in range(1, NZ):
            tot = tot + srz[d - 1]
        stat[...] = tot
        st = []
        for d in range(1, NX):
            cp = rcopy(stat, srx.at[d - 1], s_sx.at[d - 1], r_sx.at[d - 1], dev_x(d))
            cp.start()
            st.append(cp)
        for cp in st:
            cp.wait()
        for d in range(1, NX):
            tot = tot + srx[d - 1]
        stat[...] = tot
        for yy in range(NY):
            @pl.when(y != yy)
            def _():
                rcopy(stat, sry.at[y], s_sy.at[yy], r_sy.at[y], dev_col(yy)).start()
        sry[y] = tot
        for yy in range(NY):
            @pl.when(y != yy)
            def _():
                rcopy(stat, sry.at[yy], s_sy.at[yy], r_sy.at[yy], dev_col(yy)).wait()
        grand = sry[0, 3:4, :]
        for yy in range(1, NY):
            grand = grand + sry[yy, 3:4, :]
        grand_total = jnp.sum(grand, axis=1, keepdims=True)
        own = jnp.sum(tot, axis=1, keepdims=True)
        clip = jnp.minimum(1.0, max_norm / (jnp.sqrt(grand_total) + 1e-06))
        stat2[...] = jnp.broadcast_to(clip, stat2.shape)
        rcopy(stat2, clipb, s_cl.at[0], r_cl.at[0], partner).start()
        cc = (1.0 + mom_beta) * clip
        bb = mom_beta * mom_beta
        norm2 = jnp.maximum(cc * cc * own[0:1] + (2.0 * bb) * cc * own[1:2] + (bb * bb) * own[2:3], 0.0)
        inv = 1.0 / (jnp.sqrt(norm2) + 1e-07)
        return clip, inv

    def block(dz, dx):
        row = lax.rem(x + dx + NX, NX) * ROWS + at_z(dz) * ZR
        return X.at[pl.ds(pl.multiple_of(row, ZR), ZR), :]

    def adam(clip):
        vlane = lax.broadcasted_iota(jnp.int32, vt.shape, 1)
        for k in range(LOCAL):
            vg = clip * jnp.sum(jnp.where(vlane == shard * LOCAL + k, vt, 0.0), axis=1, keepdims=True)
            uf = 0.9 * fmv[:, k:k + 1] + 0.1 * vg
            us = 0.999 * smv[:, k:k + 1] + 0.001 * vg * vg
            ad = uf / (jnp.sqrt(us) + 1e-08)
            adam_dir[:, k:k + 1] = ad
            new_vecs[:, k:k + 1] = vecsv[:, k:k + 1] * (1.0 - adam_rate * adam_decay) - adam_rate * ad

    TILE = min(256, D)
    NT = D // TILE
    dn0 = (((0,), (0,)), ((), ()))

    def block_gram(src, xb, first, last):
        rows = pl.ds(pl.multiple_of(xb * ROWS, ROWS), ROWS)

        @pl.loop(0, NT)
        def _(j):
            cols = pl.ds(pl.multiple_of(j * TILE, TILE), TILE)
            pr = lax.dot_general(
                src[rows, :], src[rows, cols], dn0, preferred_element_type=f32
            ).astype(bf16).astype(f32)
            if first:
                gacc[:, cols] = pr
            elif last:
                G[:, cols] = (gacc[:, cols] + pr).astype(bf16)
            else:
                gacc[:, cols] += pr

    def step(rows):
        p1 = jnp.dot(rows, G[...], preferred_element_type=f32).astype(bf16)
        p2 = jnp.dot(p1, G[...], preferred_element_type=f32)
        return ns_first * rows.astype(f32) + ns_second * p1.astype(f32) + ns_third * p2

    @pl.when(active)
    def _():
        clip, inv = column_sum()
        cg = clip * gbuf[...]
        nm = mom_beta * mst[...] + cg
        X[pl.ds(my_off, ZR), :] = ((cg + mom_beta * nm) * inv).astype(bf16)

        mine = block(0, 0)
        zc = {}
        xc = {}
        fwd = []

        def send_x(k):
            b = block(-k, 0)
            right = rcopy(b, b, s_gr.at[k], r_gr.at[k], dev_x(1))
            left = rcopy(b, b, s_gl.at[k], r_gl.at[k], dev_x(-1))
            right.start()
            left.start()
            xc[k] = (right, left)

        def forward(k):
            xc[k][0].wait_recv()
            if k % 2 == 0:
                b = block(-k, -1)
                cp = rcopy(b, b, s_fr.at[k], r_fr.at[k], dev_x(1))
                cp.start()
                fwd.append(cp)
            xc[k][1].wait_recv()
            if k % 2 == 1:
                b = block(-k, 1)
                cp = rcopy(b, b, s_fl.at[k], r_fl.at[k], dev_x(-1))
                cp.start()
                fwd.append(cp)

        for d in zf:
            cp = rcopy(mine, mine, s_gz.at[d - 1], r_gz.at[d - 1], dev_z(d))
            cp.start()
            zc[d] = cp
        send_x(0)

        for yy in range(NY):
            nms[yy] = nm[yy * LOCAL:(yy + 1) * LOCAL, :]
        new_mom[my_m] = nms[y]
        for yy in range(NY):
            @pl.when(y != yy)
            def _():
                rcopy(nms.at[yy], new_mom.at[my_m], s_nm.at[yy], r_nm.at[my_m], dev_yabs(yy)).start()
        adam(clip)

        order = [0] + zn
        for i, k in enumerate(order):
            if k > 0:
                zc[k].wait_recv()
                send_x(k)
            if i >= 3:
                forward(order[i - 3])
        block_gram(X, x, True, False)
        for k in order[-3:]:
            forward(k)
        block_gram(X, lax.rem(x + NX - 1, NX), False, False)
        block_gram(X, lax.rem(x + 1, NX), False, False)
        for cp in fwd:
            cp.wait()
        block_gram(X, lax.rem(x + 2, NX), False, True)

        @pl.loop(0, NX)
        def _(i):
            rows = pl.ds(pl.multiple_of(i * ROWS, ROWS), ROWS)
            X1[rows, :] = step(X[rows, :]).astype(bf16)

        for b in range(NX):
            block_gram(X1, b, b == 0, b == NX - 1)
        last = step(X1[pl.ds(my_off, ZR), :])
        for yy in range(NY):
            ret[yy] = last[yy * LOCAL:(yy + 1) * LOCAL, :].astype(bf16)
        for yy in range(NY):
            @pl.when(y != yy)
            def _():
                rcopy(ret.at[yy], upd_out.at[my_m], s_rt.at[yy], r_rt.at[my_m], dev_yabs(yy)).start()
        upd_out[my_m] = ret[y]
        for k in order:
            xc[k][0].wait_send()
            xc[k][1].wait_send()
        for d in zf:
            zc[d].wait_send()
            rcopy(send_b.at[d], r2b.at[d - 1], s_2b.at[d - 1], r_2b.at[d - 1], dev_z(d)).wait_send()
        rcopy(stat2, clipb, s_cl.at[0], r_cl.at[0], partner).wait_send()

    @pl.when(jnp.logical_not(active))
    def _():
        rcopy(stat2, clipb, s_cl.at[0], r_cl.at[0], partner).wait_recv()
        adam(clipb[0:1, 0:1])

    for cp in first_a + list(last_a.values()):
        cp.wait_send()
    for m in range(MATS):
        for f, g in pairs_y:
            @pl.when(o_of[m] == f)
            def _():
                first_b(m, f, g).wait_send()

            @pl.when(o_of[m] == g)
            def _():
                second_b(m).wait_send()
        for o in single_y:
            @pl.when(o_of[m] == o)
            def _():
                single_b(m, o).wait_send()
    for cp in vz + vy:
        cp.wait_send()
    for m in range(MATS):
        @pl.when(y != y_of[m])
        def _():
            rcopy(mom.at[m], mrx.at[y], s_mm.at[m], r_mm.at[y], dev_yabs(y_of[m])).wait_send()
            rcopy(acc_a.at[m], r2a.at[y], s_2a.at[m], r_2a.at[y], dev_yabs(y_of[m])).wait_send()

    muon_scale = 0.2 * math.sqrt(D)
    for m in range(MATS):
        @pl.when(y != y_of[m])
        def _():
            rcopy(nms.at[0], new_mom.at[m], s_nm.at[0], r_nm.at[m], dev_yabs(y_of[m])).wait_recv()
            rcopy(ret.at[0], upd_out.at[m], s_rt.at[0], r_rt.at[m], dev_yabs(y_of[m])).wait_recv()
        new_wts[m] = (
            wtv[m].astype(f32) * (1.0 - muon_rate * muon_decay)
            - muon_rate * muon_scale * upd_out[m].astype(f32)
        ).astype(bf16)

    @pl.when(active)
    def _():
        for yy in range(NY):
            @pl.when(y != yy)
            def _():
                rcopy(nms.at[yy], new_mom.at[my_m], s_nm.at[yy], r_nm.at[my_m], dev_yabs(yy)).wait_send()
                rcopy(ret.at[yy], upd_out.at[my_m], s_rt.at[yy], r_rt.at[my_m], dev_yabs(yy)).wait_send()


def build(mesh_shape, NZ, NY, MATS, LOCAL, D):
    NX = mesh_shape["tensor"]
    ROWS = NZ * NY * LOCAL
    ZR = NY * LOCAL
    HC = D // 2
    DMA = pltpu.SemaphoreType.DMA
    V = pltpu.VMEM
    scratch = [
        V((MATS, ROWS), bf16),
        V((MATS, LOCAL, D), bf16),
        V((MATS, LOCAL), f32),
        V((MATS, LOCAL), f32),
        V((MATS, LOCAL), f32),
        V((MATS, ZR, HC), bf16),
        V((3, MATS, ZR, HC), bf16),
        V((3, MATS, ZR, HC), bf16),
        V((3, MATS, ZR, HC), bf16),
        V((NZ, MATS, ZR, HC), bf16),
        V((MATS, ZR, HC), f32),
        V((MATS, ROWS, HC), bf16),
        V((MATS, ROWS, HC), bf16),
        V((MATS, ROWS, HC), bf16),
        V((NY, ROWS, HC), bf16),
        V((NZ, ZR, HC), f32),
        V((NY, ZR, HC), f32),
        V((NZ - 1, ZR, HC), f32),
        V((NY, LOCAL, D), f32),
        V((ZR, D), f32),
        V((ZR, D), f32),
        V((NY, LOCAL, D), f32),
        V((NZ - 1, MATS, ROWS), bf16),
        V((NY - 1, MATS, ROWS), f32),
        V((MATS, ROWS), f32),
        V((8, LANES), f32),
        V((NZ - 1, 8, LANES), f32),
        V((NX - 1, 8, LANES), f32),
        V((NY, 8, LANES), f32),
        V((8, LANES), f32),
        V((8, LANES), f32),
        V((NX * ROWS, D), bf16),
        V((D, D), bf16),
        V((NX * ROWS, D), bf16),
        V((D, D), f32),
        V((NY, LOCAL, D), bf16),
        DMA((11,)),
        DMA((3,)), DMA((3,)), DMA((NZ,)), DMA((NZ,)), DMA((MATS,)), DMA((MATS,)), DMA((MATS,)), DMA((NY,)),
        DMA((MATS,)), DMA((NY,)), DMA((NZ - 1,)), DMA((NZ - 1,)), DMA((MATS,)), DMA((NY,)),
        DMA((NZ - 1,)), DMA((NZ - 1,)), DMA((NY - 1,)), DMA((NY - 1,)),
        DMA((NZ - 1,)), DMA((NZ - 1,)), DMA((NX - 1,)), DMA((NX - 1,)), DMA((NY,)), DMA((NY,)),
        DMA((1,)), DMA((1,)),
        DMA((NZ - 1,)), DMA((NZ - 1,)),
        DMA((NZ,)), DMA((NZ,)), DMA((NZ,)), DMA((NZ,)),
        DMA((NZ,)), DMA((NZ,)), DMA((NZ,)), DMA((NZ,)),
        DMA((NY,)), DMA((MATS,)), DMA((NY,)), DMA((MATS,)),
    ]
    vm = pl.BlockSpec(memory_space=pltpu.VMEM)
    hbm = pl.BlockSpec(memory_space=pltpu.HBM)
    return pl.pallas_call(
        functools.partial(kernel, NZ, NY, NX, MATS, LOCAL, D),
        out_shape=(
            jax.ShapeDtypeStruct((MATS, LOCAL, D), f32),
            jax.ShapeDtypeStruct((MATS, LOCAL, D), bf16),
            jax.ShapeDtypeStruct((MATS, LOCAL, D), bf16),
            jax.ShapeDtypeStruct((MATS, LOCAL), f32),
            jax.ShapeDtypeStruct((MATS, LOCAL), f32),
        ),
        in_specs=[hbm] * 7,
        out_specs=(vm,) * 5,
        scratch_shapes=scratch,
        compiler_params=pltpu.CompilerParams(
            collective_id=0, has_side_effects=True, vmem_limit_bytes=60 << 20
        ),
    )


def solution(mesh, NZ=8, NY=8):
    def per_device(grad_parts, vector_grads, momentum, weights, vectors, first_moment, second_moment):
        MATS, LOCAL, WIDTH = momentum.shape[1:]
        call = build(mesh.shape, NZ, NY, MATS, LOCAL, WIDTH)
        outs = call(
            grad_parts[0, 0], vector_grads[0, 0], momentum[0], weights[0],
            vectors[0], first_moment[0], second_moment[0],
        )
        return tuple(o[None] for o in outs)

    rows = P("section", None, ("tensor", "shard"), None)
    cols = P("section", None, ("tensor", "shard"))
    return jax.shard_map(
        per_device,
        mesh=mesh,
        in_specs=(
            P("shard", "section", None, "tensor", None),
            P("shard", "section", None, "tensor"),
            rows, rows, cols, cols, cols,
        ),
        out_specs=(rows, rows, rows, cols, cols),
        check_vma=False,
    )
```

```python
import functools
import math

import jax
import jax.numpy as jnp
from jax import lax
from jax.experimental import pallas as pl
from jax.experimental.pallas import tpu as pltpu
from jax.sharding import PartitionSpec as P


ns_first = 3.4445
ns_second = -4.775
ns_third = 2.0315
mom_beta = 0.95
max_norm = 1024.0
muon_rate = 0.02
muon_decay = 0.1
adam_rate = 0.001
adam_decay = 0.01

MESH = pl.DeviceIdType.MESH
f32 = jnp.float32
bf16 = jnp.bfloat16
LANES = 128


def near_first(n):
    order = []
    for d in range(1, n // 2 + 1):
        order.append(d)
        if n - d != d:
            order.append(n - d)
    return order


def relay_plan(n):
    if n == 8:
        return [(4, 5), (3, 2), (6, 7)], [1]
    if n == 4:
        return [(2, 3)], [1]
    return [], list(range(1, n))


def kernel(
    NZ, NY, NX, MATS, LOCAL, D,
    grad, vec, mom, wts, vecs, fm, sm,
    new_mom, upd_out, new_wts, adam_dir, new_vecs,
    vecv, wtv, vecsv, fmv, smv,
    own_a, ownp, p1a, out_a, ra, acc_a, ownb, p1b, out_b, rb, send_b, r2a, r2b, mrx, mst, gbuf, nms,
    vrz, vry, vsum, stat, srz, srx, sry, stat2, clipb, X, G, X1, gacc, ret,
    s_loc, s_p1a, r_p1a, s_ra, r_ra, s_p1b, r_p1b, s_rb, r_rb, s_2a, r_2a, s_2b, r_2b, s_mm, r_mm,
    s_vz, r_vz, s_vy, r_vy, s_sz, r_sz, s_sx, r_sx, s_sy, r_sy, s_cl, r_cl,
    s_gz, r_gz, s_gl, s_gr, r_gl, r_gr, s_fl, s_fr, r_fl, r_fr,
    s_nm, r_nm, s_rt, r_rt,
):
    ROWS = NZ * NY * LOCAL
    ZR = NY * LOCAL
    HC = D // 2
    shard = lax.axis_index("shard")
    x = lax.axis_index("tensor")
    c = lax.axis_index("section")
    z = lax.div(shard, NY)
    y = lax.rem(shard, NY)
    active = lax.div(y, MATS) == c
    my_m = lax.rem(y, MATS)

    def at_z(d):
        return lax.rem(z + d + NZ, NZ)

    def dev_z(d):
        return (at_z(d) * NY + y, x, c)

    def dev_y(d):
        return (z * NY + lax.rem(y + d + NY, NY), x, c)

    def dev_yabs(yy):
        return (z * NY + yy, x, c)

    def dev_col(yy):
        return (z * NY + yy, x, lax.div(yy, MATS))

    def dev_x(d):
        return (shard, lax.rem(x + d + NX, NX), c)

    partner = (shard, x, 1 - c)
    y_of = [c * MATS + m for m in range(MATS)]

    def rcopy(src, dst, ss, rs, dev):
        return pltpu.make_async_remote_copy(
            src_ref=src, dst_ref=dst, send_sem=ss, recv_sem=rs, device_id=dev, device_id_type=MESH
        )

    zn = near_first(NZ)
    zf = zn[::-1]
    yf = near_first(NY)[::-1]

    sg = 1 - 2 * c
    pairs_z, single_z = relay_plan(NZ)
    pairs_y, single_y = relay_plan(NY)

    def zt(o):
        return lax.rem(z - sg * o + 2 * NZ, NZ)

    def yt(o):
        return lax.rem(y - sg * o + 2 * NY, NY)

    def dev_zabs(zz):
        return (zz * NY + y, x, c)

    def chunk_a(zz):
        return grad.at[:, pl.ds(pl.multiple_of(zz * ZR, ZR), ZR), pl.ds(0, HC)]

    o_of = [lax.rem(sg * (y - y_of[m]) + 2 * NY, NY) for m in range(MATS)]

    loc = [
        pltpu.make_async_copy(chunk_a(z), own_a, s_loc.at[0]),
        pltpu.make_async_copy(grad.at[:, :, pl.ds(HC, HC)], ownb, s_loc.at[1]),
        pltpu.make_async_copy(vec, vecv, s_loc.at[2]),
        pltpu.make_async_copy(wts, wtv, s_loc.at[3]),
        pltpu.make_async_copy(vecs, vecsv, s_loc.at[4]),
        pltpu.make_async_copy(fm, fmv, s_loc.at[5]),
        pltpu.make_async_copy(sm, smv, s_loc.at[6]),
    ]
    for i, (_, g) in enumerate(pairs_z):
        loc.append(pltpu.make_async_copy(chunk_a(zt(g)), ownp.at[i], s_loc.at[8 + i]))
    for cp in loc:
        cp.start()
    loc_mm = pltpu.make_async_copy(mom.at[my_m], mrx.at[y], s_loc.at[7])

    barrier = pltpu.get_barrier_semaphore()

    def greet(dev):
        pl.semaphore_signal(barrier, inc=1, device_id=dev, device_id_type=MESH)

    for d in range(1, NZ):
        greet(dev_z(d))
    for d in range(1, NY):
        greet(dev_y(d))
    for d in range(1, NX):
        greet(dev_x(d))
    greet(partner)
    for j in range(MATS):
        greet((z * NY + (1 - lax.div(y, MATS)) * MATS + j, x, 1 - c))
    pl.semaphore_wait(barrier, NZ - 1 + NY - 1 + NX - 1 + 1 + MATS)

    MH = MATS // 2
    RH = ROWS // 2

    def half_a(h):
        return pl.ds(h * MH, MH)

    def half_b(h):
        return pl.ds(h * RH, RH)

    def chunk_ah(zz, h):
        return grad.at[half_a(h), pl.ds(pl.multiple_of(zz * ZR, ZR), ZR), pl.ds(0, HC)]

    def chunk_bh(m, h):
        return grad.at[m, half_b(h), pl.ds(HC, HC)]

    def first_a(i, h):
        f, g = pairs_z[i]
        return rcopy(
            chunk_ah(zt(f), h), p1a.at[i, half_a(h)], s_p1a.at[i, h], r_p1a.at[i, h], dev_zabs(zt(f - g))
        )

    def second_a(i, h):
        g = pairs_z[i][1]
        return rcopy(
            out_a.at[i, half_a(h)], ra.at[g, half_a(h)], s_ra.at[g, h], r_ra.at[g, h], dev_zabs(zt(g))
        )

    def single_a(o, h):
        return rcopy(
            chunk_ah(zt(o), h), ra.at[o, half_a(h)], s_ra.at[o, h], r_ra.at[o, h], dev_zabs(zt(o))
        )

    def first_b(m, f, g, h):
        return rcopy(
            chunk_bh(m, h), p1b.at[m, half_b(h)], s_p1b.at[m, h], r_p1b.at[m, h], dev_yabs(yt(f - g))
        )

    def single_b(m, o, h):
        return rcopy(chunk_bh(m, h), rb.at[o, half_b(h)], s_rb.at[m, h], r_rb.at[o, h], dev_yabs(y_of[m]))

    def second_b(m, h):
        o = o_of[m]
        return rcopy(
            out_b.at[m, half_b(h)], rb.at[o, half_b(h)], s_rb.at[m, h], r_rb.at[o, h], dev_yabs(y_of[m])
        )

    def is_relay(m):
        hit = o_of[m] == pairs_y[0][1]
        for _, g in pairs_y[1:]:
            hit = jnp.logical_or(hit, o_of[m] == g)
        return hit

    for h in range(2):
        for i in range(len(pairs_z)):
            first_a(i, h).start()
        for m in range(MATS):
            for f, g in pairs_y:
                @pl.when(o_of[m] == f)
                def _():
                    first_b(m, f, g, h).start()
    for h in range(2):
        for o in single_z:
            single_a(o, h).start()
        for m in range(MATS):
            for o in single_y:
                @pl.when(o_of[m] == o)
                def _():
                    single_b(m, o, h).start()
    vz = []
    for d in range(1, NZ):
        cp = rcopy(vec, vrz.at[d - 1], s_vz.at[d - 1], r_vz.at[d - 1], dev_z(d))
        cp.start()
        vz.append(cp)
    for m in range(MATS):
        @pl.when(y != y_of[m])
        def _():
            rcopy(mom.at[m], mrx.at[y], s_mm.at[m], r_mm.at[y], dev_yabs(y_of[m])).start()

    @pl.when(active)
    def _():
        loc_mm.start()

    for cp in loc:
        cp.wait()
    for h in range(2):
        for i in range(len(pairs_z)):
            first_a(i, h).wait_recv()
            part = (i, half_a(h))
            out_a[part] = (ownp[part].astype(f32) + p1a[part].astype(f32)).astype(bf16)
            second_a(i, h).start()
        if pairs_y:
            for m in range(MATS):
                @pl.when(is_relay(m))
                def _():
                    rcopy(
                        chunk_bh(m, h), p1b.at[m, half_b(h)], s_p1b.at[m, h], r_p1b.at[m, h], dev_yabs(y)
                    ).wait_recv()
                    part = (m, half_b(h))
                    out_b[part] = (ownb[part].astype(f32) + p1b[part].astype(f32)).astype(bf16)
                    second_b(m, h).start()

    for cp in vz:
        cp.wait_recv()
    vs = vecv[...].astype(f32)
    for d in range(1, NZ):
        vs = vs + vrz[d - 1].astype(f32)
    vsum[...] = vs
    vy = []
    for d in range(1, NY):
        cp = rcopy(vsum, vry.at[d - 1], s_vy.at[d - 1], r_vy.at[d - 1], dev_y(d))
        cp.start()
        vy.append(cp)

    @pl.when(active)
    def _():
        loc_mm.wait()
        for yy in range(NY):
            @pl.when(y != yy)
            def _():
                rcopy(mom.at[0], mrx.at[yy], s_mm.at[0], r_mm.at[yy], dev_yabs(yy)).wait_recv()
            mst[yy * LOCAL:(yy + 1) * LOCAL, :] = mrx[yy]

    sources = single_y + [g for _, g in pairs_y]

    def send_2b(zz):
        return rcopy(send_b.at[zz], r2b.at[z], s_2b.at[zz], r_2b.at[z], dev_zabs(zz))

    for h in range(2):
        part = half_a(h)
        tot = own_a[part].astype(f32)
        for o in single_z + [g for _, g in pairs_z[::-1]]:
            rcopy(
                chunk_ah(0, h), ra.at[o, part], s_ra.at[o, h], r_ra.at[o, h], dev_zabs(z)
            ).wait_recv()
        for o in single_z + [g for _, g in pairs_z[::-1]]:
            tot = tot + ra[o, part].astype(f32)
        acc_a[part] = tot
        for m in range(h * MH, (h + 1) * MH):
            @pl.when(y != y_of[m])
            def _():
                rcopy(acc_a.at[m], r2a.at[y], s_2a.at[m], r_2a.at[y], dev_yabs(y_of[m])).start()

        @pl.when(active)
        def _():
            for o in sources:
                rcopy(
                    chunk_bh(0, h), rb.at[o, half_b(h)], s_rb.at[0, h], r_rb.at[o, h], dev_yabs(y)
                ).wait_recv()
            for zz in range(h * NZ // 2, (h + 1) * NZ // 2):
                rows = slice(zz * ZR, (zz + 1) * ZR)
                tot = ownb[my_m, rows, :].astype(f32)
                for o in sources:
                    tot = tot + rb[o, rows, :].astype(f32)
                send_b[zz] = tot

                @pl.when(z != zz)
                def _():
                    send_2b(zz).start()

    for cp in vy:
        cp.wait_recv()
    vt = vsum[...]
    for d in range(1, NY):
        vt = vt + vry[d - 1]

    def lane_sum(v):
        total = jnp.sum(v, axis=0, keepdims=True)
        out = total[:, :LANES]
        for k in range(1, v.shape[1] // LANES):
            out = out + total[:, k * LANES:(k + 1) * LANES]
        return out

    def b2(v):
        return jnp.broadcast_to(v, (1, LANES))

    my_row = x * ROWS + z * ZR
    my_off = pl.multiple_of(my_row, ZR)

    def column_sum():
        r2a[y] = acc_a[my_m]
        mm_sum = lane_sum(mst[...] * mst[...])
        for yy in range(NY):
            @pl.when(y != yy)
            def _():
                rcopy(acc_a.at[0], r2a.at[yy], s_2a.at[0], r_2a.at[yy], dev_yabs(yy)).wait_recv()
        tot = r2a[0]
        for yy in range(1, NY):
            tot = tot + r2a[yy]
        gbuf[:, :HC] = tot
        r2b[z] = send_b[z]
        for zz in range(NZ):
            @pl.when(z != zz)
            def _():
                rcopy(send_b.at[0], r2b.at[zz], s_2b.at[0], r_2b.at[zz], dev_zabs(z)).wait_recv()
        tot = r2b[0]
        for zz in range(1, NZ):
            tot = tot + r2b[zz]
        gbuf[:, HC:] = tot

        gv = gbuf[...]
        gg = lane_sum(gv * gv)
        stat[...] = jnp.zeros_like(stat)
        stat[0:1, :] = gg
        stat[1:2, :] = lane_sum(gv * mst[...])
        stat[2:3, :] = mm_sum
        stat[3:4, :] = gg + lane_sum(vt * vt) * (1.0 / (NZ * MATS))
        st = []
        for d in zf:
            cp = rcopy(stat, srz.at[d - 1], s_sz.at[d - 1], r_sz.at[d - 1], dev_z(d))
            cp.start()
            st.append(cp)
        for cp in st:
            cp.wait()
        tot = stat[...]
        for d in range(1, NZ):
            tot = tot + srz[d - 1]
        stat[...] = tot
        st = []
        for d in range(1, NX):
            cp = rcopy(stat, srx.at[d - 1], s_sx.at[d - 1], r_sx.at[d - 1], dev_x(d))
            cp.start()
            st.append(cp)
        for cp in st:
            cp.wait()
        for d in range(1, NX):
            tot = tot + srx[d - 1]
        stat[...] = tot
        for yy in range(NY):
            @pl.when(y != yy)
            def _():
                rcopy(stat, sry.at[y], s_sy.at[yy], r_sy.at[y], dev_col(yy)).start()
        sry[y] = tot
        for yy in range(NY):
            @pl.when(y != yy)
            def _():
                rcopy(stat, sry.at[yy], s_sy.at[yy], r_sy.at[yy], dev_col(yy)).wait()
        grand = sry[0, 3:4, :]
        for yy in range(1, NY):
            grand = grand + sry[yy, 3:4, :]
        grand_total = jnp.sum(grand, axis=1, keepdims=True)
        own = jnp.sum(tot, axis=1, keepdims=True)
        clip = jnp.minimum(1.0, max_norm / (jnp.sqrt(grand_total) + 1e-06))
        stat2[...] = jnp.broadcast_to(clip, stat2.shape)
        rcopy(stat2, clipb, s_cl.at[0], r_cl.at[0], partner).start()
        cc = (1.0 + mom_beta) * clip
        bb = mom_beta * mom_beta
        norm2 = jnp.maximum(cc * cc * own[0:1] + (2.0 * bb) * cc * own[1:2] + (bb * bb) * own[2:3], 0.0)
        inv = 1.0 / (jnp.sqrt(norm2) + 1e-07)
        return clip, inv

    def block(dz, dx):
        row = lax.rem(x + dx + NX, NX) * ROWS + at_z(dz) * ZR
        return X.at[pl.ds(pl.multiple_of(row, ZR), ZR), :]

    def adam(clip):
        vlane = lax.broadcasted_iota(jnp.int32, vt.shape, 1)
        for k in range(LOCAL):
            vg = clip * jnp.sum(jnp.where(vlane == shard * LOCAL + k, vt, 0.0), axis=1, keepdims=True)
            uf = 0.9 * fmv[:, k:k + 1] + 0.1 * vg
            us = 0.999 * smv[:, k:k + 1] + 0.001 * vg * vg
            ad = uf / (jnp.sqrt(us) + 1e-08)
            adam_dir[:, k:k + 1] = ad
            new_vecs[:, k:k + 1] = vecsv[:, k:k + 1] * (1.0 - adam_rate * adam_decay) - adam_rate * ad

    TILE = min(256, D)
    NT = D // TILE
    dn0 = (((0,), (0,)), ((), ()))

    def block_gram(src, xb, first, last):
        rows = pl.ds(pl.multiple_of(xb * ROWS, ROWS), ROWS)

        for j in range(NT):
            n = (j + 1) * TILE
            cols = slice(j * TILE, n)
            pr = lax.dot_general(
                src[rows, :n], src[rows, cols], dn0, preferred_element_type=f32
            ).astype(bf16).astype(f32)
            if first:
                gacc[:n, cols] = pr
            elif last:
                tot = gacc[:n, cols] + pr
                G[:n, cols] = tot.astype(bf16)
                for i in range(j):
                    below = slice(i * TILE, (i + 1) * TILE)
                    G[cols, below] = tot[below, :].T.astype(bf16)
            else:
                gacc[:n, cols] += pr

    def step(rows):
        p1 = jnp.dot(rows, G[...], preferred_element_type=f32).astype(bf16)
        p2 = jnp.dot(p1, G[...], preferred_element_type=f32)
        return ns_first * rows.astype(f32) + ns_second * p1.astype(f32) + ns_third * p2

    @pl.when(active)
    def _():
        clip, inv = column_sum()
        cg = clip * gbuf[...]
        nm = mom_beta * mst[...] + cg
        X[pl.ds(my_off, ZR), :] = ((cg + mom_beta * nm) * inv).astype(bf16)

        mine = block(0, 0)
        order = [0] + zn
        zc = {}
        xc = {}
        fwd = []

        def send_x(k):
            b = block(-k, 0)
            right = rcopy(b, b, s_gr.at[k], r_gr.at[k], dev_x(1))
            left = rcopy(b, b, s_gl.at[k], r_gl.at[k], dev_x(-1))
            right.start()
            left.start()
            xc[k] = (right, left)
            if k in order[-3:]:
                cp = rcopy(b, b, s_fr.at[k], r_fr.at[k], dev_x(2))
                cp.start()
                fwd.append(cp)

        def forward(k):
            xc[k][0].wait_recv()
            if k % 2 == 0 and k not in order[-3:]:
                b = block(-k, -1)
                cp = rcopy(b, b, s_fr.at[k], r_fr.at[k], dev_x(1))
                cp.start()
                fwd.append(cp)
            xc[k][1].wait_recv()
            if k % 2 == 1 and k not in order[-3:]:
                b = block(-k, 1)
                cp = rcopy(b, b, s_fl.at[k], r_fl.at[k], dev_x(-1))
                cp.start()
                fwd.append(cp)

        for d in zf:
            cp = rcopy(mine, mine, s_gz.at[d - 1], r_gz.at[d - 1], dev_z(d))
            cp.start()
            zc[d] = cp
        send_x(0)

        for yy in range(NY):
            nms[yy] = nm[yy * LOCAL:(yy + 1) * LOCAL, :]
        new_mom[my_m] = nms[y]
        for yy in range(NY):
            @pl.when(y != yy)
            def _():
                rcopy(nms.at[yy], new_mom.at[my_m], s_nm.at[yy], r_nm.at[my_m], dev_yabs(yy)).start()
        adam(clip)

        for i, k in enumerate(order):
            if k > 0:
                zc[k].wait_recv()
                send_x(k)
            if i >= 3:
                forward(order[i - 3])
        block_gram(X, x, True, False)
        for k in order[-3:]:
            forward(k)
        block_gram(X, lax.rem(x + NX - 1, NX), False, False)
        block_gram(X, lax.rem(x + 1, NX), False, False)
        for cp in fwd:
            cp.wait()
        block_gram(X, lax.rem(x + 2, NX), False, True)

        @pl.loop(0, NX)
        def _(i):
            rows = pl.ds(pl.multiple_of(i * ROWS, ROWS), ROWS)
            X1[rows, :] = step(X[rows, :]).astype(bf16)

        for b in range(NX):
            block_gram(X1, b, b == 0, b == NX - 1)
        last = step(X1[pl.ds(my_off, ZR), :])
        for yy in range(NY):
            ret[yy] = last[yy * LOCAL:(yy + 1) * LOCAL, :].astype(bf16)
        for yy in range(NY):
            @pl.when(y != yy)
            def _():
                rcopy(ret.at[yy], upd_out.at[my_m], s_rt.at[yy], r_rt.at[my_m], dev_yabs(yy)).start()
        upd_out[my_m] = ret[y]
        for k in order:
            xc[k][0].wait_send()
            xc[k][1].wait_send()
        for d in zf:
            zc[d].wait_send()
        for zz in range(NZ):
            @pl.when(z != zz)
            def _():
                send_2b(zz).wait_send()
        rcopy(stat2, clipb, s_cl.at[0], r_cl.at[0], partner).wait_send()

    @pl.when(jnp.logical_not(active))
    def _():
        rcopy(stat2, clipb, s_cl.at[0], r_cl.at[0], partner).wait_recv()
        adam(clipb[0:1, 0:1])

    for h in range(2):
        for i in range(len(pairs_z)):
            first_a(i, h).wait_send()
            second_a(i, h).wait_send()
        for o in single_z:
            single_a(o, h).wait_send()
        for m in range(MATS):
            for f, g in pairs_y:
                @pl.when(o_of[m] == f)
                def _():
                    first_b(m, f, g, h).wait_send()

                @pl.when(o_of[m] == g)
                def _():
                    second_b(m, h).wait_send()
            for o in single_y:
                @pl.when(o_of[m] == o)
                def _():
                    single_b(m, o, h).wait_send()
    for cp in vz + vy:
        cp.wait_send()
    for m in range(MATS):
        @pl.when(y != y_of[m])
        def _():
            rcopy(mom.at[m], mrx.at[y], s_mm.at[m], r_mm.at[y], dev_yabs(y_of[m])).wait_send()
            rcopy(acc_a.at[m], r2a.at[y], s_2a.at[m], r_2a.at[y], dev_yabs(y_of[m])).wait_send()

    muon_scale = 0.2 * math.sqrt(D)
    for m in range(MATS):
        @pl.when(y != y_of[m])
        def _():
            rcopy(nms.at[0], new_mom.at[m], s_nm.at[0], r_nm.at[m], dev_yabs(y_of[m])).wait_recv()
            rcopy(ret.at[0], upd_out.at[m], s_rt.at[0], r_rt.at[m], dev_yabs(y_of[m])).wait_recv()
        new_wts[m] = (
            wtv[m].astype(f32) * (1.0 - muon_rate * muon_decay)
            - muon_rate * muon_scale * upd_out[m].astype(f32)
        ).astype(bf16)

    @pl.when(active)
    def _():
        for yy in range(NY):
            @pl.when(y != yy)
            def _():
                rcopy(nms.at[yy], new_mom.at[my_m], s_nm.at[yy], r_nm.at[my_m], dev_yabs(yy)).wait_send()
                rcopy(ret.at[yy], upd_out.at[my_m], s_rt.at[yy], r_rt.at[my_m], dev_yabs(yy)).wait_send()


def build(mesh_shape, NZ, NY, MATS, LOCAL, D):
    NX = mesh_shape["tensor"]
    ROWS = NZ * NY * LOCAL
    ZR = NY * LOCAL
    HC = D // 2
    DMA = pltpu.SemaphoreType.DMA
    V = pltpu.VMEM
    scratch = [
        V((MATS, ROWS), bf16),
        V((MATS, LOCAL, D), bf16),
        V((MATS, LOCAL), f32),
        V((MATS, LOCAL), f32),
        V((MATS, LOCAL), f32),
        V((MATS, ZR, HC), bf16),
        V((3, MATS, ZR, HC), bf16),
        V((3, MATS, ZR, HC), bf16),
        V((3, MATS, ZR, HC), bf16),
        V((NZ, MATS, ZR, HC), bf16),
        V((MATS, ZR, HC), f32),
        V((MATS, ROWS, HC), bf16),
        V((MATS, ROWS, HC), bf16),
        V((MATS, ROWS, HC), bf16),
        V((NY, ROWS, HC), bf16),
        V((NZ, ZR, HC), f32),
        V((NY, ZR, HC), f32),
        V((NZ, ZR, HC), f32),
        V((NY, LOCAL, D), f32),
        V((ZR, D), f32),
        V((ZR, D), f32),
        V((NY, LOCAL, D), f32),
        V((NZ - 1, MATS, ROWS), bf16),
        V((NY - 1, MATS, ROWS), f32),
        V((MATS, ROWS), f32),
        V((8, LANES), f32),
        V((NZ - 1, 8, LANES), f32),
        V((NX - 1, 8, LANES), f32),
        V((NY, 8, LANES), f32),
        V((8, LANES), f32),
        V((8, LANES), f32),
        V((NX * ROWS, D), bf16),
        V((D, D), bf16),
        V((NX * ROWS, D), bf16),
        V((D, D), f32),
        V((NY, LOCAL, D), bf16),
        DMA((11,)),
        DMA((3, 2)), DMA((3, 2)), DMA((NZ, 2)), DMA((NZ, 2)),
        DMA((MATS, 2)), DMA((MATS, 2)), DMA((MATS, 2)), DMA((NY, 2)),
        DMA((MATS,)), DMA((NY,)), DMA((NZ,)), DMA((NZ,)), DMA((MATS,)), DMA((NY,)),
        DMA((NZ - 1,)), DMA((NZ - 1,)), DMA((NY - 1,)), DMA((NY - 1,)),
        DMA((NZ - 1,)), DMA((NZ - 1,)), DMA((NX - 1,)), DMA((NX - 1,)), DMA((NY,)), DMA((NY,)),
        DMA((1,)), DMA((1,)),
        DMA((NZ - 1,)), DMA((NZ - 1,)),
        DMA((NZ,)), DMA((NZ,)), DMA((NZ,)), DMA((NZ,)),
        DMA((NZ,)), DMA((NZ,)), DMA((NZ,)), DMA((NZ,)),
        DMA((NY,)), DMA((MATS,)), DMA((NY,)), DMA((MATS,)),
    ]
    vm = pl.BlockSpec(memory_space=pltpu.VMEM)
    hbm = pl.BlockSpec(memory_space=pltpu.HBM)
    return pl.pallas_call(
        functools.partial(kernel, NZ, NY, NX, MATS, LOCAL, D),
        out_shape=(
            jax.ShapeDtypeStruct((MATS, LOCAL, D), f32),
            jax.ShapeDtypeStruct((MATS, LOCAL, D), bf16),
            jax.ShapeDtypeStruct((MATS, LOCAL, D), bf16),
            jax.ShapeDtypeStruct((MATS, LOCAL), f32),
            jax.ShapeDtypeStruct((MATS, LOCAL), f32),
        ),
        in_specs=[hbm] * 7,
        out_specs=(vm,) * 5,
        scratch_shapes=scratch,
        compiler_params=pltpu.CompilerParams(
            collective_id=0, has_side_effects=True, vmem_limit_bytes=60 << 20
        ),
    )


def solution(mesh, NZ=8, NY=8):
    def per_device(grad_parts, vector_grads, momentum, weights, vectors, first_moment, second_moment):
        MATS, LOCAL, WIDTH = momentum.shape[1:]
        call = build(mesh.shape, NZ, NY, MATS, LOCAL, WIDTH)
        outs = call(
            grad_parts[0, 0], vector_grads[0, 0], momentum[0], weights[0],
            vectors[0], first_moment[0], second_moment[0],
        )
        return tuple(o[None] for o in outs)

    rows = P("section", None, ("tensor", "shard"), None)
    cols = P("section", None, ("tensor", "shard"))
    return jax.shard_map(
        per_device,
        mesh=mesh,
        in_specs=(
            P("shard", "section", None, "tensor", None),
            P("shard", "section", None, "tensor"),
            rows, rows, cols, cols, cols,
        ),
        out_specs=(rows, rows, rows, cols, cols),
        check_vma=False,
    )
```

```python
import functools
import math

import jax
import jax.numpy as jnp
from jax import lax
from jax.experimental import pallas as pl
from jax.experimental.pallas import tpu as pltpu
from jax.sharding import PartitionSpec as P


ns_first = 3.4445
ns_second = -4.775
ns_third = 2.0315
mom_beta = 0.95
max_norm = 1024.0
muon_rate = 0.02
muon_decay = 0.1
adam_rate = 0.001
adam_decay = 0.01

MESH = pl.DeviceIdType.MESH
f32 = jnp.float32
bf16 = jnp.bfloat16
LANES = 128


def near_first(n):
    order = []
    for d in range(1, n // 2 + 1):
        order.append(d)
        if n - d != d:
            order.append(n - d)
    return order


def relay_plan(n):
    if n == 8:
        return [(4, 5), (3, 2), (6, 7)], [1]
    if n == 4:
        return [(2, 3)], [1]
    return [], list(range(1, n))


def kernel(
    NZ, NY, NX, MATS, LOCAL, D,
    grad, vec, mom, wts, vecs, fm, sm,
    new_mom, upd_out, new_wts, adam_dir, new_vecs,
    vecv, wtv, vecsv, fmv, smv,
    own_a, ownp, p1a, out_a, ra, acc_a, ownb, p1b, out_b, rb, send_b, r2a, r2b, mrx, mst, gbuf, nms,
    vrz, vry, vsum, stat, srz, srx, sry, stat2, clipb, X, G, X1, gacc, ret,
    s_loc, s_p1a, r_p1a, s_ra, r_ra, s_p1b, r_p1b, s_rb, r_rb, s_2a, r_2a, s_2b, r_2b, s_mm, r_mm,
    s_vz, r_vz, s_vy, r_vy, s_sz, r_sz, s_sx, r_sx, s_sy, r_sy, s_cl, r_cl,
    s_gz, r_gz, s_gl, s_gr, r_gl, r_gr, s_fl, s_fr, r_fl, r_fr,
    s_nm, r_nm, s_rt, r_rt,
):
    ROWS = NZ * NY * LOCAL
    ZR = NY * LOCAL
    HC = D // 2
    shard = lax.axis_index("shard")
    x = lax.axis_index("tensor")
    c = lax.axis_index("section")
    z = lax.div(shard, NY)
    y = lax.rem(shard, NY)
    active = lax.div(y, MATS) == c
    my_m = lax.rem(y, MATS)

    def at_z(d):
        return lax.rem(z + d + NZ, NZ)

    def dev_z(d):
        return (at_z(d) * NY + y, x, c)

    def dev_y(d):
        return (z * NY + lax.rem(y + d + NY, NY), x, c)

    def dev_yabs(yy):
        return (z * NY + yy, x, c)

    def dev_col(yy):
        return (z * NY + yy, x, lax.div(yy, MATS))

    def dev_x(d):
        return (shard, lax.rem(x + d + NX, NX), c)

    partner = (shard, x, 1 - c)
    y_of = [c * MATS + m for m in range(MATS)]

    def rcopy(src, dst, ss, rs, dev):
        return pltpu.make_async_remote_copy(
            src_ref=src, dst_ref=dst, send_sem=ss, recv_sem=rs, device_id=dev, device_id_type=MESH
        )

    zn = near_first(NZ)
    zf = zn[::-1]
    yf = near_first(NY)[::-1]

    sg = 1 - 2 * c
    pairs_z, single_z = relay_plan(NZ)
    pairs_y, single_y = relay_plan(NY)

    def zt(o):
        return lax.rem(z - sg * o + 2 * NZ, NZ)

    def yt(o):
        return lax.rem(y - sg * o + 2 * NY, NY)

    def dev_zabs(zz):
        return (zz * NY + y, x, c)

    def chunk_a(zz):
        return grad.at[:, pl.ds(pl.multiple_of(zz * ZR, ZR), ZR), pl.ds(0, HC)]

    o_of = [lax.rem(sg * (y - y_of[m]) + 2 * NY, NY) for m in range(MATS)]

    loc = [
        pltpu.make_async_copy(chunk_a(z), own_a, s_loc.at[0]),
        pltpu.make_async_copy(grad.at[:, :, pl.ds(HC, HC)], ownb, s_loc.at[1]),
        pltpu.make_async_copy(vec, vecv, s_loc.at[2]),
        pltpu.make_async_copy(wts, wtv, s_loc.at[3]),
        pltpu.make_async_copy(vecs, vecsv, s_loc.at[4]),
        pltpu.make_async_copy(fm, fmv, s_loc.at[5]),
        pltpu.make_async_copy(sm, smv, s_loc.at[6]),
    ]
    for i, (_, g) in enumerate(pairs_z):
        loc.append(pltpu.make_async_copy(chunk_a(zt(g)), ownp.at[i], s_loc.at[8 + i]))
    for cp in loc:
        cp.start()
    loc_mm = pltpu.make_async_copy(mom.at[my_m], mrx.at[y], s_loc.at[7])

    barrier = pltpu.get_barrier_semaphore()

    def greet(dev):
        pl.semaphore_signal(barrier, inc=1, device_id=dev, device_id_type=MESH)

    for d in range(1, NZ):
        greet(dev_z(d))
    for d in range(1, NY):
        greet(dev_y(d))
    for d in range(1, NX):
        greet(dev_x(d))
    greet(partner)
    for j in range(MATS):
        greet((z * NY + (1 - lax.div(y, MATS)) * MATS + j, x, 1 - c))
    pl.semaphore_wait(barrier, NZ - 1 + NY - 1 + NX - 1 + 1 + MATS)

    MH = MATS // 4
    RH = ROWS // 4

    def half_a(h):
        return pl.ds(h * MH, MH)

    def half_b(h):
        return pl.ds(h * RH, RH)

    def chunk_ah(zz, h):
        return grad.at[half_a(h), pl.ds(pl.multiple_of(zz * ZR, ZR), ZR), pl.ds(0, HC)]

    def chunk_bh(m, h):
        return grad.at[m, half_b(h), pl.ds(HC, HC)]

    def first_a(i, h):
        f, g = pairs_z[i]
        return rcopy(
            chunk_ah(zt(f), h), p1a.at[i, half_a(h)], s_p1a.at[i, h], r_p1a.at[i, h], dev_zabs(zt(f - g))
        )

    def second_a(i, h):
        g = pairs_z[i][1]
        return rcopy(
            out_a.at[i, half_a(h)], ra.at[g, half_a(h)], s_ra.at[g, h], r_ra.at[g, h], dev_zabs(zt(g))
        )

    def single_a(o, h):
        return rcopy(
            chunk_ah(zt(o), h), ra.at[o, half_a(h)], s_ra.at[o, h], r_ra.at[o, h], dev_zabs(zt(o))
        )

    def first_b(m, f, g, h):
        return rcopy(
            chunk_bh(m, h), p1b.at[m, half_b(h)], s_p1b.at[m, h], r_p1b.at[m, h], dev_yabs(yt(f - g))
        )

    def single_b(m, o, h):
        return rcopy(chunk_bh(m, h), rb.at[o, half_b(h)], s_rb.at[m, h], r_rb.at[o, h], dev_yabs(y_of[m]))

    def second_b(m, h):
        o = o_of[m]
        return rcopy(
            out_b.at[m, half_b(h)], rb.at[o, half_b(h)], s_rb.at[m, h], r_rb.at[o, h], dev_yabs(y_of[m])
        )

    def is_relay(m):
        hit = o_of[m] == pairs_y[0][1]
        for _, g in pairs_y[1:]:
            hit = jnp.logical_or(hit, o_of[m] == g)
        return hit

    for h in range(4):
        for o in single_z:
            single_a(o, h).start()
        for m in range(MATS):
            for o in single_y:
                @pl.when(o_of[m] == o)
                def _():
                    single_b(m, o, h).start()
    for h in range(4):
        for i in range(len(pairs_z)):
            first_a(i, h).start()
        for m in range(MATS):
            for f, g in pairs_y:
                @pl.when(o_of[m] == f)
                def _():
                    first_b(m, f, g, h).start()
    vz = []
    for d in range(1, NZ):
        cp = rcopy(vec, vrz.at[d - 1], s_vz.at[d - 1], r_vz.at[d - 1], dev_z(d))
        cp.start()
        vz.append(cp)
    for m in range(MATS):
        @pl.when(y != y_of[m])
        def _():
            rcopy(mom.at[m], mrx.at[y], s_mm.at[m], r_mm.at[y], dev_yabs(y_of[m])).start()

    @pl.when(active)
    def _():
        loc_mm.start()

    for cp in loc:
        cp.wait()
    for h in range(4):
        for i in range(len(pairs_z)):
            first_a(i, h).wait_recv()
            part = (i, half_a(h))
            out_a[part] = (ownp[part].astype(f32) + p1a[part].astype(f32)).astype(bf16)
            second_a(i, h).start()
        if pairs_y:
            for m in range(MATS):
                @pl.when(is_relay(m))
                def _():
                    rcopy(
                        chunk_bh(m, h), p1b.at[m, half_b(h)], s_p1b.at[m, h], r_p1b.at[m, h], dev_yabs(y)
                    ).wait_recv()
                    part = (m, half_b(h))
                    out_b[part] = (ownb[part].astype(f32) + p1b[part].astype(f32)).astype(bf16)
                    second_b(m, h).start()

    for cp in vz:
        cp.wait_recv()
    vs = vecv[...].astype(f32)
    for d in range(1, NZ):
        vs = vs + vrz[d - 1].astype(f32)
    vsum[...] = vs
    vy = []
    for d in range(1, NY):
        cp = rcopy(vsum, vry.at[d - 1], s_vy.at[d - 1], r_vy.at[d - 1], dev_y(d))
        cp.start()
        vy.append(cp)

    @pl.when(active)
    def _():
        loc_mm.wait()
        for yy in range(NY):
            @pl.when(y != yy)
            def _():
                rcopy(mom.at[0], mrx.at[yy], s_mm.at[0], r_mm.at[yy], dev_yabs(yy)).wait_recv()
            mst[yy * LOCAL:(yy + 1) * LOCAL, :] = mrx[yy]

    sources = single_y + [g for _, g in pairs_y]

    def send_2b(zz):
        return rcopy(send_b.at[zz], r2b.at[z], s_2b.at[zz], r_2b.at[z], dev_zabs(zz))

    for h in range(4):
        part = half_a(h)
        tot = own_a[part].astype(f32)
        for o in single_z + [g for _, g in pairs_z[::-1]]:
            rcopy(
                chunk_ah(0, h), ra.at[o, part], s_ra.at[o, h], r_ra.at[o, h], dev_zabs(z)
            ).wait_recv()
        for o in single_z + [g for _, g in pairs_z[::-1]]:
            tot = tot + ra[o, part].astype(f32)
        acc_a[part] = tot
        for m in range(h * MH, (h + 1) * MH):
            @pl.when(y != y_of[m])
            def _():
                rcopy(acc_a.at[m], r2a.at[y], s_2a.at[m], r_2a.at[y], dev_yabs(y_of[m])).start()

        @pl.when(active)
        def _():
            for o in sources:
                rcopy(
                    chunk_bh(0, h), rb.at[o, half_b(h)], s_rb.at[0, h], r_rb.at[o, h], dev_yabs(y)
                ).wait_recv()
            for zz in range(h * NZ // 4, (h + 1) * NZ // 4):
                rows = slice(zz * ZR, (zz + 1) * ZR)
                tot = ownb[my_m, rows, :].astype(f32)
                for o in sources:
                    tot = tot + rb[o, rows, :].astype(f32)
                send_b[zz] = tot

                @pl.when(z != zz)
                def _():
                    send_2b(zz).start()

    for cp in vy:
        cp.wait_recv()
    vt = vsum[...]
    for d in range(1, NY):
        vt = vt + vry[d - 1]

    def lane_sum(v):
        total = jnp.sum(v, axis=0, keepdims=True)
        out = total[:, :LANES]
        for k in range(1, v.shape[1] // LANES):
            out = out + total[:, k * LANES:(k + 1) * LANES]
        return out

    def b2(v):
        return jnp.broadcast_to(v, (1, LANES))

    my_row = x * ROWS + z * ZR
    my_off = pl.multiple_of(my_row, ZR)

    def column_sum():
        r2a[y] = acc_a[my_m]
        mm_sum = lane_sum(mst[...] * mst[...])
        for yy in range(NY):
            @pl.when(y != yy)
            def _():
                rcopy(acc_a.at[0], r2a.at[yy], s_2a.at[0], r_2a.at[yy], dev_yabs(yy)).wait_recv()
        tot = r2a[0]
        for yy in range(1, NY):
            tot = tot + r2a[yy]
        gbuf[:, :HC] = tot
        r2b[z] = send_b[z]
        for zz in range(NZ):
            @pl.when(z != zz)
            def _():
                rcopy(send_b.at[0], r2b.at[zz], s_2b.at[0], r_2b.at[zz], dev_zabs(z)).wait_recv()
        tot = r2b[0]
        for zz in range(1, NZ):
            tot = tot + r2b[zz]
        gbuf[:, HC:] = tot

        gv = gbuf[...]
        gg = lane_sum(gv * gv)
        stat[...] = jnp.zeros_like(stat)
        stat[0:1, :] = gg
        stat[1:2, :] = lane_sum(gv * mst[...])
        stat[2:3, :] = mm_sum
        stat[3:4, :] = gg + lane_sum(vt * vt) * (1.0 / (NZ * MATS))
        st = []
        for d in zf:
            cp = rcopy(stat, srz.at[d - 1], s_sz.at[d - 1], r_sz.at[d - 1], dev_z(d))
            cp.start()
            st.append(cp)
        for cp in st:
            cp.wait()
        tot = stat[...]
        for d in range(1, NZ):
            tot = tot + srz[d - 1]
        stat[...] = tot
        st = []
        for d in range(1, NX):
            cp = rcopy(stat, srx.at[d - 1], s_sx.at[d - 1], r_sx.at[d - 1], dev_x(d))
            cp.start()
            st.append(cp)
        for cp in st:
            cp.wait()
        for d in range(1, NX):
            tot = tot + srx[d - 1]
        stat[...] = tot
        for yy in range(NY):
            @pl.when(y != yy)
            def _():
                rcopy(stat, sry.at[y], s_sy.at[yy], r_sy.at[y], dev_col(yy)).start()
        sry[y] = tot
        for yy in range(NY):
            @pl.when(y != yy)
            def _():
                rcopy(stat, sry.at[yy], s_sy.at[yy], r_sy.at[yy], dev_col(yy)).wait()
        grand = sry[0, 3:4, :]
        for yy in range(1, NY):
            grand = grand + sry[yy, 3:4, :]
        grand_total = jnp.sum(grand, axis=1, keepdims=True)
        own = jnp.sum(tot, axis=1, keepdims=True)
        clip = jnp.minimum(1.0, max_norm / (jnp.sqrt(grand_total) + 1e-06))
        stat2[...] = jnp.broadcast_to(clip, stat2.shape)
        rcopy(stat2, clipb, s_cl.at[0], r_cl.at[0], partner).start()
        cc = (1.0 + mom_beta) * clip
        bb = mom_beta * mom_beta
        norm2 = jnp.maximum(cc * cc * own[0:1] + (2.0 * bb) * cc * own[1:2] + (bb * bb) * own[2:3], 0.0)
        inv = 1.0 / (jnp.sqrt(norm2) + 1e-07)
        return clip, inv

    def block(dz, dx):
        row = lax.rem(x + dx + NX, NX) * ROWS + at_z(dz) * ZR
        return X.at[pl.ds(pl.multiple_of(row, ZR), ZR), :]

    def adam(clip):
        vlane = lax.broadcasted_iota(jnp.int32, vt.shape, 1)
        for k in range(LOCAL):
            vg = clip * jnp.sum(jnp.where(vlane == shard * LOCAL + k, vt, 0.0), axis=1, keepdims=True)
            uf = 0.9 * fmv[:, k:k + 1] + 0.1 * vg
            us = 0.999 * smv[:, k:k + 1] + 0.001 * vg * vg
            ad = uf / (jnp.sqrt(us) + 1e-08)
            adam_dir[:, k:k + 1] = ad
            new_vecs[:, k:k + 1] = vecsv[:, k:k + 1] * (1.0 - adam_rate * adam_decay) - adam_rate * ad

    TILE = min(256, D)
    NT = D // TILE
    dn0 = (((0,), (0,)), ((), ()))

    def block_gram(src, xb, first, last):
        rows = pl.ds(pl.multiple_of(xb * ROWS, ROWS), ROWS)

        for j in range(NT):
            n = (j + 1) * TILE
            cols = slice(j * TILE, n)
            pr = lax.dot_general(
                src[rows, :n], src[rows, cols], dn0, preferred_element_type=f32
            ).astype(bf16).astype(f32)
            if first:
                gacc[:n, cols] = pr
            elif last:
                tot = gacc[:n, cols] + pr
                G[:n, cols] = tot.astype(bf16)
                for i in range(j):
                    below = slice(i * TILE, (i + 1) * TILE)
                    G[cols, below] = tot[below, :].T.astype(bf16)
            else:
                gacc[:n, cols] += pr

    def step(rows):
        p1 = jnp.dot(rows, G[...], preferred_element_type=f32).astype(bf16)
        p2 = jnp.dot(p1, G[...], preferred_element_type=f32)
        return ns_first * rows.astype(f32) + ns_second * p1.astype(f32) + ns_third * p2

    @pl.when(active)
    def _():
        clip, inv = column_sum()
        cg = clip * gbuf[...]
        nm = mom_beta * mst[...] + cg
        X[pl.ds(my_off, ZR), :] = ((cg + mom_beta * nm) * inv).astype(bf16)

        mine = block(0, 0)
        order = [0] + zn
        zc = {}
        xc = {}
        fwd = []

        def send_x(k):
            b = block(-k, 0)
            right = rcopy(b, b, s_gr.at[k], r_gr.at[k], dev_x(1))
            left = rcopy(b, b, s_gl.at[k], r_gl.at[k], dev_x(-1))
            right.start()
            left.start()
            xc[k] = (right, left)
            if k in order[-3:]:
                cp = rcopy(b, b, s_fr.at[k], r_fr.at[k], dev_x(2))
                cp.start()
                fwd.append(cp)

        def forward(k):
            xc[k][0].wait_recv()
            if k % 2 == 0 and k not in order[-3:]:
                b = block(-k, -1)
                cp = rcopy(b, b, s_fr.at[k], r_fr.at[k], dev_x(1))
                cp.start()
                fwd.append(cp)
            xc[k][1].wait_recv()
            if k % 2 == 1 and k not in order[-3:]:
                b = block(-k, 1)
                cp = rcopy(b, b, s_fl.at[k], r_fl.at[k], dev_x(-1))
                cp.start()
                fwd.append(cp)

        for d in zn:
            cp = rcopy(mine, mine, s_gz.at[d - 1], r_gz.at[d - 1], dev_z(d))
            cp.start()
            zc[d] = cp
        send_x(0)

        for yy in range(NY):
            nms[yy] = nm[yy * LOCAL:(yy + 1) * LOCAL, :]
        new_mom[my_m] = nms[y]
        for yy in range(NY):
            @pl.when(y != yy)
            def _():
                rcopy(nms.at[yy], new_mom.at[my_m], s_nm.at[yy], r_nm.at[my_m], dev_yabs(yy)).start()
        adam(clip)

        for i, k in enumerate(order):
            if k > 0:
                zc[k].wait_recv()
                send_x(k)
            if i >= 3:
                forward(order[i - 3])
        block_gram(X, x, True, False)
        for k in order[-3:]:
            forward(k)
        block_gram(X, lax.rem(x + NX - 1, NX), False, False)
        block_gram(X, lax.rem(x + 1, NX), False, False)
        for cp in fwd:
            cp.wait()
        block_gram(X, lax.rem(x + 2, NX), False, True)

        @pl.loop(0, NX)
        def _(i):
            rows = pl.ds(pl.multiple_of(i * ROWS, ROWS), ROWS)
            X1[rows, :] = step(X[rows, :]).astype(bf16)

        for b in range(NX):
            block_gram(X1, b, b == 0, b == NX - 1)
        last = step(X1[pl.ds(my_off, ZR), :])
        for yy in range(NY):
            ret[yy] = last[yy * LOCAL:(yy + 1) * LOCAL, :].astype(bf16)
        for yy in range(NY):
            @pl.when(y != yy)
            def _():
                rcopy(ret.at[yy], upd_out.at[my_m], s_rt.at[yy], r_rt.at[my_m], dev_yabs(yy)).start()
        upd_out[my_m] = ret[y]
        for k in order:
            xc[k][0].wait_send()
            xc[k][1].wait_send()
        for d in zf:
            zc[d].wait_send()
        for zz in range(NZ):
            @pl.when(z != zz)
            def _():
                send_2b(zz).wait_send()
        rcopy(stat2, clipb, s_cl.at[0], r_cl.at[0], partner).wait_send()

    @pl.when(jnp.logical_not(active))
    def _():
        rcopy(stat2, clipb, s_cl.at[0], r_cl.at[0], partner).wait_recv()
        adam(clipb[0:1, 0:1])

    for h in range(4):
        for i in range(len(pairs_z)):
            first_a(i, h).wait_send()
            second_a(i, h).wait_send()
        for o in single_z:
            single_a(o, h).wait_send()
        for m in range(MATS):
            for f, g in pairs_y:
                @pl.when(o_of[m] == f)
                def _():
                    first_b(m, f, g, h).wait_send()

                @pl.when(o_of[m] == g)
                def _():
                    second_b(m, h).wait_send()
            for o in single_y:
                @pl.when(o_of[m] == o)
                def _():
                    single_b(m, o, h).wait_send()
    for cp in vz + vy:
        cp.wait_send()
    for m in range(MATS):
        @pl.when(y != y_of[m])
        def _():
            rcopy(mom.at[m], mrx.at[y], s_mm.at[m], r_mm.at[y], dev_yabs(y_of[m])).wait_send()
            rcopy(acc_a.at[m], r2a.at[y], s_2a.at[m], r_2a.at[y], dev_yabs(y_of[m])).wait_send()

    muon_scale = 0.2 * math.sqrt(D)
    for m in range(MATS):
        @pl.when(y != y_of[m])
        def _():
            rcopy(nms.at[0], new_mom.at[m], s_nm.at[0], r_nm.at[m], dev_yabs(y_of[m])).wait_recv()
            rcopy(ret.at[0], upd_out.at[m], s_rt.at[0], r_rt.at[m], dev_yabs(y_of[m])).wait_recv()
        new_wts[m] = (
            wtv[m].astype(f32) * (1.0 - muon_rate * muon_decay)
            - muon_rate * muon_scale * upd_out[m].astype(f32)
        ).astype(bf16)

    @pl.when(active)
    def _():
        for yy in range(NY):
            @pl.when(y != yy)
            def _():
                rcopy(nms.at[yy], new_mom.at[my_m], s_nm.at[yy], r_nm.at[my_m], dev_yabs(yy)).wait_send()
                rcopy(ret.at[yy], upd_out.at[my_m], s_rt.at[yy], r_rt.at[my_m], dev_yabs(yy)).wait_send()


def place(nm, up, wt, ad, nv, nm_o, up_o, wt_o, ad_o, nv_o, sems):
    copies = [
        pltpu.make_async_copy(src, dst, sems.at[i])
        for i, (src, dst) in enumerate([(nm, nm_o), (up, up_o), (wt, wt_o), (ad, ad_o), (nv, nv_o)])
    ]
    for cp in copies:
        cp.start()
    for cp in copies:
        cp.wait()


def hand_out(*arrays):
    hbm = pl.BlockSpec(memory_space=pltpu.HBM)
    return pl.pallas_call(
        place,
        out_shape=tuple(jax.ShapeDtypeStruct(a.shape, a.dtype) for a in arrays),
        in_specs=[hbm] * len(arrays),
        out_specs=(hbm,) * len(arrays),
        scratch_shapes=[pltpu.SemaphoreType.DMA((len(arrays),))],
    )(*arrays)


def build(mesh_shape, NZ, NY, MATS, LOCAL, D):
    NX = mesh_shape["tensor"]
    ROWS = NZ * NY * LOCAL
    ZR = NY * LOCAL
    HC = D // 2
    DMA = pltpu.SemaphoreType.DMA
    V = pltpu.VMEM
    scratch = [
        V((MATS, ROWS), bf16),
        V((MATS, LOCAL, D), bf16),
        V((MATS, LOCAL), f32),
        V((MATS, LOCAL), f32),
        V((MATS, LOCAL), f32),
        V((MATS, ZR, HC), bf16),
        V((3, MATS, ZR, HC), bf16),
        V((3, MATS, ZR, HC), bf16),
        V((3, MATS, ZR, HC), bf16),
        V((NZ, MATS, ZR, HC), bf16),
        V((MATS, ZR, HC), f32),
        V((MATS, ROWS, HC), bf16),
        V((MATS, ROWS, HC), bf16),
        V((MATS, ROWS, HC), bf16),
        V((NY, ROWS, HC), bf16),
        V((NZ, ZR, HC), f32),
        V((NY, ZR, HC), f32),
        V((NZ, ZR, HC), f32),
        V((NY, LOCAL, D), f32),
        V((ZR, D), f32),
        V((ZR, D), f32),
        V((NY, LOCAL, D), f32),
        V((NZ - 1, MATS, ROWS), bf16),
        V((NY - 1, MATS, ROWS), f32),
        V((MATS, ROWS), f32),
        V((8, LANES), f32),
        V((NZ - 1, 8, LANES), f32),
        V((NX - 1, 8, LANES), f32),
        V((NY, 8, LANES), f32),
        V((8, LANES), f32),
        V((8, LANES), f32),
        V((NX * ROWS, D), bf16),
        V((D, D), bf16),
        V((NX * ROWS, D), bf16),
        V((D, D), f32),
        V((NY, LOCAL, D), bf16),
        DMA((11,)),
        DMA((3, 4)), DMA((3, 4)), DMA((NZ, 4)), DMA((NZ, 4)),
        DMA((MATS, 4)), DMA((MATS, 4)), DMA((MATS, 4)), DMA((NY, 4)),
        DMA((MATS,)), DMA((NY,)), DMA((NZ,)), DMA((NZ,)), DMA((MATS,)), DMA((NY,)),
        DMA((NZ - 1,)), DMA((NZ - 1,)), DMA((NY - 1,)), DMA((NY - 1,)),
        DMA((NZ - 1,)), DMA((NZ - 1,)), DMA((NX - 1,)), DMA((NX - 1,)), DMA((NY,)), DMA((NY,)),
        DMA((1,)), DMA((1,)),
        DMA((NZ - 1,)), DMA((NZ - 1,)),
        DMA((NZ,)), DMA((NZ,)), DMA((NZ,)), DMA((NZ,)),
        DMA((NZ,)), DMA((NZ,)), DMA((NZ,)), DMA((NZ,)),
        DMA((NY,)), DMA((MATS,)), DMA((NY,)), DMA((MATS,)),
    ]
    vm = pl.BlockSpec(memory_space=pltpu.VMEM)
    hbm = pl.BlockSpec(memory_space=pltpu.HBM)
    return pl.pallas_call(
        functools.partial(kernel, NZ, NY, NX, MATS, LOCAL, D),
        out_shape=(
            jax.ShapeDtypeStruct((MATS, LOCAL, D), f32),
            jax.ShapeDtypeStruct((MATS, LOCAL, D), bf16),
            jax.ShapeDtypeStruct((MATS, LOCAL, D), bf16),
            jax.ShapeDtypeStruct((MATS, LOCAL), f32),
            jax.ShapeDtypeStruct((MATS, LOCAL), f32),
        ),
        in_specs=[hbm] * 7,
        out_specs=(vm,) * 5,
        scratch_shapes=scratch,
        compiler_params=pltpu.CompilerParams(
            collective_id=0, has_side_effects=True, vmem_limit_bytes=60 << 20
        ),
    )


def solution(mesh, NZ=8, NY=8):
    def per_device(grad_parts, vector_grads, momentum, weights, vectors, first_moment, second_moment):
        MATS, LOCAL, WIDTH = momentum.shape[1:]
        call = build(mesh.shape, NZ, NY, MATS, LOCAL, WIDTH)
        outs = call(
            grad_parts[0, 0], vector_grads[0, 0], momentum[0], weights[0],
            vectors[0], first_moment[0], second_moment[0],
        )
        return tuple(o[None] for o in hand_out(*outs))

    rows = P("section", None, ("tensor", "shard"), None)
    cols = P("section", None, ("tensor", "shard"))
    return jax.shard_map(
        per_device,
        mesh=mesh,
        in_specs=(
            P("shard", "section", None, "tensor", None),
            P("shard", "section", None, "tensor"),
            rows, rows, cols, cols, cols,
        ),
        out_specs=(rows, rows, rows, cols, cols),
        check_vma=False,
    )
```

```python
import functools
import math

import jax
import jax.numpy as jnp
from jax import lax
from jax.experimental import pallas as pl
from jax.experimental.pallas import tpu as pltpu
from jax.sharding import PartitionSpec as P


ns_first = 3.4445
ns_second = -4.775
ns_third = 2.0315
mom_beta = 0.95
max_norm = 1024.0
muon_rate = 0.02
muon_decay = 0.1
adam_rate = 0.001
adam_decay = 0.01

MESH = pl.DeviceIdType.MESH
f32 = jnp.float32
bf16 = jnp.bfloat16
LANES = 128


def near_first(n):
    order = []
    for d in range(1, n // 2 + 1):
        order.append(d)
        if n - d != d:
            order.append(n - d)
    return order


def relay_plan(n):
    if n == 8:
        return [(4, 5), (3, 2), (6, 7)], [1]
    if n == 4:
        return [(2, 3)], [1]
    return [], list(range(1, n))


def kernel(
    NZ, NY, NX, MATS, LOCAL, D,
    grad, vec, mom, wts, vecs, fm, sm,
    new_mom, upd_out, new_wts, adam_dir, new_vecs,
    vecv, wtv, vecsv, fmv, smv,
    own_a, ownp, p1a, out_a, ra, acc_a, sent_a, own_b, ownb, p1b, out_b, rb, send_b, r2a, r2b, mrx, mst, gbuf, nms,
    vrz, vry, vsum, stat, srz, srx, sry, stat2, clipb, X, G, X1, gacc, ret,
    s_loc, s_p1a, r_p1a, s_ra, r_ra, s_p1b, r_p1b, s_rb, r_rb, s_2a, r_2a, s_2b, r_2b, s_mm, r_mm,
    s_vz, r_vz, s_vy, r_vy, s_sz, r_sz, s_sx, r_sx, s_sy, r_sy, s_cl, r_cl,
    s_gz, r_gz, s_gl, s_gr, r_gl, r_gr, s_fl, s_fr, r_fl, r_fr,
    s_nm, r_nm, s_rt, r_rt,
):
    ROWS = NZ * NY * LOCAL
    ZR = NY * LOCAL
    HC = D // 2
    shard = lax.axis_index("shard")
    x = lax.axis_index("tensor")
    c = lax.axis_index("section")
    z = lax.div(shard, NY)
    y = lax.rem(shard, NY)
    active = lax.div(y, MATS) == c
    my_m = lax.rem(y, MATS)

    def at_z(d):
        return lax.rem(z + d + NZ, NZ)

    def dev_z(d):
        return (at_z(d) * NY + y, x, c)

    def dev_y(d):
        return (z * NY + lax.rem(y + d + NY, NY), x, c)

    def dev_yabs(yy):
        return (z * NY + yy, x, c)

    def dev_col(yy):
        return (z * NY + yy, x, lax.div(yy, MATS))

    def dev_x(d):
        return (shard, lax.rem(x + d + NX, NX), c)

    partner = (shard, x, 1 - c)
    y_of = [c * MATS + m for m in range(MATS)]

    def rcopy(src, dst, ss, rs, dev):
        return pltpu.make_async_remote_copy(
            src_ref=src, dst_ref=dst, send_sem=ss, recv_sem=rs, device_id=dev, device_id_type=MESH
        )

    zn = near_first(NZ)
    zf = zn[::-1]
    yf = near_first(NY)[::-1]

    sg = 1 - 2 * c
    pairs_z, single_z = relay_plan(NZ)
    pairs_y, single_y = relay_plan(NY)

    def zt(o):
        return lax.rem(z - sg * o + 2 * NZ, NZ)

    def yt(o):
        return lax.rem(y - sg * o + 2 * NY, NY)

    def dev_zabs(zz):
        return (zz * NY + y, x, c)

    def chunk_a(zz):
        return grad.at[:, pl.ds(pl.multiple_of(zz * ZR, ZR), ZR), pl.ds(0, HC)]

    o_of = [lax.rem(sg * (y - y_of[m]) + 2 * NY, NY) for m in range(MATS)]

    loc = [
        pltpu.make_async_copy(chunk_a(z), own_a, s_loc.at[0]),
        pltpu.make_async_copy(grad.at[:, :, pl.ds(HC, HC)], ownb, s_loc.at[1]),
        pltpu.make_async_copy(vec, vecv, s_loc.at[2]),
        pltpu.make_async_copy(wts, wtv, s_loc.at[3]),
        pltpu.make_async_copy(vecs, vecsv, s_loc.at[4]),
        pltpu.make_async_copy(fm, fmv, s_loc.at[5]),
        pltpu.make_async_copy(sm, smv, s_loc.at[6]),
    ]
    for i, (_, g) in enumerate(pairs_z):
        loc.append(pltpu.make_async_copy(chunk_a(zt(g)), ownp.at[i], s_loc.at[8 + i]))
    for cp in loc:
        cp.start()
    loc_mm = pltpu.make_async_copy(mom.at[my_m], mrx.at[y], s_loc.at[7])

    barrier = pltpu.get_barrier_semaphore()

    def greet(dev):
        pl.semaphore_signal(barrier, inc=1, device_id=dev, device_id_type=MESH)

    for d in zf:
        greet(dev_z(d))
    for d in yf:
        greet(dev_y(d))
    for d in range(1, NX):
        greet(dev_x(d))
    greet(partner)
    for j in range(MATS):
        greet((z * NY + (1 - lax.div(y, MATS)) * MATS + j, x, 1 - c))
    pl.semaphore_wait(barrier, NZ - 1 + NY - 1 + NX - 1 + 1 + MATS)

    MH = MATS // 4
    RH = ROWS // 4

    def half_a(h):
        return pl.ds(h * MH, MH)

    def half_b(h):
        return pl.ds(h * RH, RH)

    def chunk_ah(zz, h):
        return grad.at[half_a(h), pl.ds(pl.multiple_of(zz * ZR, ZR), ZR), pl.ds(0, HC)]

    def chunk_bh(m, h):
        return grad.at[m, half_b(h), pl.ds(HC, HC)]

    def first_a(i, h):
        f, g = pairs_z[i]
        return rcopy(
            chunk_ah(zt(f), h), p1a.at[i, half_a(h)], s_p1a.at[i, h], r_p1a.at[i, h], dev_zabs(zt(f - g))
        )

    def second_a(i, h):
        g = pairs_z[i][1]
        return rcopy(
            out_a.at[i, half_a(h)], ra.at[g, half_a(h)], s_ra.at[g, h], r_ra.at[g, h], dev_zabs(zt(g))
        )

    def single_a(o, h):
        return rcopy(
            chunk_ah(zt(o), h), ra.at[o, half_a(h)], s_ra.at[o, h], r_ra.at[o, h], dev_zabs(zt(o))
        )

    def first_b(m, f, g, h):
        return rcopy(
            chunk_bh(m, h), p1b.at[m, half_b(h)], s_p1b.at[m, h], r_p1b.at[m, h], dev_yabs(yt(f - g))
        )

    def single_b(m, o, h):
        return rcopy(chunk_bh(m, h), rb.at[o, half_b(h)], s_rb.at[m, h], r_rb.at[o, h], dev_yabs(y_of[m]))

    def second_b(m, h):
        o = o_of[m]
        return rcopy(
            out_b.at[m, half_b(h)], rb.at[o, half_b(h)], s_rb.at[m, h], r_rb.at[o, h], dev_yabs(y_of[m])
        )

    def is_relay(m):
        hit = o_of[m] == pairs_y[0][1]
        for _, g in pairs_y[1:]:
            hit = jnp.logical_or(hit, o_of[m] == g)
        return hit

    for h in range(4):
        for o in single_z:
            single_a(o, h).start()
        for m in range(MATS):
            for o in single_y:
                @pl.when(o_of[m] == o)
                def _():
                    single_b(m, o, h).start()
    for h in range(4):
        for i in range(len(pairs_z)):
            first_a(i, h).start()
        for m in range(MATS):
            for f, g in pairs_y:
                @pl.when(o_of[m] == f)
                def _():
                    first_b(m, f, g, h).start()
    vz = []
    for d in range(1, NZ):
        cp = rcopy(vec, vrz.at[d - 1], s_vz.at[d - 1], r_vz.at[d - 1], dev_z(d))
        cp.start()
        vz.append(cp)
    for m in range(MATS):
        @pl.when(y != y_of[m])
        def _():
            rcopy(mom.at[m], mrx.at[y], s_mm.at[m], r_mm.at[y], dev_yabs(y_of[m])).start()

    @pl.when(active)
    def _():
        loc_mm.start()

    for cp in loc:
        cp.wait()
    for h in range(4):
        for i in range(len(pairs_z)):
            first_a(i, h).wait_recv()
            part = (i, half_a(h))
            out_a[part] = (ownp[part].astype(f32) + p1a[part].astype(f32)).astype(bf16)
            second_a(i, h).start()
        if pairs_y:
            for m in range(MATS):
                @pl.when(is_relay(m))
                def _():
                    rcopy(
                        chunk_bh(m, h), p1b.at[m, half_b(h)], s_p1b.at[m, h], r_p1b.at[m, h], dev_yabs(y)
                    ).wait_recv()
                    part = (m, half_b(h))
                    out_b[part] = (ownb[part].astype(f32) + p1b[part].astype(f32)).astype(bf16)
                    second_b(m, h).start()

    for cp in vz:
        cp.wait_recv()
    vs = vecv[...].astype(f32)
    for d in range(1, NZ):
        vs = vs + vrz[d - 1].astype(f32)
    vsum[...] = vs
    vy = []
    for d in range(1, NY):
        cp = rcopy(vsum, vry.at[d - 1], s_vy.at[d - 1], r_vy.at[d - 1], dev_y(d))
        cp.start()
        vy.append(cp)

    @pl.when(active)
    def _():
        loc_mm.wait()
        for yy in range(NY):
            @pl.when(y != yy)
            def _():
                rcopy(mom.at[0], mrx.at[yy], s_mm.at[0], r_mm.at[yy], dev_yabs(yy)).wait_recv()
            mst[yy * LOCAL:(yy + 1) * LOCAL, :] = mrx[yy]

    sources = single_y + [g for _, g in pairs_y]

    def send_2b(zz):
        return rcopy(send_b.at[zz], r2b.at[z], s_2b.at[zz], r_2b.at[z], dev_zabs(zz))

    for h in range(4):
        part = half_a(h)
        tot = own_a[part].astype(f32)
        for o in single_z + [g for _, g in pairs_z[::-1]]:
            rcopy(
                chunk_ah(0, h), ra.at[o, part], s_ra.at[o, h], r_ra.at[o, h], dev_zabs(z)
            ).wait_recv()
        for o in single_z + [g for _, g in pairs_z[::-1]]:
            tot = tot + ra[o, part].astype(f32)
        acc_a[part] = tot
        sent_a[part] = tot.astype(bf16)
        for m in range(h * MH, (h + 1) * MH):
            @pl.when(y != y_of[m])
            def _():
                rcopy(sent_a.at[m], r2a.at[y], s_2a.at[m], r_2a.at[y], dev_yabs(y_of[m])).start()

        @pl.when(active)
        def _():
            for o in sources:
                rcopy(
                    chunk_bh(0, h), rb.at[o, half_b(h)], s_rb.at[0, h], r_rb.at[o, h], dev_yabs(y)
                ).wait_recv()
            for zz in range(h * NZ // 4, (h + 1) * NZ // 4):
                rows = slice(zz * ZR, (zz + 1) * ZR)
                tot = ownb[my_m, rows, :].astype(f32)
                for o in sources:
                    tot = tot + rb[o, rows, :].astype(f32)
                send_b[zz] = tot.astype(bf16)

                @pl.when(z == zz)
                def _():
                    own_b[...] = tot

                @pl.when(z != zz)
                def _():
                    send_2b(zz).start()

    for cp in vy:
        cp.wait_recv()
    vt = vsum[...]
    for d in range(1, NY):
        vt = vt + vry[d - 1]

    def lane_sum(v):
        total = jnp.sum(v, axis=0, keepdims=True)
        out = total[:, :LANES]
        for k in range(1, v.shape[1] // LANES):
            out = out + total[:, k * LANES:(k + 1) * LANES]
        return out

    def b2(v):
        return jnp.broadcast_to(v, (1, LANES))

    my_row = x * ROWS + z * ZR
    my_off = pl.multiple_of(my_row, ZR)

    def column_sum():
        r2a[y] = jnp.zeros((ZR, HC), bf16)
        mm_sum = lane_sum(mst[...] * mst[...])
        for yy in range(NY):
            @pl.when(y != yy)
            def _():
                rcopy(sent_a.at[0], r2a.at[yy], s_2a.at[0], r_2a.at[yy], dev_yabs(yy)).wait_recv()
        tot = acc_a[my_m]
        for yy in range(NY):
            tot = tot + r2a[yy].astype(f32)
        gbuf[:, :HC] = tot
        r2b[z] = jnp.zeros((ZR, HC), bf16)
        for zz in range(NZ):
            @pl.when(z != zz)
            def _():
                rcopy(send_b.at[0], r2b.at[zz], s_2b.at[0], r_2b.at[zz], dev_zabs(z)).wait_recv()
        tot = own_b[...]
        for zz in range(NZ):
            tot = tot + r2b[zz].astype(f32)
        gbuf[:, HC:] = tot

        gv = gbuf[...]
        gg = lane_sum(gv * gv)
        stat[...] = jnp.zeros_like(stat)
        stat[0:1, :] = gg
        stat[1:2, :] = lane_sum(gv * mst[...])
        stat[2:3, :] = mm_sum
        stat[3:4, :] = gg + lane_sum(vt * vt) * (1.0 / (NZ * MATS))
        st = []
        for d in zf:
            cp = rcopy(stat, srz.at[d - 1], s_sz.at[d - 1], r_sz.at[d - 1], dev_z(d))
            cp.start()
            st.append(cp)
        for cp in st:
            cp.wait()
        tot = stat[...]
        for d in range(1, NZ):
            tot = tot + srz[d - 1]
        stat[...] = tot
        st = []
        for d in range(1, NX):
            cp = rcopy(stat, srx.at[d - 1], s_sx.at[d - 1], r_sx.at[d - 1], dev_x(d))
            cp.start()
            st.append(cp)
        for cp in st:
            cp.wait()
        for d in range(1, NX):
            tot = tot + srx[d - 1]
        stat[...] = tot
        for yy in range(NY):
            @pl.when(y != yy)
            def _():
                rcopy(stat, sry.at[y], s_sy.at[yy], r_sy.at[y], dev_col(yy)).start()
        sry[y] = tot
        for yy in range(NY):
            @pl.when(y != yy)
            def _():
                rcopy(stat, sry.at[yy], s_sy.at[yy], r_sy.at[yy], dev_col(yy)).wait()
        grand = sry[0, 3:4, :]
        for yy in range(1, NY):
            grand = grand + sry[yy, 3:4, :]
        grand_total = jnp.sum(grand, axis=1, keepdims=True)
        own = jnp.sum(tot, axis=1, keepdims=True)
        clip = jnp.minimum(1.0, max_norm / (jnp.sqrt(grand_total) + 1e-06))
        stat2[...] = jnp.broadcast_to(clip, stat2.shape)
        rcopy(stat2, clipb, s_cl.at[0], r_cl.at[0], partner).start()
        cc = (1.0 + mom_beta) * clip
        bb = mom_beta * mom_beta
        norm2 = jnp.maximum(cc * cc * own[0:1] + (2.0 * bb) * cc * own[1:2] + (bb * bb) * own[2:3], 0.0)
        inv = 1.0 / (jnp.sqrt(norm2) + 1e-07)
        return clip, inv

    def block(dz, dx):
        row = lax.rem(x + dx + NX, NX) * ROWS + at_z(dz) * ZR
        return X.at[pl.ds(pl.multiple_of(row, ZR), ZR), :]

    def adam(clip):
        vlane = lax.broadcasted_iota(jnp.int32, vt.shape, 1)
        for k in range(LOCAL):
            vg = clip * jnp.sum(jnp.where(vlane == shard * LOCAL + k, vt, 0.0), axis=1, keepdims=True)
            uf = 0.9 * fmv[:, k:k + 1] + 0.1 * vg
            us = 0.999 * smv[:, k:k + 1] + 0.001 * vg * vg
            ad = uf / (jnp.sqrt(us) + 1e-08)
            adam_dir[:, k:k + 1] = ad
            new_vecs[:, k:k + 1] = vecsv[:, k:k + 1] * (1.0 - adam_rate * adam_decay) - adam_rate * ad

    TILE = min(256, D)
    NT = D // TILE
    dn0 = (((0,), (0,)), ((), ()))

    def block_gram(src, xb, first, last):
        rows = pl.ds(pl.multiple_of(xb * ROWS, ROWS), ROWS)

        for j in range(NT):
            n = (j + 1) * TILE
            cols = slice(j * TILE, n)
            pr = lax.dot_general(
                src[rows, :n], src[rows, cols], dn0, preferred_element_type=f32
            ).astype(bf16).astype(f32)
            if first:
                gacc[:n, cols] = pr
            elif last:
                tot = gacc[:n, cols] + pr
                G[:n, cols] = tot.astype(bf16)
                for i in range(j):
                    below = slice(i * TILE, (i + 1) * TILE)
                    G[cols, below] = tot[below, :].T.astype(bf16)
            else:
                gacc[:n, cols] += pr

    def step(rows):
        p1 = jnp.dot(rows, G[...], preferred_element_type=f32).astype(bf16)
        p2 = jnp.dot(p1, G[...], preferred_element_type=f32)
        return ns_first * rows.astype(f32) + ns_second * p1.astype(f32) + ns_third * p2

    @pl.when(active)
    def _():
        clip, inv = column_sum()
        cg = clip * gbuf[...]
        nm = mom_beta * mst[...] + cg
        X[pl.ds(my_off, ZR), :] = ((cg + mom_beta * nm) * inv).astype(bf16)

        mine = block(0, 0)
        order = [0] + zn
        zc = {}
        xc = {}
        fwd = []

        def send_x(k):
            b = block(-k, 0)
            right = rcopy(b, b, s_gr.at[k], r_gr.at[k], dev_x(1))
            left = rcopy(b, b, s_gl.at[k], r_gl.at[k], dev_x(-1))
            right.start()
            left.start()
            xc[k] = (right, left)
            if k in order[-5:]:
                cp = rcopy(b, b, s_fr.at[k], r_fr.at[k], dev_x(2))
                cp.start()
                fwd.append(cp)

        def forward(k):
            xc[k][0].wait_recv()
            if k % 2 == 0 and k not in order[-5:]:
                b = block(-k, -1)
                cp = rcopy(b, b, s_fr.at[k], r_fr.at[k], dev_x(1))
                cp.start()
                fwd.append(cp)
            xc[k][1].wait_recv()
            if k % 2 == 1 and k not in order[-5:]:
                b = block(-k, 1)
                cp = rcopy(b, b, s_fl.at[k], r_fl.at[k], dev_x(-1))
                cp.start()
                fwd.append(cp)

        for d in zn:
            cp = rcopy(mine, mine, s_gz.at[d - 1], r_gz.at[d - 1], dev_z(d))
            cp.start()
            zc[d] = cp
        send_x(0)

        for yy in range(NY):
            nms[yy] = nm[yy * LOCAL:(yy + 1) * LOCAL, :]
        new_mom[my_m] = nms[y]
        for yy in range(NY):
            @pl.when(y != yy)
            def _():
                rcopy(nms.at[yy], new_mom.at[my_m], s_nm.at[yy], r_nm.at[my_m], dev_yabs(yy)).start()
        adam(clip)

        for i, k in enumerate(order):
            if k > 0:
                zc[k].wait_recv()
                send_x(k)
            if i >= 3:
                forward(order[i - 3])
        block_gram(X, x, True, False)
        for k in order[-3:]:
            forward(k)
        block_gram(X, lax.rem(x + NX - 1, NX), False, False)
        block_gram(X, lax.rem(x + 1, NX), False, False)
        for cp in fwd:
            cp.wait()
        block_gram(X, lax.rem(x + 2, NX), False, True)

        @pl.loop(0, NX)
        def _(i):
            rows = pl.ds(pl.multiple_of(i * ROWS, ROWS), ROWS)
            X1[rows, :] = step(X[rows, :]).astype(bf16)

        for b in range(NX):
            block_gram(X1, b, b == 0, b == NX - 1)
        last = step(X1[pl.ds(my_off, ZR), :])
        for yy in range(NY):
            ret[yy] = last[yy * LOCAL:(yy + 1) * LOCAL, :].astype(bf16)
        for yy in range(NY):
            @pl.when(y != yy)
            def _():
                rcopy(ret.at[yy], upd_out.at[my_m], s_rt.at[yy], r_rt.at[my_m], dev_yabs(yy)).start()
        upd_out[my_m] = ret[y]
        for k in order:
            xc[k][0].wait_send()
            xc[k][1].wait_send()
        for d in zf:
            zc[d].wait_send()
        for zz in range(NZ):
            @pl.when(z != zz)
            def _():
                send_2b(zz).wait_send()
        rcopy(stat2, clipb, s_cl.at[0], r_cl.at[0], partner).wait_send()

    @pl.when(jnp.logical_not(active))
    def _():
        rcopy(stat2, clipb, s_cl.at[0], r_cl.at[0], partner).wait_recv()
        adam(clipb[0:1, 0:1])

    for h in range(4):
        for i in range(len(pairs_z)):
            first_a(i, h).wait_send()
            second_a(i, h).wait_send()
        for o in single_z:
            single_a(o, h).wait_send()
        for m in range(MATS):
            for f, g in pairs_y:
                @pl.when(o_of[m] == f)
                def _():
                    first_b(m, f, g, h).wait_send()

                @pl.when(o_of[m] == g)
                def _():
                    second_b(m, h).wait_send()
            for o in single_y:
                @pl.when(o_of[m] == o)
                def _():
                    single_b(m, o, h).wait_send()
    for cp in vz + vy:
        cp.wait_send()
    for m in range(MATS):
        @pl.when(y != y_of[m])
        def _():
            rcopy(mom.at[m], mrx.at[y], s_mm.at[m], r_mm.at[y], dev_yabs(y_of[m])).wait_send()
            rcopy(sent_a.at[m], r2a.at[y], s_2a.at[m], r_2a.at[y], dev_yabs(y_of[m])).wait_send()

    muon_scale = 0.2 * math.sqrt(D)
    for m in range(MATS):
        @pl.when(y != y_of[m])
        def _():
            rcopy(nms.at[0], new_mom.at[m], s_nm.at[0], r_nm.at[m], dev_yabs(y_of[m])).wait_recv()
            rcopy(ret.at[0], upd_out.at[m], s_rt.at[0], r_rt.at[m], dev_yabs(y_of[m])).wait_recv()
        new_wts[m] = (
            wtv[m].astype(f32) * (1.0 - muon_rate * muon_decay)
            - muon_rate * muon_scale * upd_out[m].astype(f32)
        ).astype(bf16)

    @pl.when(active)
    def _():
        for yy in range(NY):
            @pl.when(y != yy)
            def _():
                rcopy(nms.at[yy], new_mom.at[my_m], s_nm.at[yy], r_nm.at[my_m], dev_yabs(yy)).wait_send()
                rcopy(ret.at[yy], upd_out.at[my_m], s_rt.at[yy], r_rt.at[my_m], dev_yabs(yy)).wait_send()


def place(nm, up, wt, ad, nv, nm_o, up_o, wt_o, ad_o, nv_o, sems):
    copies = [
        pltpu.make_async_copy(src, dst, sems.at[i])
        for i, (src, dst) in enumerate([(nm, nm_o), (up, up_o), (wt, wt_o), (ad, ad_o), (nv, nv_o)])
    ]
    for cp in copies:
        cp.start()
    for cp in copies:
        cp.wait()


def hand_out(*arrays):
    hbm = pl.BlockSpec(memory_space=pltpu.HBM)
    return pl.pallas_call(
        place,
        out_shape=tuple(jax.ShapeDtypeStruct(a.shape, a.dtype) for a in arrays),
        in_specs=[hbm] * len(arrays),
        out_specs=(hbm,) * len(arrays),
        scratch_shapes=[pltpu.SemaphoreType.DMA((len(arrays),))],
    )(*arrays)


def build(mesh_shape, NZ, NY, MATS, LOCAL, D):
    NX = mesh_shape["tensor"]
    ROWS = NZ * NY * LOCAL
    ZR = NY * LOCAL
    HC = D // 2
    DMA = pltpu.SemaphoreType.DMA
    V = pltpu.VMEM
    scratch = [
        V((MATS, ROWS), bf16),
        V((MATS, LOCAL, D), bf16),
        V((MATS, LOCAL), f32),
        V((MATS, LOCAL), f32),
        V((MATS, LOCAL), f32),
        V((MATS, ZR, HC), bf16),
        V((3, MATS, ZR, HC), bf16),
        V((3, MATS, ZR, HC), bf16),
        V((3, MATS, ZR, HC), bf16),
        V((NZ, MATS, ZR, HC), bf16),
        V((MATS, ZR, HC), f32),
        V((MATS, ZR, HC), bf16),
        V((ZR, HC), f32),
        V((MATS, ROWS, HC), bf16),
        V((MATS, ROWS, HC), bf16),
        V((MATS, ROWS, HC), bf16),
        V((NY, ROWS, HC), bf16),
        V((NZ, ZR, HC), bf16),
        V((NY, ZR, HC), bf16),
        V((NZ, ZR, HC), bf16),
        V((NY, LOCAL, D), f32),
        V((ZR, D), f32),
        V((ZR, D), f32),
        V((NY, LOCAL, D), f32),
        V((NZ - 1, MATS, ROWS), bf16),
        V((NY - 1, MATS, ROWS), f32),
        V((MATS, ROWS), f32),
        V((8, LANES), f32),
        V((NZ - 1, 8, LANES), f32),
        V((NX - 1, 8, LANES), f32),
        V((NY, 8, LANES), f32),
        V((8, LANES), f32),
        V((8, LANES), f32),
        V((NX * ROWS, D), bf16),
        V((D, D), bf16),
        V((NX * ROWS, D), bf16),
        V((D, D), f32),
        V((NY, LOCAL, D), bf16),
        DMA((11,)),
        DMA((3, 4)), DMA((3, 4)), DMA((NZ, 4)), DMA((NZ, 4)),
        DMA((MATS, 4)), DMA((MATS, 4)), DMA((MATS, 4)), DMA((NY, 4)),
        DMA((MATS,)), DMA((NY,)), DMA((NZ,)), DMA((NZ,)), DMA((MATS,)), DMA((NY,)),
        DMA((NZ - 1,)), DMA((NZ - 1,)), DMA((NY - 1,)), DMA((NY - 1,)),
        DMA((NZ - 1,)), DMA((NZ - 1,)), DMA((NX - 1,)), DMA((NX - 1,)), DMA((NY,)), DMA((NY,)),
        DMA((1,)), DMA((1,)),
        DMA((NZ - 1,)), DMA((NZ - 1,)),
        DMA((NZ,)), DMA((NZ,)), DMA((NZ,)), DMA((NZ,)),
        DMA((NZ,)), DMA((NZ,)), DMA((NZ,)), DMA((NZ,)),
        DMA((NY,)), DMA((MATS,)), DMA((NY,)), DMA((MATS,)),
    ]
    vm = pl.BlockSpec(memory_space=pltpu.VMEM)
    hbm = pl.BlockSpec(memory_space=pltpu.HBM)
    return pl.pallas_call(
        functools.partial(kernel, NZ, NY, NX, MATS, LOCAL, D),
        out_shape=(
            jax.ShapeDtypeStruct((MATS, LOCAL, D), f32),
            jax.ShapeDtypeStruct((MATS, LOCAL, D), bf16),
            jax.ShapeDtypeStruct((MATS, LOCAL, D), bf16),
            jax.ShapeDtypeStruct((MATS, LOCAL), f32),
            jax.ShapeDtypeStruct((MATS, LOCAL), f32),
        ),
        in_specs=[hbm] * 7,
        out_specs=(vm,) * 5,
        scratch_shapes=scratch,
        compiler_params=pltpu.CompilerParams(
            collective_id=0, has_side_effects=True, vmem_limit_bytes=60 << 20
        ),
    )


def solution(mesh, NZ=8, NY=8):
    def per_device(grad_parts, vector_grads, momentum, weights, vectors, first_moment, second_moment):
        MATS, LOCAL, WIDTH = momentum.shape[1:]
        call = build(mesh.shape, NZ, NY, MATS, LOCAL, WIDTH)
        outs = call(
            grad_parts[0, 0], vector_grads[0, 0], momentum[0], weights[0],
            vectors[0], first_moment[0], second_moment[0],
        )
        return tuple(o[None] for o in hand_out(*outs))

    rows = P("section", None, ("tensor", "shard"), None)
    cols = P("section", None, ("tensor", "shard"))
    return jax.shard_map(
        per_device,
        mesh=mesh,
        in_specs=(
            P("shard", "section", None, "tensor", None),
            P("shard", "section", None, "tensor"),
            rows, rows, cols, cols, cols,
        ),
        out_specs=(rows, rows, rows, cols, cols),
        check_vma=False,
    )
```

```python
import functools
import math

import jax
import jax.numpy as jnp
from jax import lax
from jax.experimental import pallas as pl
from jax.experimental.pallas import tpu as pltpu
from jax.sharding import PartitionSpec as P


ns_first = 3.4445
ns_second = -4.775
ns_third = 2.0315
mom_beta = 0.95
max_norm = 1024.0
muon_rate = 0.02
muon_decay = 0.1
adam_rate = 0.001
adam_decay = 0.01

MESH = pl.DeviceIdType.MESH
f32 = jnp.float32
bf16 = jnp.bfloat16
LANES = 128


def near_first(n):
    order = []
    for d in range(1, n // 2 + 1):
        order.append(d)
        if n - d != d:
            order.append(n - d)
    return order


def relay_plan(n):
    if n == 8:
        return [(4, 5), (3, 2), (6, 7)], [1]
    if n == 4:
        return [(2, 3)], [1]
    return [], list(range(1, n))


def kernel(
    NZ, NY, NX, MATS, LOCAL, D,
    grad, vec, mom, wts, vecs, fm, sm,
    new_mom, upd_out, new_wts, adam_dir, new_vecs,
    vecv, wtv, vecsv, fmv, smv,
    own_a, ownp, p1a, out_a, ra, acc_a, sent_a, own_b, ownb, p1b, out_b, rb, send_b, r2a, r2b, mrx, mst, gbuf, nms,
    vrz, vry, vsum, stat, srz, srx, sry, stat2, clipb, X, G, X1, gacc, ret,
    s_loc, s_p1a, r_p1a, s_ra, r_ra, s_p1b, r_p1b, s_rb, r_rb, s_2a, r_2a, s_2b, r_2b, s_mm, r_mm,
    s_vz, r_vz, s_vy, r_vy, s_sz, r_sz, s_sx, r_sx, s_sy, r_sy, s_cl, r_cl,
    s_gz, r_gz, s_gl, s_gr, r_gl, r_gr, s_fl, s_fr, r_fl, r_fr,
    s_nm, r_nm, s_rt, r_rt,
):
    ROWS = NZ * NY * LOCAL
    ZR = NY * LOCAL
    HC = D // 2
    shard = lax.axis_index("shard")
    x = lax.axis_index("tensor")
    c = lax.axis_index("section")
    z = lax.div(shard, NY)
    y = lax.rem(shard, NY)
    active = lax.div(y, MATS) == c
    my_m = lax.rem(y, MATS)

    def at_z(d):
        return lax.rem(z + d + NZ, NZ)

    def dev_z(d):
        return (at_z(d) * NY + y, x, c)

    def dev_y(d):
        return (z * NY + lax.rem(y + d + NY, NY), x, c)

    def dev_yabs(yy):
        return (z * NY + yy, x, c)

    def dev_col(yy):
        return (z * NY + yy, x, lax.div(yy, MATS))

    def dev_x(d):
        return (shard, lax.rem(x + d + NX, NX), c)

    partner = (shard, x, 1 - c)
    y_of = [c * MATS + m for m in range(MATS)]

    def rcopy(src, dst, ss, rs, dev):
        return pltpu.make_async_remote_copy(
            src_ref=src, dst_ref=dst, send_sem=ss, recv_sem=rs, device_id=dev, device_id_type=MESH
        )

    zn = near_first(NZ)
    zf = zn[::-1]
    yf = near_first(NY)[::-1]

    sg = 1 - 2 * c
    pairs_z, single_z = relay_plan(NZ)
    pairs_y, single_y = relay_plan(NY)

    def zt(o):
        return lax.rem(z - sg * o + 2 * NZ, NZ)

    def yt(o):
        return lax.rem(y - sg * o + 2 * NY, NY)

    def dev_zabs(zz):
        return (zz * NY + y, x, c)

    def chunk_a(zz):
        return grad.at[:, pl.ds(pl.multiple_of(zz * ZR, ZR), ZR), pl.ds(0, HC)]

    o_of = [lax.rem(sg * (y - y_of[m]) + 2 * NY, NY) for m in range(MATS)]

    loc = [
        pltpu.make_async_copy(chunk_a(z), own_a, s_loc.at[0]),
        pltpu.make_async_copy(grad.at[:, :, pl.ds(HC, HC)], ownb, s_loc.at[1]),
        pltpu.make_async_copy(vec, vecv, s_loc.at[2]),
        pltpu.make_async_copy(wts, wtv, s_loc.at[3]),
        pltpu.make_async_copy(vecs, vecsv, s_loc.at[4]),
        pltpu.make_async_copy(fm, fmv, s_loc.at[5]),
        pltpu.make_async_copy(sm, smv, s_loc.at[6]),
    ]
    for i, (_, g) in enumerate(pairs_z):
        loc.append(pltpu.make_async_copy(chunk_a(zt(g)), ownp.at[i], s_loc.at[8 + i]))
    for cp in loc:
        cp.start()
    loc_mm = pltpu.make_async_copy(mom.at[my_m], mrx.at[y], s_loc.at[7])

    barrier = pltpu.get_barrier_semaphore()

    def greet(dev):
        pl.semaphore_signal(barrier, inc=1, device_id=dev, device_id_type=MESH)

    for d in zf:
        greet(dev_z(d))
    for d in yf:
        greet(dev_y(d))
    for d in range(1, NX):
        greet(dev_x(d))
    greet(partner)
    for j in range(MATS):
        greet((z * NY + (1 - lax.div(y, MATS)) * MATS + j, x, 1 - c))
    pl.semaphore_wait(barrier, NZ - 1 + NY - 1 + NX - 1 + 1 + MATS)

    MH = MATS // 4
    RH = ROWS // 4

    def half_a(h):
        return pl.ds(h * MH, MH)

    def half_b(h):
        return pl.ds(h * RH, RH)

    def chunk_ah(zz, h):
        return grad.at[half_a(h), pl.ds(pl.multiple_of(zz * ZR, ZR), ZR), pl.ds(0, HC)]

    def chunk_bh(m, h):
        return grad.at[m, half_b(h), pl.ds(HC, HC)]

    def first_a(i, h):
        f, g = pairs_z[i]
        return rcopy(
            chunk_ah(zt(f), h), p1a.at[i, half_a(h)], s_p1a.at[i, h], r_p1a.at[i, h], dev_zabs(zt(f - g))
        )

    def second_a(i, h):
        g = pairs_z[i][1]
        return rcopy(
            out_a.at[i, half_a(h)], ra.at[g, half_a(h)], s_ra.at[g, h], r_ra.at[g, h], dev_zabs(zt(g))
        )

    def single_a(o, h):
        return rcopy(
            chunk_ah(zt(o), h), ra.at[o, half_a(h)], s_ra.at[o, h], r_ra.at[o, h], dev_zabs(zt(o))
        )

    def first_b(m, f, g, h):
        return rcopy(
            chunk_bh(m, h), p1b.at[m, half_b(h)], s_p1b.at[m, h], r_p1b.at[m, h], dev_yabs(yt(f - g))
        )

    def single_b(m, o, h):
        return rcopy(chunk_bh(m, h), rb.at[o, half_b(h)], s_rb.at[m, h], r_rb.at[o, h], dev_yabs(y_of[m]))

    def second_b(m, h):
        o = o_of[m]
        return rcopy(
            out_b.at[m, half_b(h)], rb.at[o, half_b(h)], s_rb.at[m, h], r_rb.at[o, h], dev_yabs(y_of[m])
        )

    def is_relay(m):
        hit = o_of[m] == pairs_y[0][1]
        for _, g in pairs_y[1:]:
            hit = jnp.logical_or(hit, o_of[m] == g)
        return hit

    for h in range(4):
        for o in single_z:
            single_a(o, h).start()
        for m in range(MATS):
            for o in single_y:
                @pl.when(o_of[m] == o)
                def _():
                    single_b(m, o, h).start()
    for h in range(4):
        for i in range(len(pairs_z)):
            first_a(i, h).start()
        for m in range(MATS):
            for f, g in pairs_y:
                @pl.when(o_of[m] == f)
                def _():
                    first_b(m, f, g, h).start()
    vz = []
    for d in range(1, NZ):
        cp = rcopy(vec, vrz.at[d - 1], s_vz.at[d - 1], r_vz.at[d - 1], dev_z(d))
        cp.start()
        vz.append(cp)
    for m in range(MATS):
        @pl.when(y != y_of[m])
        def _():
            rcopy(mom.at[m], mrx.at[y], s_mm.at[m], r_mm.at[y], dev_yabs(y_of[m])).start()

    @pl.when(active)
    def _():
        loc_mm.start()

    for cp in loc:
        cp.wait()
    for h in range(4):
        for i in range(len(pairs_z)):
            first_a(i, h).wait_recv()
            part = (i, half_a(h))
            out_a[part] = (ownp[part].astype(f32) + p1a[part].astype(f32)).astype(bf16)
            second_a(i, h).start()
        if pairs_y:
            for m in range(MATS):
                @pl.when(is_relay(m))
                def _():
                    rcopy(
                        chunk_bh(m, h), p1b.at[m, half_b(h)], s_p1b.at[m, h], r_p1b.at[m, h], dev_yabs(y)
                    ).wait_recv()
                    part = (m, half_b(h))
                    out_b[part] = (ownb[part].astype(f32) + p1b[part].astype(f32)).astype(bf16)
                    second_b(m, h).start()

    for cp in vz:
        cp.wait_recv()
    vs = vecv[...].astype(f32)
    for d in range(1, NZ):
        vs = vs + vrz[d - 1].astype(f32)
    vsum[...] = vs
    vy = []
    for d in range(1, NY):
        cp = rcopy(vsum, vry.at[d - 1], s_vy.at[d - 1], r_vy.at[d - 1], dev_y(d))
        cp.start()
        vy.append(cp)

    @pl.when(active)
    def _():
        loc_mm.wait()
        for yy in range(NY):
            @pl.when(y != yy)
            def _():
                rcopy(mom.at[0], mrx.at[yy], s_mm.at[0], r_mm.at[yy], dev_yabs(yy)).wait_recv()
            mst[yy * LOCAL:(yy + 1) * LOCAL, :] = mrx[yy]

    sources = single_y + [g for _, g in pairs_y]

    def send_2b(zz):
        return rcopy(send_b.at[zz], r2b.at[z], s_2b.at[zz], r_2b.at[z], dev_zabs(zz))

    for h in range(4):
        part = half_a(h)
        tot = own_a[part].astype(f32)
        for o in single_z + [g for _, g in pairs_z[::-1]]:
            rcopy(
                chunk_ah(0, h), ra.at[o, part], s_ra.at[o, h], r_ra.at[o, h], dev_zabs(z)
            ).wait_recv()
        for o in single_z + [g for _, g in pairs_z[::-1]]:
            tot = tot + ra[o, part].astype(f32)
        acc_a[part] = tot
        sent_a[part] = tot.astype(bf16)
        for m in range(h * MH, (h + 1) * MH):
            @pl.when(y != y_of[m])
            def _():
                rcopy(sent_a.at[m], r2a.at[y], s_2a.at[m], r_2a.at[y], dev_yabs(y_of[m])).start()

        @pl.when(active)
        def _():
            for o in sources:
                rcopy(
                    chunk_bh(0, h), rb.at[o, half_b(h)], s_rb.at[0, h], r_rb.at[o, h], dev_yabs(y)
                ).wait_recv()
            for zz in range(h * NZ // 4, (h + 1) * NZ // 4):
                rows = slice(zz * ZR, (zz + 1) * ZR)
                tot = ownb[my_m, rows, :].astype(f32)
                for o in sources:
                    tot = tot + rb[o, rows, :].astype(f32)
                send_b[zz] = tot.astype(bf16)

                @pl.when(z == zz)
                def _():
                    own_b[...] = tot

                @pl.when(z != zz)
                def _():
                    send_2b(zz).start()

    for cp in vy:
        cp.wait_recv()
    vt = vsum[...]
    for d in range(1, NY):
        vt = vt + vry[d - 1]

    def lane_sum(v):
        total = jnp.sum(v, axis=0, keepdims=True)
        out = total[:, :LANES]
        for k in range(1, v.shape[1] // LANES):
            out = out + total[:, k * LANES:(k + 1) * LANES]
        return out

    def b2(v):
        return jnp.broadcast_to(v, (1, LANES))

    my_row = x * ROWS + z * ZR
    my_off = pl.multiple_of(my_row, ZR)

    def column_sum():
        r2a[y] = jnp.zeros((ZR, HC), bf16)
        mm_sum = lane_sum(mst[...] * mst[...])
        for yy in range(NY):
            @pl.when(y != yy)
            def _():
                rcopy(sent_a.at[0], r2a.at[yy], s_2a.at[0], r_2a.at[yy], dev_yabs(yy)).wait_recv()
        tot = acc_a[my_m]
        for yy in range(NY):
            tot = tot + r2a[yy].astype(f32)
        gbuf[:, :HC] = tot
        r2b[z] = jnp.zeros((ZR, HC), bf16)
        for zz in range(NZ):
            @pl.when(z != zz)
            def _():
                rcopy(send_b.at[0], r2b.at[zz], s_2b.at[0], r_2b.at[zz], dev_zabs(z)).wait_recv()
        tot = own_b[...]
        for zz in range(NZ):
            tot = tot + r2b[zz].astype(f32)
        gbuf[:, HC:] = tot

        gv = gbuf[...]
        gg = lane_sum(gv * gv)
        stat[...] = jnp.zeros_like(stat)
        stat[0:1, :] = gg
        stat[1:2, :] = lane_sum(gv * mst[...])
        stat[2:3, :] = mm_sum
        stat[3:4, :] = gg + lane_sum(vt * vt) * (1.0 / (NZ * MATS))
        st = []
        for d in zf:
            cp = rcopy(stat, srz.at[d - 1], s_sz.at[d - 1], r_sz.at[d - 1], dev_z(d))
            cp.start()
            st.append(cp)
        for cp in st:
            cp.wait()
        tot = stat[...]
        for d in range(1, NZ):
            tot = tot + srz[d - 1]
        stat[...] = tot
        st = []
        for d in range(1, NX):
            cp = rcopy(stat, srx.at[d - 1], s_sx.at[d - 1], r_sx.at[d - 1], dev_x(d))
            cp.start()
            st.append(cp)
        for cp in st:
            cp.wait()
        for d in range(1, NX):
            tot = tot + srx[d - 1]
        stat[...] = tot
        for yy in range(NY):
            @pl.when(y != yy)
            def _():
                rcopy(stat, sry.at[y], s_sy.at[yy], r_sy.at[y], dev_col(yy)).start()
        sry[y] = tot
        for yy in range(NY):
            @pl.when(y != yy)
            def _():
                rcopy(stat, sry.at[yy], s_sy.at[yy], r_sy.at[yy], dev_col(yy)).wait()
        grand = sry[0, 3:4, :]
        for yy in range(1, NY):
            grand = grand + sry[yy, 3:4, :]
        grand_total = jnp.sum(grand, axis=1, keepdims=True)
        own = jnp.sum(tot, axis=1, keepdims=True)
        clip = jnp.minimum(1.0, max_norm / (jnp.sqrt(grand_total) + 1e-06))
        stat2[...] = jnp.broadcast_to(clip, stat2.shape)
        rcopy(stat2, clipb, s_cl.at[0], r_cl.at[0], partner).start()
        cc = (1.0 + mom_beta) * clip
        bb = mom_beta * mom_beta
        norm2 = jnp.maximum(cc * cc * own[0:1] + (2.0 * bb) * cc * own[1:2] + (bb * bb) * own[2:3], 0.0)
        inv = 1.0 / (jnp.sqrt(norm2) + 1e-07)
        return clip, inv

    def block(dz, dx):
        row = lax.rem(x + dx + NX, NX) * ROWS + at_z(dz) * ZR
        return X.at[pl.ds(pl.multiple_of(row, ZR), ZR), :]

    def adam(clip):
        vlane = lax.broadcasted_iota(jnp.int32, vt.shape, 1)
        for k in range(LOCAL):
            vg = clip * jnp.sum(jnp.where(vlane == shard * LOCAL + k, vt, 0.0), axis=1, keepdims=True)
            uf = 0.9 * fmv[:, k:k + 1] + 0.1 * vg
            us = 0.999 * smv[:, k:k + 1] + 0.001 * vg * vg
            ad = uf / (jnp.sqrt(us) + 1e-08)
            adam_dir[:, k:k + 1] = ad
            new_vecs[:, k:k + 1] = vecsv[:, k:k + 1] * (1.0 - adam_rate * adam_decay) - adam_rate * ad

    TILE = min(256, D)
    NT = D // TILE
    dn0 = (((0,), (0,)), ((), ()))

    def block_gram(src, xb, first, last):
        rows = pl.ds(pl.multiple_of(xb * ROWS, ROWS), ROWS)

        for j in range(NT):
            n = (j + 1) * TILE
            cols = slice(j * TILE, n)
            pr = lax.dot_general(
                src[rows, :n], src[rows, cols], dn0, preferred_element_type=f32
            ).astype(bf16).astype(f32)
            if first:
                gacc[:n, cols] = pr
            elif last:
                tot = gacc[:n, cols] + pr
                G[:n, cols] = tot.astype(bf16)
                for i in range(j):
                    below = slice(i * TILE, (i + 1) * TILE)
                    G[cols, below] = tot[below, :].T.astype(bf16)
            else:
                gacc[:n, cols] += pr

    def step(rows):
        p1 = jnp.dot(rows, G[...], preferred_element_type=f32).astype(bf16)
        p2 = jnp.dot(p1, G[...], preferred_element_type=f32)
        return ns_first * rows.astype(f32) + ns_second * p1.astype(f32) + ns_third * p2

    @pl.when(active)
    def _():
        clip, inv = column_sum()
        cg = clip * gbuf[...]
        nm = mom_beta * mst[...] + cg
        X[pl.ds(my_off, ZR), :] = ((cg + mom_beta * nm) * inv).astype(bf16)

        mine = block(0, 0)
        order = [0] + zn
        zc = {}
        xc = {}
        fwd = []

        def send_x(k):
            b = block(-k, 0)
            right = rcopy(b, b, s_gr.at[k], r_gr.at[k], dev_x(1))
            left = rcopy(b, b, s_gl.at[k], r_gl.at[k], dev_x(-1))
            right.start()
            left.start()
            xc[k] = (right, left)
            if k in order[-5:]:
                cp = rcopy(b, b, s_fr.at[k], r_fr.at[k], dev_x(2))
                cp.start()
                fwd.append(cp)

        def forward(k):
            xc[k][0].wait_recv()
            if k % 2 == 0 and k not in order[-5:]:
                b = block(-k, -1)
                cp = rcopy(b, b, s_fr.at[k], r_fr.at[k], dev_x(1))
                cp.start()
                fwd.append(cp)
            xc[k][1].wait_recv()
            if k % 2 == 1 and k not in order[-5:]:
                b = block(-k, 1)
                cp = rcopy(b, b, s_fl.at[k], r_fl.at[k], dev_x(-1))
                cp.start()
                fwd.append(cp)

        send_x(0)
        for d in zn:
            cp = rcopy(mine, mine, s_gz.at[d - 1], r_gz.at[d - 1], dev_z(d))
            cp.start()
            zc[d] = cp

        for yy in range(NY):
            nms[yy] = nm[yy * LOCAL:(yy + 1) * LOCAL, :]
        new_mom[my_m] = nms[y]
        for yy in range(NY):
            @pl.when(y != yy)
            def _():
                rcopy(nms.at[yy], new_mom.at[my_m], s_nm.at[yy], r_nm.at[my_m], dev_yabs(yy)).start()

        for i, k in enumerate(order):
            if k > 0:
                zc[k].wait_recv()
                send_x(k)
            if i >= 3:
                forward(order[i - 3])
        block_gram(X, x, True, False)
        for k in order[-3:]:
            forward(k)
        block_gram(X, lax.rem(x + NX - 1, NX), False, False)
        block_gram(X, lax.rem(x + 1, NX), False, False)
        for cp in fwd:
            cp.wait()
        block_gram(X, lax.rem(x + 2, NX), False, True)

        for b in range(NX):
            rows = slice(b * ROWS, (b + 1) * ROWS)
            X1[rows, :] = step(X[rows, :]).astype(bf16)
        for b in range(NX):
            block_gram(X1, b, b == 0, b == NX - 1)
        last = step(X1[pl.ds(my_off, ZR), :])
        for yy in range(NY):
            ret[yy] = last[yy * LOCAL:(yy + 1) * LOCAL, :].astype(bf16)
        for yy in range(NY):
            @pl.when(y != yy)
            def _():
                rcopy(ret.at[yy], upd_out.at[my_m], s_rt.at[yy], r_rt.at[my_m], dev_yabs(yy)).start()
        upd_out[my_m] = ret[y]
        adam(clip)
        for k in order:
            xc[k][0].wait_send()
            xc[k][1].wait_send()
        for d in zf:
            zc[d].wait_send()
        for zz in range(NZ):
            @pl.when(z != zz)
            def _():
                send_2b(zz).wait_send()
        rcopy(stat2, clipb, s_cl.at[0], r_cl.at[0], partner).wait_send()

    @pl.when(jnp.logical_not(active))
    def _():
        rcopy(stat2, clipb, s_cl.at[0], r_cl.at[0], partner).wait_recv()
        adam(clipb[0:1, 0:1])

    for h in range(4):
        for i in range(len(pairs_z)):
            first_a(i, h).wait_send()
            second_a(i, h).wait_send()
        for o in single_z:
            single_a(o, h).wait_send()
        for m in range(MATS):
            for f, g in pairs_y:
                @pl.when(o_of[m] == f)
                def _():
                    first_b(m, f, g, h).wait_send()

                @pl.when(o_of[m] == g)
                def _():
                    second_b(m, h).wait_send()
            for o in single_y:
                @pl.when(o_of[m] == o)
                def _():
                    single_b(m, o, h).wait_send()
    for cp in vz + vy:
        cp.wait_send()
    for m in range(MATS):
        @pl.when(y != y_of[m])
        def _():
            rcopy(mom.at[m], mrx.at[y], s_mm.at[m], r_mm.at[y], dev_yabs(y_of[m])).wait_send()
            rcopy(sent_a.at[m], r2a.at[y], s_2a.at[m], r_2a.at[y], dev_yabs(y_of[m])).wait_send()

    muon_scale = 0.2 * math.sqrt(D)
    for m in range(MATS):
        @pl.when(y != y_of[m])
        def _():
            rcopy(nms.at[0], new_mom.at[m], s_nm.at[0], r_nm.at[m], dev_yabs(y_of[m])).wait_recv()
            rcopy(ret.at[0], upd_out.at[m], s_rt.at[0], r_rt.at[m], dev_yabs(y_of[m])).wait_recv()
        new_wts[m] = (
            wtv[m].astype(f32) * (1.0 - muon_rate * muon_decay)
            - muon_rate * muon_scale * upd_out[m].astype(f32)
        ).astype(bf16)

    @pl.when(active)
    def _():
        for yy in range(NY):
            @pl.when(y != yy)
            def _():
                rcopy(nms.at[yy], new_mom.at[my_m], s_nm.at[yy], r_nm.at[my_m], dev_yabs(yy)).wait_send()
                rcopy(ret.at[yy], upd_out.at[my_m], s_rt.at[yy], r_rt.at[my_m], dev_yabs(yy)).wait_send()


def place(nm, up, wt, ad, nv, nm_o, up_o, wt_o, ad_o, nv_o, sems):
    copies = [
        pltpu.make_async_copy(src, dst, sems.at[i])
        for i, (src, dst) in enumerate([(nm, nm_o), (up, up_o), (wt, wt_o), (ad, ad_o), (nv, nv_o)])
    ]
    for cp in copies:
        cp.start()
    for cp in copies:
        cp.wait()


def hand_out(*arrays):
    hbm = pl.BlockSpec(memory_space=pltpu.HBM)
    return pl.pallas_call(
        place,
        out_shape=tuple(jax.ShapeDtypeStruct(a.shape, a.dtype) for a in arrays),
        in_specs=[hbm] * len(arrays),
        out_specs=(hbm,) * len(arrays),
        scratch_shapes=[pltpu.SemaphoreType.DMA((len(arrays),))],
    )(*arrays)


def build(mesh_shape, NZ, NY, MATS, LOCAL, D):
    NX = mesh_shape["tensor"]
    ROWS = NZ * NY * LOCAL
    ZR = NY * LOCAL
    HC = D // 2
    DMA = pltpu.SemaphoreType.DMA
    V = pltpu.VMEM
    scratch = [
        V((MATS, ROWS), bf16),
        V((MATS, LOCAL, D), bf16),
        V((MATS, LOCAL), f32),
        V((MATS, LOCAL), f32),
        V((MATS, LOCAL), f32),
        V((MATS, ZR, HC), bf16),
        V((3, MATS, ZR, HC), bf16),
        V((3, MATS, ZR, HC), bf16),
        V((3, MATS, ZR, HC), bf16),
        V((NZ, MATS, ZR, HC), bf16),
        V((MATS, ZR, HC), f32),
        V((MATS, ZR, HC), bf16),
        V((ZR, HC), f32),
        V((MATS, ROWS, HC), bf16),
        V((MATS, ROWS, HC), bf16),
        V((MATS, ROWS, HC), bf16),
        V((NY, ROWS, HC), bf16),
        V((NZ, ZR, HC), bf16),
        V((NY, ZR, HC), bf16),
        V((NZ, ZR, HC), bf16),
        V((NY, LOCAL, D), f32),
        V((ZR, D), f32),
        V((ZR, D), f32),
        V((NY, LOCAL, D), f32),
        V((NZ - 1, MATS, ROWS), bf16),
        V((NY - 1, MATS, ROWS), f32),
        V((MATS, ROWS), f32),
        V((8, LANES), f32),
        V((NZ - 1, 8, LANES), f32),
        V((NX - 1, 8, LANES), f32),
        V((NY, 8, LANES), f32),
        V((8, LANES), f32),
        V((8, LANES), f32),
        V((NX * ROWS, D), bf16),
        V((D, D), bf16),
        V((NX * ROWS, D), bf16),
        V((D, D), f32),
        V((NY, LOCAL, D), bf16),
        DMA((11,)),
        DMA((3, 4)), DMA((3, 4)), DMA((NZ, 4)), DMA((NZ, 4)),
        DMA((MATS, 4)), DMA((MATS, 4)), DMA((MATS, 4)), DMA((NY, 4)),
        DMA((MATS,)), DMA((NY,)), DMA((NZ,)), DMA((NZ,)), DMA((MATS,)), DMA((NY,)),
        DMA((NZ - 1,)), DMA((NZ - 1,)), DMA((NY - 1,)), DMA((NY - 1,)),
        DMA((NZ - 1,)), DMA((NZ - 1,)), DMA((NX - 1,)), DMA((NX - 1,)), DMA((NY,)), DMA((NY,)),
        DMA((1,)), DMA((1,)),
        DMA((NZ - 1,)), DMA((NZ - 1,)),
        DMA((NZ,)), DMA((NZ,)), DMA((NZ,)), DMA((NZ,)),
        DMA((NZ,)), DMA((NZ,)), DMA((NZ,)), DMA((NZ,)),
        DMA((NY,)), DMA((MATS,)), DMA((NY,)), DMA((MATS,)),
    ]
    vm = pl.BlockSpec(memory_space=pltpu.VMEM)
    hbm = pl.BlockSpec(memory_space=pltpu.HBM)
    return pl.pallas_call(
        functools.partial(kernel, NZ, NY, NX, MATS, LOCAL, D),
        out_shape=(
            jax.ShapeDtypeStruct((MATS, LOCAL, D), f32),
            jax.ShapeDtypeStruct((MATS, LOCAL, D), bf16),
            jax.ShapeDtypeStruct((MATS, LOCAL, D), bf16),
            jax.ShapeDtypeStruct((MATS, LOCAL), f32),
            jax.ShapeDtypeStruct((MATS, LOCAL), f32),
        ),
        in_specs=[hbm] * 7,
        out_specs=(vm,) * 5,
        scratch_shapes=scratch,
        compiler_params=pltpu.CompilerParams(
            collective_id=0, has_side_effects=True, vmem_limit_bytes=60 << 20
        ),
    )


def solution(mesh, NZ=8, NY=8):
    def per_device(grad_parts, vector_grads, momentum, weights, vectors, first_moment, second_moment):
        MATS, LOCAL, WIDTH = momentum.shape[1:]
        call = build(mesh.shape, NZ, NY, MATS, LOCAL, WIDTH)
        outs = call(
            grad_parts[0, 0], vector_grads[0, 0], momentum[0], weights[0],
            vectors[0], first_moment[0], second_moment[0],
        )
        return tuple(o[None] for o in hand_out(*outs))

    rows = P("section", None, ("tensor", "shard"), None)
    cols = P("section", None, ("tensor", "shard"))
    return jax.shard_map(
        per_device,
        mesh=mesh,
        in_specs=(
            P("shard", "section", None, "tensor", None),
            P("shard", "section", None, "tensor"),
            rows, rows, cols, cols, cols,
        ),
        out_specs=(rows, rows, rows, cols, cols),
        check_vma=False,
    )
```

```python
import functools
import math

import jax
import jax.numpy as jnp
from jax import lax
from jax.experimental import pallas as pl
from jax.experimental.pallas import tpu as pltpu
from jax.sharding import PartitionSpec as P


ns_first = 3.4445
ns_second = -4.775
ns_third = 2.0315
mom_beta = 0.95
max_norm = 1024.0
muon_rate = 0.02
muon_decay = 0.1
adam_rate = 0.001
adam_decay = 0.01

MESH = pl.DeviceIdType.MESH
f32 = jnp.float32
bf16 = jnp.bfloat16
LANES = 128


def near_first(n):
    order = []
    for d in range(1, n // 2 + 1):
        order.append(d)
        if n - d != d:
            order.append(n - d)
    return order


def relay_plan(n):
    if n == 8:
        return [(4, 5), (3, 2), (6, 7)], [1]
    if n == 4:
        return [(2, 3)], [1]
    return [], list(range(1, n))


def kernel(
    NZ, NY, NX, MATS, LOCAL, D,
    grad, vec, mom, wts, vecs, fm, sm,
    new_mom, upd_out, new_wts, adam_dir, new_vecs,
    vecv, wtv, vecsv, fmv, smv,
    own_a, ownp, p1a, out_a, ra, acc_a, sent_a, own_b, ownb, p1b, out_b, rb, send_b, r2a, r2b, mrx, mst, gbuf, nms,
    vrz, vry, vsum, stat, srz, srx, sry, stat2, clipb, X, G, X1, gacc, ret,
    s_loc, s_p1a, r_p1a, s_ra, r_ra, s_p1b, r_p1b, s_rb, r_rb, s_2a, r_2a, s_2b, r_2b, s_mm, r_mm,
    s_vz, r_vz, s_vy, r_vy, s_sz, r_sz, s_sx, r_sx, s_sy, r_sy, s_cl, r_cl,
    s_gz, r_gz, s_gl, s_gr, r_gl, r_gr, s_fl, s_fr, r_fl, r_fr,
    s_nm, r_nm, s_rt, r_rt,
):
    ROWS = NZ * NY * LOCAL
    ZR = NY * LOCAL
    HC = D // 2
    shard = lax.axis_index("shard")
    x = lax.axis_index("tensor")
    c = lax.axis_index("section")
    z = lax.div(shard, NY)
    y = lax.rem(shard, NY)
    active = lax.div(y, MATS) == c
    my_m = lax.rem(y, MATS)

    def at_z(d):
        return lax.rem(z + d + NZ, NZ)

    def dev_z(d):
        return (at_z(d) * NY + y, x, c)

    def dev_y(d):
        return (z * NY + lax.rem(y + d + NY, NY), x, c)

    def dev_yabs(yy):
        return (z * NY + yy, x, c)

    def dev_col(yy):
        return (z * NY + yy, x, lax.div(yy, MATS))

    def dev_x(d):
        return (shard, lax.rem(x + d + NX, NX), c)

    partner = (shard, x, 1 - c)
    y_of = [c * MATS + m for m in range(MATS)]

    def rcopy(src, dst, ss, rs, dev):
        return pltpu.make_async_remote_copy(
            src_ref=src, dst_ref=dst, send_sem=ss, recv_sem=rs, device_id=dev, device_id_type=MESH
        )

    zn = near_first(NZ)
    zf = zn[::-1]
    yf = near_first(NY)[::-1]

    sg = 1 - 2 * c
    pairs_z, single_z = relay_plan(NZ)
    pairs_y, single_y = relay_plan(NY)

    def zt(o):
        return lax.rem(z - sg * o + 2 * NZ, NZ)

    def yt(o):
        return lax.rem(y - sg * o + 2 * NY, NY)

    def dev_zabs(zz):
        return (zz * NY + y, x, c)

    def chunk_a(zz):
        return grad.at[:, pl.ds(pl.multiple_of(zz * ZR, ZR), ZR), pl.ds(0, HC)]

    o_of = [lax.rem(sg * (y - y_of[m]) + 2 * NY, NY) for m in range(MATS)]

    loc = [
        pltpu.make_async_copy(chunk_a(z), own_a, s_loc.at[0]),
        pltpu.make_async_copy(grad.at[:, :, pl.ds(HC, HC)], ownb, s_loc.at[1]),
        pltpu.make_async_copy(vec, vecv, s_loc.at[2]),
        pltpu.make_async_copy(wts, wtv, s_loc.at[3]),
        pltpu.make_async_copy(vecs, vecsv, s_loc.at[4]),
        pltpu.make_async_copy(fm, fmv, s_loc.at[5]),
        pltpu.make_async_copy(sm, smv, s_loc.at[6]),
    ]
    for i, (_, g) in enumerate(pairs_z):
        loc.append(pltpu.make_async_copy(chunk_a(zt(g)), ownp.at[i], s_loc.at[8 + i]))
    for cp in loc:
        cp.start()
    loc_mm = pltpu.make_async_copy(mom.at[my_m], mrx.at[y], s_loc.at[7])

    barrier = pltpu.get_barrier_semaphore()

    def greet(dev):
        pl.semaphore_signal(barrier, inc=1, device_id=dev, device_id_type=MESH)

    for d in zf:
        greet(dev_z(d))
    for d in yf:
        greet(dev_y(d))
    for d in range(1, NX):
        greet(dev_x(d))
    greet(partner)
    for j in range(MATS):
        greet((z * NY + (1 - lax.div(y, MATS)) * MATS + j, x, 1 - c))
    pl.semaphore_wait(barrier, NZ - 1 + NY - 1 + NX - 1 + 1 + MATS)

    MH = MATS // 4
    RH = ROWS // 4

    def half_a(h):
        return pl.ds(h * MH, MH)

    def half_b(h):
        return pl.ds(h * RH, RH)

    def chunk_ah(zz, h):
        return grad.at[half_a(h), pl.ds(pl.multiple_of(zz * ZR, ZR), ZR), pl.ds(0, HC)]

    def chunk_bh(m, h):
        return grad.at[m, half_b(h), pl.ds(HC, HC)]

    def first_a(i, h):
        f, g = pairs_z[i]
        return rcopy(
            chunk_ah(zt(f), h), p1a.at[i, half_a(h)], s_p1a.at[i, h], r_p1a.at[i, h], dev_zabs(zt(f - g))
        )

    def second_a(i, h):
        g = pairs_z[i][1]
        return rcopy(
            out_a.at[i, half_a(h)], ra.at[g, half_a(h)], s_ra.at[g, h], r_ra.at[g, h], dev_zabs(zt(g))
        )

    def single_a(o, h):
        return rcopy(
            chunk_ah(zt(o), h), ra.at[o, half_a(h)], s_ra.at[o, h], r_ra.at[o, h], dev_zabs(zt(o))
        )

    def first_b(m, f, g, h):
        return rcopy(
            chunk_bh(m, h), p1b.at[m, half_b(h)], s_p1b.at[m, h], r_p1b.at[m, h], dev_yabs(yt(f - g))
        )

    def single_b(m, o, h):
        return rcopy(chunk_bh(m, h), rb.at[o, half_b(h)], s_rb.at[m, h], r_rb.at[o, h], dev_yabs(y_of[m]))

    def second_b(m, h):
        o = o_of[m]
        return rcopy(
            out_b.at[m, half_b(h)], rb.at[o, half_b(h)], s_rb.at[m, h], r_rb.at[o, h], dev_yabs(y_of[m])
        )

    def is_relay(m):
        hit = o_of[m] == pairs_y[0][1]
        for _, g in pairs_y[1:]:
            hit = jnp.logical_or(hit, o_of[m] == g)
        return hit

    for h in range(4):
        for o in single_z:
            single_a(o, h).start()
        for m in range(MATS):
            for o in single_y:
                @pl.when(o_of[m] == o)
                def _():
                    single_b(m, o, h).start()
    for h in range(4):
        for i in range(len(pairs_z)):
            first_a(i, h).start()
        for m in range(MATS):
            for f, g in pairs_y:
                @pl.when(o_of[m] == f)
                def _():
                    first_b(m, f, g, h).start()
    vz = []
    for d in range(1, NZ):
        cp = rcopy(vec, vrz.at[d - 1], s_vz.at[d - 1], r_vz.at[d - 1], dev_z(d))
        cp.start()
        vz.append(cp)
    for m in range(MATS):
        @pl.when(y != y_of[m])
        def _():
            rcopy(mom.at[m], mrx.at[y], s_mm.at[m], r_mm.at[y], dev_yabs(y_of[m])).start()

    @pl.when(active)
    def _():
        loc_mm.start()

    for cp in loc:
        cp.wait()
    for h in range(4):
        for i in range(len(pairs_z)):
            first_a(i, h).wait_recv()
            part = (i, half_a(h))
            out_a[part] = (ownp[part].astype(f32) + p1a[part].astype(f32)).astype(bf16)
            second_a(i, h).start()
        if pairs_y:
            for m in range(MATS):
                @pl.when(is_relay(m))
                def _():
                    rcopy(
                        chunk_bh(m, h), p1b.at[m, half_b(h)], s_p1b.at[m, h], r_p1b.at[m, h], dev_yabs(y)
                    ).wait_recv()
                    part = (m, half_b(h))
                    out_b[part] = (ownb[part].astype(f32) + p1b[part].astype(f32)).astype(bf16)
                    second_b(m, h).start()

    for cp in vz:
        cp.wait_recv()
    vs = vecv[...].astype(f32)
    for d in range(1, NZ):
        vs = vs + vrz[d - 1].astype(f32)
    vsum[...] = vs
    vy = []
    for d in range(1, NY):
        cp = rcopy(vsum, vry.at[d - 1], s_vy.at[d - 1], r_vy.at[d - 1], dev_y(d))
        cp.start()
        vy.append(cp)

    @pl.when(active)
    def _():
        loc_mm.wait()
        for yy in range(NY):
            @pl.when(y != yy)
            def _():
                rcopy(mom.at[0], mrx.at[yy], s_mm.at[0], r_mm.at[yy], dev_yabs(yy)).wait_recv()
            mst[yy * LOCAL:(yy + 1) * LOCAL, :] = mrx[yy]

    sources = single_y + [g for _, g in pairs_y]

    def send_2b(zz):
        return rcopy(send_b.at[zz], r2b.at[z], s_2b.at[zz], r_2b.at[z], dev_zabs(zz))

    for h in range(4):
        part = half_a(h)
        tot = own_a[part].astype(f32)
        for o in single_z + [g for _, g in pairs_z[::-1]]:
            rcopy(
                chunk_ah(0, h), ra.at[o, part], s_ra.at[o, h], r_ra.at[o, h], dev_zabs(z)
            ).wait_recv()
        for o in single_z + [g for _, g in pairs_z[::-1]]:
            tot = tot + ra[o, part].astype(f32)
        acc_a[part] = tot
        sent_a[part] = tot.astype(bf16)
        for m in range(h * MH, (h + 1) * MH):
            @pl.when(y != y_of[m])
            def _():
                rcopy(sent_a.at[m], r2a.at[y], s_2a.at[m], r_2a.at[y], dev_yabs(y_of[m])).start()

        @pl.when(active)
        def _():
            for o in sources:
                rcopy(
                    chunk_bh(0, h), rb.at[o, half_b(h)], s_rb.at[0, h], r_rb.at[o, h], dev_yabs(y)
                ).wait_recv()
            for zz in range(h * NZ // 4, (h + 1) * NZ // 4):
                rows = slice(zz * ZR, (zz + 1) * ZR)
                tot = ownb[my_m, rows, :].astype(f32)
                for o in sources:
                    tot = tot + rb[o, rows, :].astype(f32)
                send_b[zz] = tot.astype(bf16)

                @pl.when(z == zz)
                def _():
                    own_b[...] = tot

                @pl.when(z != zz)
                def _():
                    send_2b(zz).start()

    for cp in vy:
        cp.wait_recv()
    vt = vsum[...]
    for d in range(1, NY):
        vt = vt + vry[d - 1]

    def lane_sum(v):
        total = jnp.sum(v, axis=0, keepdims=True)
        out = total[:, :LANES]
        for k in range(1, v.shape[1] // LANES):
            out = out + total[:, k * LANES:(k + 1) * LANES]
        return out

    def b2(v):
        return jnp.broadcast_to(v, (1, LANES))

    my_row = x * ROWS + z * ZR
    my_off = pl.multiple_of(my_row, ZR)

    def finish_sends():
        for h in range(4):
            for i in range(len(pairs_z)):
                first_a(i, h).wait_send()
                second_a(i, h).wait_send()
            for o in single_z:
                single_a(o, h).wait_send()
            for m in range(MATS):
                for f, g in pairs_y:
                    @pl.when(o_of[m] == f)
                    def _():
                        first_b(m, f, g, h).wait_send()

                    @pl.when(o_of[m] == g)
                    def _():
                        second_b(m, h).wait_send()
                for o in single_y:
                    @pl.when(o_of[m] == o)
                    def _():
                        single_b(m, o, h).wait_send()
        for cp in vz + vy:
            cp.wait_send()
        for m in range(MATS):
            @pl.when(y != y_of[m])
            def _():
                rcopy(mom.at[m], mrx.at[y], s_mm.at[m], r_mm.at[y], dev_yabs(y_of[m])).wait_send()
                rcopy(sent_a.at[m], r2a.at[y], s_2a.at[m], r_2a.at[y], dev_yabs(y_of[m])).wait_send()

    def column_sum():
        r2a[y] = jnp.zeros((ZR, HC), bf16)
        mm_sum = lane_sum(mst[...] * mst[...])
        for yy in range(NY):
            @pl.when(y != yy)
            def _():
                rcopy(sent_a.at[0], r2a.at[yy], s_2a.at[0], r_2a.at[yy], dev_yabs(yy)).wait_recv()
        tot = acc_a[my_m]
        for yy in range(NY):
            tot = tot + r2a[yy].astype(f32)
        gbuf[:, :HC] = tot
        r2b[z] = jnp.zeros((ZR, HC), bf16)
        for zz in range(NZ):
            @pl.when(z != zz)
            def _():
                rcopy(send_b.at[0], r2b.at[zz], s_2b.at[0], r_2b.at[zz], dev_zabs(z)).wait_recv()
        tot = own_b[...]
        for zz in range(NZ):
            tot = tot + r2b[zz].astype(f32)
        gbuf[:, HC:] = tot

        gv = gbuf[...]
        gg = lane_sum(gv * gv)
        stat[...] = jnp.zeros_like(stat)
        stat[0:1, :] = gg
        stat[1:2, :] = lane_sum(gv * mst[...])
        stat[2:3, :] = mm_sum
        stat[3:4, :] = gg + lane_sum(vt * vt) * (1.0 / (NZ * MATS))
        st = []
        for d in zf:
            cp = rcopy(stat, srz.at[d - 1], s_sz.at[d - 1], r_sz.at[d - 1], dev_z(d))
            cp.start()
            st.append(cp)
        finish_sends()
        for cp in st:
            cp.wait()
        tot = stat[...]
        for d in range(1, NZ):
            tot = tot + srz[d - 1]
        stat[...] = tot
        st = []
        for d in range(1, NX):
            cp = rcopy(stat, srx.at[d - 1], s_sx.at[d - 1], r_sx.at[d - 1], dev_x(d))
            cp.start()
            st.append(cp)
        for cp in st:
            cp.wait()
        for d in range(1, NX):
            tot = tot + srx[d - 1]
        stat[...] = tot
        for yy in range(NY):
            @pl.when(y != yy)
            def _():
                rcopy(stat, sry.at[y], s_sy.at[yy], r_sy.at[y], dev_col(yy)).start()
        sry[y] = tot
        for yy in range(NY):
            @pl.when(y != yy)
            def _():
                rcopy(stat, sry.at[yy], s_sy.at[yy], r_sy.at[yy], dev_col(yy)).wait()
        grand = sry[0, 3:4, :]
        for yy in range(1, NY):
            grand = grand + sry[yy, 3:4, :]
        grand_total = jnp.sum(grand, axis=1, keepdims=True)
        own = jnp.sum(tot, axis=1, keepdims=True)
        clip = jnp.minimum(1.0, max_norm / (jnp.sqrt(grand_total) + 1e-06))
        stat2[...] = jnp.broadcast_to(clip, stat2.shape)
        rcopy(stat2, clipb, s_cl.at[0], r_cl.at[0], partner).start()
        cc = (1.0 + mom_beta) * clip
        bb = mom_beta * mom_beta
        norm2 = jnp.maximum(cc * cc * own[0:1] + (2.0 * bb) * cc * own[1:2] + (bb * bb) * own[2:3], 0.0)
        inv = 1.0 / (jnp.sqrt(norm2) + 1e-07)
        return clip, inv

    def block(dz, dx):
        row = lax.rem(x + dx + NX, NX) * ROWS + at_z(dz) * ZR
        return X.at[pl.ds(pl.multiple_of(row, ZR), ZR), :]

    def adam(clip):
        vlane = lax.broadcasted_iota(jnp.int32, vt.shape, 1)
        for k in range(LOCAL):
            vg = clip * jnp.sum(jnp.where(vlane == shard * LOCAL + k, vt, 0.0), axis=1, keepdims=True)
            uf = 0.9 * fmv[:, k:k + 1] + 0.1 * vg
            us = 0.999 * smv[:, k:k + 1] + 0.001 * vg * vg
            ad = uf / (jnp.sqrt(us) + 1e-08)
            adam_dir[:, k:k + 1] = ad
            new_vecs[:, k:k + 1] = vecsv[:, k:k + 1] * (1.0 - adam_rate * adam_decay) - adam_rate * ad

    TILE = min(256, D)
    NT = D // TILE
    dn0 = (((0,), (0,)), ((), ()))

    def block_gram(src, xb, first, last):
        rows = pl.ds(pl.multiple_of(xb * ROWS, ROWS), ROWS)

        for j in range(NT):
            n = (j + 1) * TILE
            cols = slice(j * TILE, n)
            pr = lax.dot_general(
                src[rows, :n], src[rows, cols], dn0, preferred_element_type=f32
            ).astype(bf16).astype(f32)
            if first:
                gacc[:n, cols] = pr
            elif last:
                tot = gacc[:n, cols] + pr
                G[:n, cols] = tot.astype(bf16)
                for i in range(j):
                    below = slice(i * TILE, (i + 1) * TILE)
                    G[cols, below] = tot[below, :].T.astype(bf16)
            else:
                gacc[:n, cols] += pr

    def step(rows):
        p1 = jnp.dot(rows, G[...], preferred_element_type=f32).astype(bf16)
        p2 = jnp.dot(p1, G[...], preferred_element_type=f32)
        return ns_first * rows.astype(f32) + ns_second * p1.astype(f32) + ns_third * p2

    @pl.when(active)
    def _():
        clip, inv = column_sum()
        cg = clip * gbuf[...]
        nm = mom_beta * mst[...] + cg
        X[pl.ds(my_off, ZR), :] = ((cg + mom_beta * nm) * inv).astype(bf16)

        mine = block(0, 0)
        order = [0] + zn
        zc = {}
        xc = {}
        fwd = []

        def send_x(k):
            b = block(-k, 0)
            right = rcopy(b, b, s_gr.at[k], r_gr.at[k], dev_x(1))
            left = rcopy(b, b, s_gl.at[k], r_gl.at[k], dev_x(-1))
            right.start()
            left.start()
            xc[k] = (right, left)
            if k in order[-5:]:
                cp = rcopy(b, b, s_fr.at[k], r_fr.at[k], dev_x(2))
                cp.start()
                fwd.append(cp)

        def forward(k):
            xc[k][0].wait_recv()
            if k % 2 == 0 and k not in order[-5:]:
                b = block(-k, -1)
                cp = rcopy(b, b, s_fr.at[k], r_fr.at[k], dev_x(1))
                cp.start()
                fwd.append(cp)
            xc[k][1].wait_recv()
            if k % 2 == 1 and k not in order[-5:]:
                b = block(-k, 1)
                cp = rcopy(b, b, s_fl.at[k], r_fl.at[k], dev_x(-1))
                cp.start()
                fwd.append(cp)

        send_x(0)
        for d in zn:
            cp = rcopy(mine, mine, s_gz.at[d - 1], r_gz.at[d - 1], dev_z(d))
            cp.start()
            zc[d] = cp

        for yy in range(NY):
            nms[yy] = nm[yy * LOCAL:(yy + 1) * LOCAL, :]
        new_mom[my_m] = nms[y]
        for yy in range(NY):
            @pl.when(y != yy)
            def _():
                rcopy(nms.at[yy], new_mom.at[my_m], s_nm.at[yy], r_nm.at[my_m], dev_yabs(yy)).start()

        for i, k in enumerate(order):
            if k > 0:
                zc[k].wait_recv()
                send_x(k)
            if i >= 3:
                forward(order[i - 3])
        block_gram(X, x, True, False)
        for k in order[-3:]:
            forward(k)
        block_gram(X, lax.rem(x + NX - 1, NX), False, False)
        block_gram(X, lax.rem(x + 1, NX), False, False)
        for cp in fwd:
            cp.wait()
        block_gram(X, lax.rem(x + 2, NX), False, True)

        for b in range(NX):
            rows = slice(b * ROWS, (b + 1) * ROWS)
            X1[rows, :] = step(X[rows, :]).astype(bf16)
        for b in range(NX):
            block_gram(X1, b, b == 0, b == NX - 1)
        last = step(X1[pl.ds(my_off, ZR), :])
        for yy in range(NY):
            ret[yy] = last[yy * LOCAL:(yy + 1) * LOCAL, :].astype(bf16)
        for yy in range(NY):
            @pl.when(y != yy)
            def _():
                rcopy(ret.at[yy], upd_out.at[my_m], s_rt.at[yy], r_rt.at[my_m], dev_yabs(yy)).start()
        upd_out[my_m] = ret[y]
        adam(clip)
        for k in order:
            xc[k][0].wait_send()
            xc[k][1].wait_send()
        for d in zf:
            zc[d].wait_send()
        for zz in range(NZ):
            @pl.when(z != zz)
            def _():
                send_2b(zz).wait_send()
        rcopy(stat2, clipb, s_cl.at[0], r_cl.at[0], partner).wait_send()

    @pl.when(jnp.logical_not(active))
    def _():
        finish_sends()
        rcopy(stat2, clipb, s_cl.at[0], r_cl.at[0], partner).wait_recv()
        adam(clipb[0:1, 0:1])

    muon_scale = 0.2 * math.sqrt(D)
    for m in range(MATS):
        @pl.when(y != y_of[m])
        def _():
            rcopy(nms.at[0], new_mom.at[m], s_nm.at[0], r_nm.at[m], dev_yabs(y_of[m])).wait_recv()
            rcopy(ret.at[0], upd_out.at[m], s_rt.at[0], r_rt.at[m], dev_yabs(y_of[m])).wait_recv()
        new_wts[m] = (
            wtv[m].astype(f32) * (1.0 - muon_rate * muon_decay)
            - muon_rate * muon_scale * upd_out[m].astype(f32)
        ).astype(bf16)

    @pl.when(active)
    def _():
        for yy in range(NY):
            @pl.when(y != yy)
            def _():
                rcopy(nms.at[yy], new_mom.at[my_m], s_nm.at[yy], r_nm.at[my_m], dev_yabs(yy)).wait_send()
                rcopy(ret.at[yy], upd_out.at[my_m], s_rt.at[yy], r_rt.at[my_m], dev_yabs(yy)).wait_send()


def place(nm, up, wt, ad, nv, nm_o, up_o, wt_o, ad_o, nv_o, sems):
    copies = [
        pltpu.make_async_copy(src, dst, sems.at[i])
        for i, (src, dst) in enumerate([(nm, nm_o), (up, up_o), (wt, wt_o), (ad, ad_o), (nv, nv_o)])
    ]
    for cp in copies:
        cp.start()
    for cp in copies:
        cp.wait()


def hand_out(*arrays):
    hbm = pl.BlockSpec(memory_space=pltpu.HBM)
    return pl.pallas_call(
        place,
        out_shape=tuple(jax.ShapeDtypeStruct(a.shape, a.dtype) for a in arrays),
        in_specs=[hbm] * len(arrays),
        out_specs=(hbm,) * len(arrays),
        scratch_shapes=[pltpu.SemaphoreType.DMA((len(arrays),))],
    )(*arrays)


def build(mesh_shape, NZ, NY, MATS, LOCAL, D):
    NX = mesh_shape["tensor"]
    ROWS = NZ * NY * LOCAL
    ZR = NY * LOCAL
    HC = D // 2
    DMA = pltpu.SemaphoreType.DMA
    V = pltpu.VMEM
    scratch = [
        V((MATS, ROWS), bf16),
        V((MATS, LOCAL, D), bf16),
        V((MATS, LOCAL), f32),
        V((MATS, LOCAL), f32),
        V((MATS, LOCAL), f32),
        V((MATS, ZR, HC), bf16),
        V((3, MATS, ZR, HC), bf16),
        V((3, MATS, ZR, HC), bf16),
        V((3, MATS, ZR, HC), bf16),
        V((NZ, MATS, ZR, HC), bf16),
        V((MATS, ZR, HC), f32),
        V((MATS, ZR, HC), bf16),
        V((ZR, HC), f32),
        V((MATS, ROWS, HC), bf16),
        V((MATS, ROWS, HC), bf16),
        V((MATS, ROWS, HC), bf16),
        V((NY, ROWS, HC), bf16),
        V((NZ, ZR, HC), bf16),
        V((NY, ZR, HC), bf16),
        V((NZ, ZR, HC), bf16),
        V((NY, LOCAL, D), f32),
        V((ZR, D), f32),
        V((ZR, D), f32),
        V((NY, LOCAL, D), f32),
        V((NZ - 1, MATS, ROWS), bf16),
        V((NY - 1, MATS, ROWS), f32),
        V((MATS, ROWS), f32),
        V((8, LANES), f32),
        V((NZ - 1, 8, LANES), f32),
        V((NX - 1, 8, LANES), f32),
        V((NY, 8, LANES), f32),
        V((8, LANES), f32),
        V((8, LANES), f32),
        V((NX * ROWS, D), bf16),
        V((D, D), bf16),
        V((NX * ROWS, D), bf16),
        V((D, D), f32),
        V((NY, LOCAL, D), bf16),
        DMA((11,)),
        DMA((3, 4)), DMA((3, 4)), DMA((NZ, 4)), DMA((NZ, 4)),
        DMA((MATS, 4)), DMA((MATS, 4)), DMA((MATS, 4)), DMA((NY, 4)),
        DMA((MATS,)), DMA((NY,)), DMA((NZ,)), DMA((NZ,)), DMA((MATS,)), DMA((NY,)),
        DMA((NZ - 1,)), DMA((NZ - 1,)), DMA((NY - 1,)), DMA((NY - 1,)),
        DMA((NZ - 1,)), DMA((NZ - 1,)), DMA((NX - 1,)), DMA((NX - 1,)), DMA((NY,)), DMA((NY,)),
        DMA((1,)), DMA((1,)),
        DMA((NZ - 1,)), DMA((NZ - 1,)),
        DMA((NZ,)), DMA((NZ,)), DMA((NZ,)), DMA((NZ,)),
        DMA((NZ,)), DMA((NZ,)), DMA((NZ,)), DMA((NZ,)),
        DMA((NY,)), DMA((MATS,)), DMA((NY,)), DMA((MATS,)),
    ]
    vm = pl.BlockSpec(memory_space=pltpu.VMEM)
    hbm = pl.BlockSpec(memory_space=pltpu.HBM)
    return pl.pallas_call(
        functools.partial(kernel, NZ, NY, NX, MATS, LOCAL, D),
        out_shape=(
            jax.ShapeDtypeStruct((MATS, LOCAL, D), f32),
            jax.ShapeDtypeStruct((MATS, LOCAL, D), bf16),
            jax.ShapeDtypeStruct((MATS, LOCAL, D), bf16),
            jax.ShapeDtypeStruct((MATS, LOCAL), f32),
            jax.ShapeDtypeStruct((MATS, LOCAL), f32),
        ),
        in_specs=[hbm] * 7,
        out_specs=(vm,) * 5,
        scratch_shapes=scratch,
        compiler_params=pltpu.CompilerParams(
            collective_id=0, has_side_effects=True, vmem_limit_bytes=60 << 20
        ),
    )


def solution(mesh, NZ=8, NY=8):
    def per_device(grad_parts, vector_grads, momentum, weights, vectors, first_moment, second_moment):
        MATS, LOCAL, WIDTH = momentum.shape[1:]
        call = build(mesh.shape, NZ, NY, MATS, LOCAL, WIDTH)
        outs = call(
            grad_parts[0, 0], vector_grads[0, 0], momentum[0], weights[0],
            vectors[0], first_moment[0], second_moment[0],
        )
        return tuple(o[None] for o in hand_out(*outs))

    rows = P("section", None, ("tensor", "shard"), None)
    cols = P("section", None, ("tensor", "shard"))
    return jax.shard_map(
        per_device,
        mesh=mesh,
        in_specs=(
            P("shard", "section", None, "tensor", None),
            P("shard", "section", None, "tensor"),
            rows, rows, cols, cols, cols,
        ),
        out_specs=(rows, rows, rows, cols, cols),
        check_vma=False,
    )
```
